512 devices in a mesh: blk: 8 (over x, z_hi), grp: 64 (over y, z_lo, core).
Axes of the slice: x: 4, y: 4, z: 16 (z_hi: 2, z_lo: 8; z = z_hi * 8 + z_lo), core: 2. Of those that a mesh axis runs over, the one named last changes fastest.
Arguments:
- images: bfloat16 [8192, 1152], P(('blk', 'grp')), may hold values from -6 to 6
- texts: bfloat16 [8192, 1152], P(('blk', 'grp')), may hold values from -6 to 6
- scale: float32 [], replicated, may hold values from 8 to 16
- shift: float32 [], replicated, may hold values from -5 to -3
Outputs:
- image_loss: float32 [8192], P(('blk', 'grp'))
- image_grad: float32 [8192, 1152], P(('blk', 'grp'))
- text_grad: float32 [8192, 1152], P(('blk', 'grp'))
The draws below stay inside these ranges and needn't reach their ends.
All inputs are finite; a program needn't handle non-finite values.
Results may differ from the reference program's by a relative error of at most 0.0045.
Values may be sent and summed in bfloat16 or wider, within the bound.
A program may use at most 64 MiB of HBM per device.

```python
import jax
import jax.numpy as jnp
from jax import lax

D = 1152
BATCH = 8192


def level_of(stream_key, extent, split, smallest, top_value):
    def one(position, parts):
        draws = jax.random.uniform(jax.random.fold_in(jax.random.fold_in(stream_key, 6), position), (parts,), jnp.float32, smallest / len(split), top_value / len(split))
        return jnp.repeat(jnp.exp(draws), extent[position] // parts).reshape((-1,) + (1,) * (len(extent) - position - 1))

    level = one(*split[0])
    for cut in split[1:]:
        level = level * one(*cut)
    return level


def bell_draw(key, extent, scale, limit, cuts=(), kind=jnp.bfloat16):
    drawn = jax.random.normal(key, extent, jnp.float32) * scale
    if len(cuts) > 0:
        drawn = level_of(key, extent, cuts, -0.22, 0.18) * drawn
    return jnp.clip(drawn, min=-limit, max=limit).astype(kind)


def setup_inputs(seed: int = 0) -> dict:
    streams_of = jax.random.split(jax.random.key(seed), 5)
    return {
        "images": bell_draw(streams_of[0], (BATCH, D), 1.0, 6.0, ((0, 512),)),
        "texts": bell_draw(streams_of[1], (BATCH, D), 1.0, 6.0, ((0, 512),)),
        "scale": jnp.clip(jax.random.uniform(streams_of[2], (), jnp.float32, 8.0, 16.0), 8.0, 16.0),
        "shift": jnp.clip(jax.random.uniform(streams_of[3], (), jnp.float32, -5.0, -3.0), -5.0, -3.0),
    }


def unit_rows(values):
    floats = values.astype(jnp.float32)
    norms = jnp.sqrt(lax.optimization_barrier(jnp.sum(floats * floats, 1, keepdims=True)) + 1e-06)
    return (floats / norms, norms)

def back_rows(grads, units, norms):
    return (grads - units * lax.optimization_barrier(jnp.sum(units * grads, 1, keepdims=True))) / norms

def reference(images, texts, scale, shift):
    image_unit, image_norm = unit_rows(images)
    text_unit, text_norm = unit_rows(texts)
    image_emb = image_unit.astype(jnp.bfloat16)
    text_emb = text_unit.astype(jnp.bfloat16)
    total = images.shape[0]
    width = 512 if total % 512 == 0 else total
    count = total // width
    blocks = image_emb.reshape(count, width, -1)

    def step(carry, item):
        block, index = item
        logit = scale * lax.dot_general(block, text_emb, (((1,), (1,)), ((), ())), preferred_element_type=jnp.float32) + shift
        rows_ids = index * width + jnp.arange(width, dtype=jnp.int32)[:, None]
        cols_ids = jnp.arange(total, dtype=jnp.int32)[None, :]
        label = (rows_ids == cols_ids).astype(jnp.float32)
        loss = lax.optimization_barrier(jnp.sum(jax.nn.softplus(logit * (1.0 - 2.0 * label)), 1)) / total
        coef = ((jax.nn.sigmoid(logit) - label) * scale).astype(jnp.bfloat16)
        grad_image = jnp.dot(coef, text_emb, preferred_element_type=jnp.float32)
        carry = carry + lax.dot_general(coef, block, (((0,), (0,)), ((), ())), preferred_element_type=jnp.float32)
        return (carry, (loss, grad_image))
    start = jnp.zeros((total, images.shape[1]), jnp.float32)
    text_sum, (losses, image_sum) = lax.scan(step, start, (blocks, jnp.arange(count, dtype=jnp.int32)))
    image_grad = back_rows(image_sum.reshape(total, -1), image_unit, image_norm)
    text_grad = back_rows(text_sum, text_unit, text_norm)
    return (losses.reshape(total), image_grad, text_grad)
```

```python
import jax
import jax.numpy as jnp
from jax import lax
from jax.sharding import PartitionSpec as P


def unit_rows(values):
    floats = values.astype(jnp.float32)
    norms = jnp.sqrt(jnp.sum(floats * floats, 1, keepdims=True) + 1e-06)
    return (floats / norms, norms)


def back_rows(grads, units, norms):
    return (grads - units * jnp.sum(units * grads, 1, keepdims=True)) / norms


def local(images, texts, scale, shift):
    rows = images.shape[0]
    image_unit, image_norm = unit_rows(images)
    text_unit, text_norm = unit_rows(texts)
    image_emb = image_unit.astype(jnp.bfloat16)
    text_emb = text_unit.astype(jnp.bfloat16)
    groups = lax.axis_size("grp")
    loops = lax.axis_size("blk")
    total = loops * groups * rows
    gathered = lax.all_gather(image_emb, "grp", axis=0, tiled=True)
    seen = lax.all_gather(text_emb, "blk", axis=0, tiled=True)
    place = lax.axis_index("grp")
    here = lax.axis_index("blk")
    image_ids = jnp.arange(groups * rows, dtype=jnp.int32)[:, None]
    column_ids = place * rows + (jnp.arange(loops * rows, dtype=jnp.int32) % rows)[None, :]
    column_blk = (jnp.arange(loops * rows, dtype=jnp.int32) // rows)[None, :]
    label = ((image_ids == column_ids) & (column_blk == here)).astype(jnp.float32)
    logit = (
        scale
        * lax.dot_general(gathered, seen, (((1,), (1,)), ((), ())), preferred_element_type=jnp.float32)
        + shift
    )
    loss = jnp.sum(jax.nn.softplus(logit * (1.0 - 2.0 * label)), 1) / total
    coef = ((jax.nn.sigmoid(logit) - label) * scale).astype(jnp.bfloat16)
    image_part = jnp.dot(coef, seen, preferred_element_type=jnp.float32)
    text_part = lax.dot_general(coef, gathered, (((0,), (0,)), ((), ())), preferred_element_type=jnp.float32)
    image_sum = lax.psum_scatter(image_part, "grp", scatter_dimension=0, tiled=True)
    image_loss = lax.psum_scatter(loss, "grp", scatter_dimension=0, tiled=True)
    text_sum = lax.psum_scatter(text_part, "blk", scatter_dimension=0, tiled=True)
    image_grad = back_rows(image_sum, image_unit, image_norm)
    text_grad = back_rows(text_sum, text_unit, text_norm)
    return (image_loss, image_grad, text_grad)


def solution(mesh):
    in_specs = (P(("blk", "grp"), None), P(("blk", "grp"), None), P(), P())
    out_specs = (P(("blk", "grp")), P(("blk", "grp"), None), P(("blk", "grp"), None))
    return jax.shard_map(local, mesh=mesh, in_specs=in_specs, out_specs=out_specs, check_vma=False)
```

```python
import jax
import jax.numpy as jnp
from jax import lax
from jax.sharding import PartitionSpec as P


def unit_rows(values):
    floats = values.astype(jnp.float32)
    norms = jnp.sqrt(jnp.sum(floats * floats, 1, keepdims=True) + 1e-06)
    return (floats / norms, norms)


def back_rows(grads, units, norms):
    return (grads - units * jnp.sum(units * grads, 1, keepdims=True)) / norms


def spread(block, axis, count):
    copies = jnp.tile(block, (count,) + (1,) * (block.ndim - 1))
    return lax.all_to_all(copies, axis, 0, 0, tiled=True)


def gather_sum(parts, axis, count):
    received = lax.all_to_all(parts, axis, 0, 0, tiled=True)
    return jnp.sum(received.reshape((count, -1) + parts.shape[1:]), 0)


def local(images, texts, scale, shift):
    rows = images.shape[0]
    image_unit, image_norm = unit_rows(images)
    text_unit, text_norm = unit_rows(texts)
    image_emb = image_unit.astype(jnp.bfloat16)
    text_emb = text_unit.astype(jnp.bfloat16)
    groups = lax.axis_size("grp")
    loops = lax.axis_size("blk")
    total = loops * groups * rows
    gathered = spread(image_emb, "grp", groups)
    seen = spread(text_emb, "blk", loops)
    place = lax.axis_index("grp")
    here = lax.axis_index("blk")
    image_ids = jnp.arange(groups * rows, dtype=jnp.int32)[:, None]
    column_ids = place * rows + (jnp.arange(loops * rows, dtype=jnp.int32) % rows)[None, :]
    column_blk = (jnp.arange(loops * rows, dtype=jnp.int32) // rows)[None, :]
    label = ((image_ids == column_ids) & (column_blk == here)).astype(jnp.float32)
    logit = (
        scale
        * lax.dot_general(gathered, seen, (((1,), (1,)), ((), ())), preferred_element_type=jnp.float32)
        + shift
    )
    loss = jnp.sum(jax.nn.softplus(logit * (1.0 - 2.0 * label)), 1) / total
    coef = ((jax.nn.sigmoid(logit) - label) * scale).astype(jnp.bfloat16)
    image_part = jnp.dot(coef, seen, preferred_element_type=jnp.float32)
    text_part = lax.dot_general(coef, gathered, (((0,), (0,)), ((), ())), preferred_element_type=jnp.float32)
    image_sum = gather_sum(image_part, "grp", groups)
    image_loss = gather_sum(loss, "grp", groups)
    text_sum = gather_sum(text_part, "blk", loops)
    image_grad = back_rows(image_sum, image_unit, image_norm)
    text_grad = back_rows(text_sum, text_unit, text_norm)
    return (image_loss, image_grad, text_grad)


def solution(mesh):
    in_specs = (P(("blk", "grp"), None), P(("blk", "grp"), None), P(), P())
    out_specs = (P(("blk", "grp")), P(("blk", "grp"), None), P(("blk", "grp"), None))
    return jax.shard_map(local, mesh=mesh, in_specs=in_specs, out_specs=out_specs, check_vma=False)
```

```python
import jax
import jax.numpy as jnp
from jax import lax
from jax.sharding import Mesh, PartitionSpec as P

ROWS_AXES = ("x", "zh", "y", "zl", "c")
IMAGE_AXES = ("x", "y", "c")
TEXT_AXES = ("zh", "zl")


def unit_rows(values):
    floats = values.astype(jnp.float32)
    norms = jnp.sqrt(jnp.sum(floats * floats, 1, keepdims=True) + 1e-06)
    return (floats / norms, norms)


def back_rows(grads, units, norms):
    return (grads - units * jnp.sum(units * grads, 1, keepdims=True)) / norms


def linear_index(axes):
    index = 0
    for name in axes:
        index = index * lax.axis_size(name) + lax.axis_index(name)
    return index


def group_size(axes):
    size = 1
    for name in axes:
        size *= lax.axis_size(name)
    return size


def spread(block, axes, count):
    copies = jnp.tile(block, (count,) + (1,) * (block.ndim - 1))
    return lax.all_to_all(copies, axes, 0, 0, tiled=True)


def gather_sum(parts, axes, count):
    received = lax.all_to_all(parts, axes, 0, 0, tiled=True)
    return jnp.sum(received.reshape((count, -1) + parts.shape[1:]), 0)


def local(images, texts, scale, shift):
    rows = images.shape[0]
    image_unit, image_norm = unit_rows(images)
    text_unit, text_norm = unit_rows(texts)
    image_emb = image_unit.astype(jnp.bfloat16)
    text_emb = text_unit.astype(jnp.bfloat16)
    image_count = group_size(IMAGE_AXES)
    text_count = group_size(TEXT_AXES)
    total = image_count * text_count * rows
    gathered = spread(image_emb, IMAGE_AXES, image_count)
    seen = spread(text_emb, TEXT_AXES, text_count)
    image_ids = jnp.arange(image_count * rows, dtype=jnp.int32)[:, None]
    text_ids = jnp.arange(text_count * rows, dtype=jnp.int32)[None, :]
    mine_i = linear_index(IMAGE_AXES)
    mine_t = linear_index(TEXT_AXES)
    label = (
        (image_ids // rows == mine_i) & (text_ids // rows == mine_t) & (image_ids % rows == text_ids % rows)
    ).astype(jnp.float32)
    logit = (
        scale
        * lax.dot_general(gathered, seen, (((1,), (1,)), ((), ())), preferred_element_type=jnp.float32)
        + shift
    )
    loss = jnp.sum(jax.nn.softplus(logit * (1.0 - 2.0 * label)), 1) / total
    coef = ((jax.nn.sigmoid(logit) - label) * scale).astype(jnp.bfloat16)
    image_part = jnp.dot(coef, seen, preferred_element_type=jnp.float32)
    text_part = lax.dot_general(coef, gathered, (((0,), (0,)), ((), ())), preferred_element_type=jnp.float32)
    image_sum = gather_sum(image_part, IMAGE_AXES, image_count)
    image_loss = gather_sum(loss, IMAGE_AXES, image_count)
    text_sum = gather_sum(text_part, TEXT_AXES, text_count)
    image_grad = back_rows(image_sum, image_unit, image_norm)
    text_grad = back_rows(text_sum, text_unit, text_norm)
    return (image_loss, image_grad, text_grad)


def solution(mesh):
    blk, grp = mesh.devices.shape
    fine = Mesh(mesh.devices.reshape(blk // 2, 2, grp // 16, 8, 2), ROWS_AXES)
    in_specs = (P(ROWS_AXES, None), P(ROWS_AXES, None), P(), P())
    out_specs = (P(ROWS_AXES), P(ROWS_AXES, None), P(ROWS_AXES, None))
    return jax.shard_map(local, mesh=fine, in_specs=in_specs, out_specs=out_specs, check_vma=False)
```

```python
import functools

import jax
import jax.numpy as jnp
from jax import lax
from jax.experimental import pallas as pl
from jax.experimental.pallas import tpu as pltpu
from jax.sharding import Mesh, PartitionSpec as P

ROWS_AXES = ("x", "zh", "y", "zl", "c")
IMAGE_AXES = ("x", "y", "c")
TEXT_AXES = ("zh", "zl")
MESH_IDS = pl.DeviceIdType.MESH
LOSS_LANES = 128


def unit_rows(values):
    floats = values.astype(jnp.float32)
    norms = jnp.sqrt(jnp.sum(floats * floats, 1, keepdims=True) + 1e-06)
    return (floats / norms, norms)


def back_rows(grads, units, norms):
    return (grads - units * jnp.sum(units * grads, 1, keepdims=True)) / norms


def linear_index(axes):
    index = 0
    for name in axes:
        index = index * lax.axis_size(name) + lax.axis_index(name)
    return index


def group_size(axes):
    size = 1
    for name in axes:
        size *= lax.axis_size(name)
    return size


def member(axes, k):
    coords = {}
    for name in reversed(axes):
        size = lax.axis_size(name)
        coords[name] = k % size
        k = k // size
    return tuple(coords[name] if name in coords else lax.axis_index(name) for name in ROWS_AXES)


def exchange_kernel(scatter, image_src, text_src, image_out, text_out, image_send, image_recv, text_send, text_recv):
    groups = ((IMAGE_AXES, image_src, image_out, image_send, image_recv),
              (TEXT_AXES, text_src, text_out, text_send, text_recv))
    barrier = pltpu.get_barrier_semaphore()
    peers = 0
    for axes, src, out, send, recv in groups:
        count, me = group_size(axes), linear_index(axes)
        peers += count - 1

        def greet(step, carry, axes=axes, count=count, me=me):
            pl.semaphore_signal(barrier, 1, device_id=member(axes, (me + step) % count), device_id_type=MESH_IDS)
            return carry

        lax.fori_loop(1, count, greet, 0)
    pl.semaphore_wait(barrier, peers)

    for axes, src, out, send, recv in groups:
        count, me = group_size(axes), linear_index(axes)
        out[me] = src[me] if scatter else src[...]

        def start(step, carry, axes=axes, count=count, me=me, src=src, out=out, send=send, recv=recv):
            peer = (me + step) % count
            pltpu.make_async_remote_copy(
                src.at[peer] if scatter else src, out.at[me], send.at[peer], recv.at[me],
                device_id=member(axes, peer), device_id_type=MESH_IDS,
            ).start()
            return carry

        lax.fori_loop(1, count, start, 0)

    for axes, src, out, send, recv in groups:
        count, me = group_size(axes), linear_index(axes)

        def finish(step, carry, axes=axes, count=count, me=me, src=src, out=out, send=send, recv=recv):
            peer = (me + step) % count
            copy = pltpu.make_async_remote_copy(
                src.at[peer] if scatter else src, out.at[peer], send.at[peer], recv.at[peer],
                device_id=member(axes, peer), device_id_type=MESH_IDS,
            )
            copy.wait_send()
            copy.wait_recv()
            return carry

        lax.fori_loop(1, count, finish, 0)


def exchange(image_src, text_src, scatter, tag):
    image_count, text_count = group_size(IMAGE_AXES), group_size(TEXT_AXES)
    image_shape = image_src.shape if scatter else (image_count,) + image_src.shape
    text_shape = text_src.shape if scatter else (text_count,) + text_src.shape
    vmem = pl.BlockSpec(memory_space=pltpu.VMEM)
    return pl.pallas_call(
        functools.partial(exchange_kernel, scatter),
        out_shape=(jax.ShapeDtypeStruct(image_shape, image_src.dtype), jax.ShapeDtypeStruct(text_shape, text_src.dtype)),
        in_specs=[vmem, vmem],
        out_specs=(vmem, vmem),
        scratch_shapes=[
            pltpu.SemaphoreType.DMA((image_count,)),
            pltpu.SemaphoreType.DMA((image_count,)),
            pltpu.SemaphoreType.DMA((text_count,)),
            pltpu.SemaphoreType.DMA((text_count,)),
        ],
        compiler_params=pltpu.CompilerParams(collective_id=tag, has_side_effects=True),
    )(image_src, text_src)


def local(images, texts, scale, shift):
    rows, width = images.shape
    image_unit, image_norm = unit_rows(images)
    text_unit, text_norm = unit_rows(texts)
    image_emb = image_unit.astype(jnp.bfloat16)
    text_emb = text_unit.astype(jnp.bfloat16)
    image_count = group_size(IMAGE_AXES)
    text_count = group_size(TEXT_AXES)
    total = image_count * text_count * rows
    gathered, seen = exchange(image_emb, text_emb, False, 0)
    gathered = gathered.reshape(image_count * rows, width)
    seen = seen.reshape(text_count * rows, width)
    image_ids = jnp.arange(image_count * rows, dtype=jnp.int32)[:, None]
    text_ids = jnp.arange(text_count * rows, dtype=jnp.int32)[None, :]
    mine_i = linear_index(IMAGE_AXES)
    mine_t = linear_index(TEXT_AXES)
    label = (
        (image_ids // rows == mine_i) & (text_ids // rows == mine_t) & (image_ids % rows == text_ids % rows)
    ).astype(jnp.float32)
    logit = (
        scale
        * lax.dot_general(gathered, seen, (((1,), (1,)), ((), ())), preferred_element_type=jnp.float32)
        + shift
    )
    loss = jnp.sum(jax.nn.softplus(logit * (1.0 - 2.0 * label)), 1, keepdims=True) / total
    coef = ((jax.nn.sigmoid(logit) - label) * scale).astype(jnp.bfloat16)
    image_part = jnp.dot(coef, seen, preferred_element_type=jnp.float32)
    text_part = lax.dot_general(coef, gathered, (((0,), (0,)), ((), ())), preferred_element_type=jnp.float32)
    image_part = jnp.concatenate([image_part, jnp.broadcast_to(loss, (image_count * rows, LOSS_LANES))], 1)
    image_in, text_in = exchange(
        image_part.reshape(image_count, rows, width + LOSS_LANES), text_part.reshape(text_count, rows, width), True, 1
    )
    image_in = jnp.sum(image_in, 0)
    text_sum = jnp.sum(text_in, 0)
    image_grad = back_rows(image_in[:, :width], image_unit, image_norm)
    text_grad = back_rows(text_sum, text_unit, text_norm)
    return (image_in[:, width], image_grad, text_grad)


def solution(mesh):
    blk, grp = mesh.devices.shape
    fine = Mesh(mesh.devices.reshape(blk // 2, 2, grp // 16, 8, 2), ROWS_AXES)
    in_specs = (P(ROWS_AXES, None), P(ROWS_AXES, None), P(), P())
    out_specs = (P(ROWS_AXES), P(ROWS_AXES, None), P(ROWS_AXES, None))
    return jax.shard_map(local, mesh=fine, in_specs=in_specs, out_specs=out_specs, check_vma=False)
```

```python
import functools

import jax
import jax.numpy as jnp
from jax import lax
from jax.experimental import pallas as pl
from jax.experimental.pallas import tpu as pltpu
from jax.sharding import Mesh, PartitionSpec as P

ROWS_AXES = ("x", "zh", "y", "zl", "c")
CHIP_AXES = ("x", "y")
CORE_AXES = ("c",)
TEXT_AXES = ("zh", "zl")
MESH_IDS = pl.DeviceIdType.MESH
LOSS_LANES = 128


def unit_rows(values):
    floats = values.astype(jnp.float32)
    norms = jnp.sqrt(jnp.sum(floats * floats, 1, keepdims=True) + 1e-06)
    return (floats / norms, norms)


def back_rows(grads, units, norms):
    return (grads - units * jnp.sum(units * grads, 1, keepdims=True)) / norms


def linear_index(axes):
    index = 0
    for name in axes:
        index = index * lax.axis_size(name) + lax.axis_index(name)
    return index


def group_size(axes):
    size = 1
    for name in axes:
        size *= lax.axis_size(name)
    return size


def member(axes, k):
    coords = {}
    for name in reversed(axes):
        size = lax.axis_size(name)
        coords[name] = k % size
        k = k // size
    return tuple(coords[name] if name in coords else lax.axis_index(name) for name in ROWS_AXES)


def exchange_kernel(plan, *refs):
    count_groups = len(plan)
    srcs, outs = refs[:count_groups], refs[count_groups:2 * count_groups]
    sems = refs[2 * count_groups:]
    groups = [
        (axes, scatter, srcs[g], outs[g], sems[2 * g], sems[2 * g + 1]) for g, (axes, scatter) in enumerate(plan)
    ]
    barrier = pltpu.get_barrier_semaphore()
    peers = 0
    for axes, scatter, src, out, send, recv in groups:
        count, me = group_size(axes), linear_index(axes)
        peers += count - 1

        def greet(step, carry, axes=axes, count=count, me=me):
            pl.semaphore_signal(barrier, 1, device_id=member(axes, (me + step) % count), device_id_type=MESH_IDS)
            return carry

        lax.fori_loop(1, count, greet, 0)
    pl.semaphore_wait(barrier, peers)

    for axes, scatter, src, out, send, recv in groups:
        count, me = group_size(axes), linear_index(axes)

        def start(step, carry, axes=axes, scatter=scatter, count=count, me=me, src=src, out=out, send=send, recv=recv):
            peer = (me + step) % count
            pltpu.make_async_remote_copy(
                src.at[peer] if scatter else src, out.at[me], send.at[peer], recv.at[me],
                device_id=member(axes, peer), device_id_type=MESH_IDS,
            ).start()
            return carry

        lax.fori_loop(1, count, start, 0)

    for axes, scatter, src, out, send, recv in groups:
        count, me = group_size(axes), linear_index(axes)
        out[me] = src[me] if scatter else src[...]

    for axes, scatter, src, out, send, recv in groups:
        count, me = group_size(axes), linear_index(axes)

        def finish(step, carry, axes=axes, scatter=scatter, count=count, me=me, src=src, out=out, send=send, recv=recv):
            peer = (me + step) % count
            copy = pltpu.make_async_remote_copy(
                src.at[peer] if scatter else src, out.at[peer], send.at[peer], recv.at[peer],
                device_id=member(axes, peer), device_id_type=MESH_IDS,
            )
            copy.wait_send()
            copy.wait_recv()
            return carry

        lax.fori_loop(1, count, finish, 0)


def exchange(routes, tag):
    plan = tuple((axes, scatter) for axes, src, scatter in routes)
    srcs = [src for axes, src, scatter in routes]
    shapes = [
        jax.ShapeDtypeStruct(src.shape if scatter else (group_size(axes),) + src.shape, src.dtype)
        for axes, src, scatter in routes
    ]
    sems = []
    for axes, src, scatter in routes:
        sems += [pltpu.SemaphoreType.DMA((group_size(axes),))] * 2
    vmem = pl.BlockSpec(memory_space=pltpu.VMEM)
    return pl.pallas_call(
        functools.partial(exchange_kernel, plan),
        out_shape=tuple(shapes),
        in_specs=[vmem] * len(routes),
        out_specs=tuple([vmem] * len(routes)),
        scratch_shapes=sems,
        compiler_params=pltpu.CompilerParams(collective_id=tag, has_side_effects=True),
    )(*srcs)


def local(images, texts, scale, shift):
    rows, width = images.shape
    image_unit, image_norm = unit_rows(images)
    text_unit, text_norm = unit_rows(texts)
    image_emb = image_unit.astype(jnp.bfloat16)
    text_emb = text_unit.astype(jnp.bfloat16)
    chips = group_size(CHIP_AXES)
    cores = group_size(CORE_AXES)
    image_count = chips * cores
    text_count = group_size(TEXT_AXES)
    total = image_count * text_count * rows
    same_core, seen = exchange([(CHIP_AXES, image_emb, False), (TEXT_AXES, text_emb, False)], 0)
    (gathered,) = exchange([(CORE_AXES, same_core, False)], 1)
    gathered = gathered.reshape(image_count * rows, width)
    seen = seen.reshape(text_count * rows, width)
    image_ids = jnp.arange(image_count * rows, dtype=jnp.int32)[:, None]
    text_ids = jnp.arange(text_count * rows, dtype=jnp.int32)[None, :]
    mine_i = linear_index(CORE_AXES + CHIP_AXES)
    mine_t = linear_index(TEXT_AXES)
    label = (
        (image_ids // rows == mine_i) & (text_ids // rows == mine_t) & (image_ids % rows == text_ids % rows)
    ).astype(jnp.float32)
    logit = (
        scale
        * lax.dot_general(gathered, seen, (((1,), (1,)), ((), ())), preferred_element_type=jnp.float32)
        + shift
    )
    loss = jnp.sum(jax.nn.softplus(logit * (1.0 - 2.0 * label)), 1, keepdims=True) / total
    coef = ((jax.nn.sigmoid(logit) - label) * scale).astype(jnp.bfloat16)
    image_part = jnp.dot(coef, seen, preferred_element_type=jnp.float32)
    text_part = lax.dot_general(coef, gathered, (((0,), (0,)), ((), ())), preferred_element_type=jnp.float32)
    image_part = jnp.concatenate([image_part, jnp.broadcast_to(loss, (image_count * rows, LOSS_LANES))], 1)
    (halves,) = exchange([(CORE_AXES, image_part.reshape(cores, chips, rows, width + LOSS_LANES), True)], 2)
    chip_sum = jnp.sum(halves, 0)
    image_in, text_in = exchange(
        [(CHIP_AXES, chip_sum, True), (TEXT_AXES, text_part.reshape(text_count, rows, width), True)], 3
    )
    image_in = jnp.sum(image_in, 0)
    text_sum = jnp.sum(text_in, 0)
    image_grad = back_rows(image_in[:, :width], image_unit, image_norm)
    text_grad = back_rows(text_sum, text_unit, text_norm)
    return (image_in[:, width], image_grad, text_grad)


def solution(mesh):
    blk, grp = mesh.devices.shape
    fine = Mesh(mesh.devices.reshape(blk // 2, 2, grp // 16, 8, 2), ROWS_AXES)
    in_specs = (P(ROWS_AXES, None), P(ROWS_AXES, None), P(), P())
    out_specs = (P(ROWS_AXES), P(ROWS_AXES, None), P(ROWS_AXES, None))
    return jax.shard_map(local, mesh=fine, in_specs=in_specs, out_specs=out_specs, check_vma=False)
```

```python
import functools

import jax
import jax.numpy as jnp
from jax import lax
from jax.experimental import pallas as pl
from jax.experimental.pallas import tpu as pltpu
from jax.sharding import Mesh, PartitionSpec as P

ROWS_AXES = ("x", "zh", "y", "zl", "c")
IMAGE_AXES = ("x", "y", "c")
TEXT_AXES = ("zh", "zl")
MESH_IDS = pl.DeviceIdType.MESH
LOSS_LANES = 128


def unit_rows(values):
    floats = values.astype(jnp.float32)
    norms = jnp.sqrt(jnp.sum(floats * floats, 1, keepdims=True) + 1e-06)
    return (floats / norms, norms)


def back_rows(grads, units, norms):
    return (grads - units * jnp.sum(units * grads, 1, keepdims=True)) / norms


def linear_index(axes):
    index = 0
    for name in axes:
        index = index * lax.axis_size(name) + lax.axis_index(name)
    return index


def group_size(axes):
    size = 1
    for name in axes:
        size *= lax.axis_size(name)
    return size


def member(axes, k):
    coords = {}
    for name in reversed(axes):
        size = lax.axis_size(name)
        coords[name] = k % size
        k = k // size
    return tuple(coords[name] if name in coords else lax.axis_index(name) for name in ROWS_AXES)


def ring_peers():
    count, me = group_size(TEXT_AXES), linear_index(TEXT_AXES)
    return count, me, member(TEXT_AXES, (me + 1) % count), member(TEXT_AXES, (me + count - 1) % count)


def remote(src, dst, send, recv, device):
    return pltpu.make_async_remote_copy(src, dst, send, recv, device_id=device, device_id_type=MESH_IDS)


def greet_all(barrier, image_count, image_me, right, left):
    def greet(step, carry):
        pl.semaphore_signal(barrier, 1, device_id=member(IMAGE_AXES, (image_me + step) % image_count),
                            device_id_type=MESH_IDS)
        return carry

    lax.fori_loop(1, image_count, greet, 0)
    for device in (right, left):
        pl.semaphore_signal(barrier, 1, device_id=device, device_id_type=MESH_IDS)
    pl.semaphore_wait(barrier, image_count + 1)


def image_direct(scatter, src, out, send, recv, count, me):
    def start(step, carry):
        peer = (me + step) % count
        remote(src.at[peer] if scatter else src, out.at[me], send.at[peer], recv.at[me],
               member(IMAGE_AXES, peer)).start()
        return carry

    lax.fori_loop(1, count, start, 0)
    out[me] = src[me] if scatter else src[...]

    def finish(step, carry):
        peer = (me + step) % count
        copy = remote(src.at[peer] if scatter else src, out.at[peer], send.at[peer], recv.at[peer],
                      member(IMAGE_AXES, peer))
        copy.wait_send()
        copy.wait_recv()
        return carry

    return finish


def gather_kernel(image_src, text_src, image_out, text_out, image_send, image_recv, text_send, text_recv):
    image_count, image_me = group_size(IMAGE_AXES), linear_index(IMAGE_AXES)
    count, me, right, left = ring_peers()
    half = count // 2
    greet_all(pltpu.get_barrier_semaphore(), image_count, image_me, right, left)
    finish = image_direct(False, image_src, image_out, image_send, image_recv, image_count, image_me)
    sends = [remote(text_src, text_out.at[me], text_send.at[0], text_recv.at[me], right),
             remote(text_src, text_out.at[me], text_send.at[half], text_recv.at[me], left)]
    for copy in sends:
        copy.start()
    text_out[me] = text_src[...]
    for step in range(1, half):
        for origin, device, slot in (((me + count - step) % count, right, step), ((me + step) % count, left, half + step)):
            if slot >= count - 1:
                continue
            arrived = remote(text_out.at[origin], text_out.at[origin], text_send.at[slot], text_recv.at[origin], device)
            arrived.wait_recv()
            arrived.start()
            sends.append(arrived)
    for origin in ((me + count - half) % count, (me + half - 1) % count):
        remote(text_out.at[origin], text_out.at[origin], text_send.at[0], text_recv.at[origin], right).wait_recv()
    for copy in sends:
        copy.wait_send()
    lax.fori_loop(1, image_count, finish, 0)


def reduce_kernel(image_src, text_src, image_out, text_out, image_send, image_recv, text_send, text_recv,
                  inbox, outbox):
    image_count, image_me = group_size(IMAGE_AXES), linear_index(IMAGE_AXES)
    count, me, right, left = ring_peers()
    half = count // 2
    greet_all(pltpu.get_barrier_semaphore(), image_count, image_me, right, left)
    finish = image_direct(True, image_src, image_out, image_send, image_recv, image_count, image_me)
    sends = [remote(text_src.at[(me + half) % count], inbox.at[0], text_send.at[0], text_recv.at[0], right),
             remote(text_src.at[(me + half + 1) % count], inbox.at[half], text_send.at[half], text_recv.at[half], left)]
    for copy in sends:
        copy.start()
    for step in range(1, half):
        chains = ((step, (me + half - step) % count, right), (half + step, (me + half + 1 + step) % count, left))
        for slot, target, device in chains:
            if slot >= count - 1:
                continue
            remote(inbox.at[slot - 1], inbox.at[slot - 1], text_send.at[slot], text_recv.at[slot - 1], device).wait_recv()
            outbox[slot] = inbox[slot - 1] + text_src[target]
            copy = remote(outbox.at[slot], inbox.at[slot], text_send.at[slot], text_recv.at[slot], device)
            copy.start()
            sends.append(copy)
    last_right, last_left = half - 1, count - 2
    for slot in (last_right, last_left):
        remote(inbox.at[slot], inbox.at[slot], text_send.at[0], text_recv.at[slot], right).wait_recv()
    text_out[...] = text_src[me] + inbox[last_right] + inbox[last_left]
    for copy in sends:
        copy.wait_send()
    lax.fori_loop(1, image_count, finish, 0)


def exchange(image_src, text_src, scatter, tag):
    image_count, text_count = group_size(IMAGE_AXES), group_size(TEXT_AXES)
    image_shape = image_src.shape if scatter else (image_count,) + image_src.shape
    text_shape = text_src.shape[1:] if scatter else (text_count,) + text_src.shape
    block = text_src.shape[1:] if scatter else text_src.shape
    vmem = pl.BlockSpec(memory_space=pltpu.VMEM)
    scratch = [
        pltpu.SemaphoreType.DMA((image_count,)),
        pltpu.SemaphoreType.DMA((image_count,)),
        pltpu.SemaphoreType.DMA((text_count,)),
        pltpu.SemaphoreType.DMA((text_count,)),
    ]
    if scatter:
        scratch += [pltpu.VMEM((text_count,) + block, text_src.dtype)] * 2
    return pl.pallas_call(
        reduce_kernel if scatter else gather_kernel,
        out_shape=(jax.ShapeDtypeStruct(image_shape, image_src.dtype), jax.ShapeDtypeStruct(text_shape, text_src.dtype)),
        in_specs=[vmem, vmem],
        out_specs=(vmem, vmem),
        scratch_shapes=scratch,
        compiler_params=pltpu.CompilerParams(collective_id=tag, has_side_effects=True),
    )(image_src, text_src)


def local(images, texts, scale, shift):
    rows, width = images.shape
    image_unit, image_norm = unit_rows(images)
    text_unit, text_norm = unit_rows(texts)
    image_emb = image_unit.astype(jnp.bfloat16)
    text_emb = text_unit.astype(jnp.bfloat16)
    image_count = group_size(IMAGE_AXES)
    text_count = group_size(TEXT_AXES)
    total = image_count * text_count * rows
    gathered, seen = exchange(image_emb, text_emb, False, 0)
    gathered = gathered.reshape(image_count * rows, width)
    seen = seen.reshape(text_count * rows, width)
    image_ids = jnp.arange(image_count * rows, dtype=jnp.int32)[:, None]
    text_ids = jnp.arange(text_count * rows, dtype=jnp.int32)[None, :]
    mine_i = linear_index(IMAGE_AXES)
    mine_t = linear_index(TEXT_AXES)
    label = (
        (image_ids // rows == mine_i) & (text_ids // rows == mine_t) & (image_ids % rows == text_ids % rows)
    ).astype(jnp.float32)
    logit = (
        scale
        * lax.dot_general(gathered, seen, (((1,), (1,)), ((), ())), preferred_element_type=jnp.float32)
        + shift
    )
    loss = jnp.sum(jax.nn.softplus(logit * (1.0 - 2.0 * label)), 1, keepdims=True) / total
    coef = ((jax.nn.sigmoid(logit) - label) * scale).astype(jnp.bfloat16)
    image_part = jnp.dot(coef, seen, preferred_element_type=jnp.float32)
    text_part = lax.dot_general(coef, gathered, (((0,), (0,)), ((), ())), preferred_element_type=jnp.float32)
    image_part = jnp.concatenate([image_part, jnp.broadcast_to(loss, (image_count * rows, LOSS_LANES))], 1)
    image_in, text_in = exchange(
        image_part.reshape(image_count, rows, width + LOSS_LANES), text_part.reshape(text_count, rows, width), True, 1
    )
    image_in = jnp.sum(image_in, 0)
    text_sum = text_in
    image_grad = back_rows(image_in[:, :width], image_unit, image_norm)
    text_grad = back_rows(text_sum, text_unit, text_norm)
    return (image_in[:, width], image_grad, text_grad)


def solution(mesh):
    blk, grp = mesh.devices.shape
    fine = Mesh(mesh.devices.reshape(blk // 2, 2, grp // 16, 8, 2), ROWS_AXES)
    in_specs = (P(ROWS_AXES, None), P(ROWS_AXES, None), P(), P())
    out_specs = (P(ROWS_AXES), P(ROWS_AXES, None), P(ROWS_AXES, None))
    return jax.shard_map(local, mesh=fine, in_specs=in_specs, out_specs=out_specs, check_vma=False)
```

```python
import functools

import jax
import jax.numpy as jnp
from jax import lax
from jax.experimental import pallas as pl
from jax.experimental.pallas import tpu as pltpu
from jax.sharding import Mesh, PartitionSpec as P

ROWS_AXES = ("x", "zh", "y", "zl", "c")
CHIP_AXES = ("x", "y")
CORE_AXES = ("c",)
TEXT_AXES = ("zh", "zl")
MESH_IDS = pl.DeviceIdType.MESH
LOSS_LANES = 128


def unit_rows(values):
    floats = values.astype(jnp.float32)
    norms = jnp.sqrt(jnp.sum(floats * floats, 1, keepdims=True) + 1e-06)
    return (floats / norms, norms)


def back_rows(grads, units, norms):
    return (grads - units * jnp.sum(units * grads, 1, keepdims=True)) / norms


def linear_index(axes):
    index = 0
    for name in axes:
        index = index * lax.axis_size(name) + lax.axis_index(name)
    return index


def group_size(axes):
    size = 1
    for name in axes:
        size *= lax.axis_size(name)
    return size


def member(axes, k):
    coords = {}
    for name in reversed(axes):
        size = lax.axis_size(name)
        coords[name] = k % size
        k = k // size
    return tuple(coords[name] if name in coords else lax.axis_index(name) for name in ROWS_AXES)


def ring_peers():
    count, me = group_size(TEXT_AXES), linear_index(TEXT_AXES)
    return count, me, member(TEXT_AXES, (me + 1) % count), member(TEXT_AXES, (me + count - 1) % count)


def remote(src, dst, send, recv, device):
    return pltpu.make_async_remote_copy(src, dst, send, recv, device_id=device, device_id_type=MESH_IDS)


def greet_all(image_axes, barrier, image_count, image_me, right, left):
    def greet(step, carry):
        pl.semaphore_signal(barrier, 1, device_id=member(image_axes, (image_me + step) % image_count),
                            device_id_type=MESH_IDS)
        return carry

    lax.fori_loop(1, image_count, greet, 0)
    for device in (right, left):
        pl.semaphore_signal(barrier, 1, device_id=device, device_id_type=MESH_IDS)
    pl.semaphore_wait(barrier, image_count + 1)


def image_direct(image_axes, scatter, src, out, send, recv, count, me):
    def start(step, carry):
        peer = (me + step) % count
        remote(src.at[peer] if scatter else src, out.at[me], send.at[peer], recv.at[me],
               member(image_axes, peer)).start()
        return carry

    lax.fori_loop(1, count, start, 0)
    out[me] = src[me] if scatter else src[...]

    def finish(step, carry):
        peer = (me + step) % count
        copy = remote(src.at[peer] if scatter else src, out.at[peer], send.at[peer], recv.at[peer],
                      member(image_axes, peer))
        copy.wait_send()
        copy.wait_recv()
        return carry

    return finish


def gather_kernel(image_axes, image_src, text_src, image_out, text_out, image_send, image_recv, text_send, text_recv):
    image_count, image_me = group_size(image_axes), linear_index(image_axes)
    count, me, right, left = ring_peers()
    half = count // 2
    greet_all(image_axes, pltpu.get_barrier_semaphore(), image_count, image_me, right, left)
    finish = image_direct(image_axes, False, image_src, image_out, image_send, image_recv, image_count, image_me)
    sends = [remote(text_src, text_out.at[me], text_send.at[0], text_recv.at[me], right),
             remote(text_src, text_out.at[me], text_send.at[half], text_recv.at[me], left)]
    for copy in sends:
        copy.start()
    text_out[me] = text_src[...]
    for step in range(1, half):
        for origin, device, slot in (((me + count - step) % count, right, step), ((me + step) % count, left, half + step)):
            if slot >= count - 1:
                continue
            arrived = remote(text_out.at[origin], text_out.at[origin], text_send.at[slot], text_recv.at[origin], device)
            arrived.wait_recv()
            arrived.start()
            sends.append(arrived)
    for origin in ((me + count - half) % count, (me + half - 1) % count):
        remote(text_out.at[origin], text_out.at[origin], text_send.at[0], text_recv.at[origin], right).wait_recv()
    for copy in sends:
        copy.wait_send()
    lax.fori_loop(1, image_count, finish, 0)


def reduce_kernel(image_axes, image_src, text_src, image_out, text_out, image_send, image_recv, text_send, text_recv,
                  inbox, outbox):
    image_count, image_me = group_size(image_axes), linear_index(image_axes)
    count, me, right, left = ring_peers()
    half = count // 2
    greet_all(image_axes, pltpu.get_barrier_semaphore(), image_count, image_me, right, left)
    finish = image_direct(image_axes, True, image_src, image_out, image_send, image_recv, image_count, image_me)
    sends = [remote(text_src.at[(me + half) % count], inbox.at[0], text_send.at[0], text_recv.at[0], right),
             remote(text_src.at[(me + half + 1) % count], inbox.at[half], text_send.at[half], text_recv.at[half], left)]
    for copy in sends:
        copy.start()
    for step in range(1, half):
        chains = ((step, (me + half - step) % count, right), (half + step, (me + half + 1 + step) % count, left))
        for slot, target, device in chains:
            if slot >= count - 1:
                continue
            remote(inbox.at[slot - 1], inbox.at[slot - 1], text_send.at[slot], text_recv.at[slot - 1], device).wait_recv()
            outbox[slot] = inbox[slot - 1] + text_src[target]
            copy = remote(outbox.at[slot], inbox.at[slot], text_send.at[slot], text_recv.at[slot], device)
            copy.start()
            sends.append(copy)
    last_right, last_left = half - 1, count - 2
    for slot in (last_right, last_left):
        remote(inbox.at[slot], inbox.at[slot], text_send.at[0], text_recv.at[slot], right).wait_recv()
    text_out[...] = text_src[me] + inbox[last_right] + inbox[last_left]
    for copy in sends:
        copy.wait_send()
    lax.fori_loop(1, image_count, finish, 0)


def exchange(image_src, text_src, scatter, tag):
    image_count, text_count = group_size(CHIP_AXES), group_size(TEXT_AXES)
    image_shape = image_src.shape if scatter else (image_count,) + image_src.shape
    text_shape = text_src.shape[1:] if scatter else (text_count,) + text_src.shape
    block = text_src.shape[1:] if scatter else text_src.shape
    vmem = pl.BlockSpec(memory_space=pltpu.VMEM)
    scratch = [
        pltpu.SemaphoreType.DMA((image_count,)),
        pltpu.SemaphoreType.DMA((image_count,)),
        pltpu.SemaphoreType.DMA((text_count,)),
        pltpu.SemaphoreType.DMA((text_count,)),
    ]
    if scatter:
        scratch += [pltpu.VMEM((text_count,) + block, text_src.dtype)] * 2
    return pl.pallas_call(
        functools.partial(reduce_kernel if scatter else gather_kernel, CHIP_AXES),
        out_shape=(jax.ShapeDtypeStruct(image_shape, image_src.dtype), jax.ShapeDtypeStruct(text_shape, text_src.dtype)),
        in_specs=[vmem, vmem],
        out_specs=(vmem, vmem),
        scratch_shapes=scratch,
        compiler_params=pltpu.CompilerParams(collective_id=tag, has_side_effects=True),
    )(image_src, text_src)


def pair_kernel(plan, *refs):
    count_groups = len(plan)
    srcs, outs = refs[:count_groups], refs[count_groups:2 * count_groups]
    sems = refs[2 * count_groups:]
    groups = [
        (axes, scatter, srcs[g], outs[g], sems[2 * g], sems[2 * g + 1]) for g, (axes, scatter) in enumerate(plan)
    ]
    barrier = pltpu.get_barrier_semaphore()
    peers = 0
    for axes, scatter, src, out, send, recv in groups:
        count, me = group_size(axes), linear_index(axes)
        peers += count - 1

        def greet(step, carry, axes=axes, count=count, me=me):
            pl.semaphore_signal(barrier, 1, device_id=member(axes, (me + step) % count), device_id_type=MESH_IDS)
            return carry

        lax.fori_loop(1, count, greet, 0)
    pl.semaphore_wait(barrier, peers)

    for axes, scatter, src, out, send, recv in groups:
        count, me = group_size(axes), linear_index(axes)

        def start(step, carry, axes=axes, scatter=scatter, count=count, me=me, src=src, out=out, send=send, recv=recv):
            peer = (me + step) % count
            pltpu.make_async_remote_copy(
                src.at[peer] if scatter else src, out.at[me], send.at[peer], recv.at[me],
                device_id=member(axes, peer), device_id_type=MESH_IDS,
            ).start()
            return carry

        lax.fori_loop(1, count, start, 0)

    for axes, scatter, src, out, send, recv in groups:
        count, me = group_size(axes), linear_index(axes)
        out[me] = src[me] if scatter else src[...]

    for axes, scatter, src, out, send, recv in groups:
        count, me = group_size(axes), linear_index(axes)

        def finish(step, carry, axes=axes, scatter=scatter, count=count, me=me, src=src, out=out, send=send, recv=recv):
            peer = (me + step) % count
            copy = pltpu.make_async_remote_copy(
                src.at[peer] if scatter else src, out.at[peer], send.at[peer], recv.at[peer],
                device_id=member(axes, peer), device_id_type=MESH_IDS,
            )
            copy.wait_send()
            copy.wait_recv()
            return carry

        lax.fori_loop(1, count, finish, 0)


def pair_exchange(routes, tag):
    plan = tuple((axes, scatter) for axes, src, scatter in routes)
    srcs = [src for axes, src, scatter in routes]
    shapes = [
        jax.ShapeDtypeStruct(src.shape if scatter else (group_size(axes),) + src.shape, src.dtype)
        for axes, src, scatter in routes
    ]
    sems = []
    for axes, src, scatter in routes:
        sems += [pltpu.SemaphoreType.DMA((group_size(axes),))] * 2
    vmem = pl.BlockSpec(memory_space=pltpu.VMEM)
    return pl.pallas_call(
        functools.partial(pair_kernel, plan),
        out_shape=tuple(shapes),
        in_specs=[vmem] * len(routes),
        out_specs=tuple([vmem] * len(routes)),
        scratch_shapes=sems,
        compiler_params=pltpu.CompilerParams(collective_id=tag, has_side_effects=True),
    )(*srcs)


def local(images, texts, scale, shift):
    rows, width = images.shape
    image_unit, image_norm = unit_rows(images)
    text_unit, text_norm = unit_rows(texts)
    image_emb = image_unit.astype(jnp.bfloat16)
    text_emb = text_unit.astype(jnp.bfloat16)
    chips = group_size(CHIP_AXES)
    cores = group_size(CORE_AXES)
    image_count = chips * cores
    text_count = group_size(TEXT_AXES)
    total = image_count * text_count * rows
    same_core, seen = exchange(image_emb, text_emb, False, 0)
    (gathered,) = pair_exchange([(CORE_AXES, same_core, False)], 1)
    gathered = gathered.reshape(image_count * rows, width)
    seen = seen.reshape(text_count * rows, width)
    image_ids = jnp.arange(image_count * rows, dtype=jnp.int32)[:, None]
    text_ids = jnp.arange(text_count * rows, dtype=jnp.int32)[None, :]
    mine_i = linear_index(CORE_AXES + CHIP_AXES)
    mine_t = linear_index(TEXT_AXES)
    label = (
        (image_ids // rows == mine_i) & (text_ids // rows == mine_t) & (image_ids % rows == text_ids % rows)
    ).astype(jnp.float32)
    logit = (
        scale
        * lax.dot_general(gathered, seen, (((1,), (1,)), ((), ())), preferred_element_type=jnp.float32)
        + shift
    )
    loss = jnp.sum(jax.nn.softplus(logit * (1.0 - 2.0 * label)), 1, keepdims=True) / total
    coef = ((jax.nn.sigmoid(logit) - label) * scale).astype(jnp.bfloat16)
    image_part = jnp.dot(coef, seen, preferred_element_type=jnp.float32)
    text_part = lax.dot_general(coef, gathered, (((0,), (0,)), ((), ())), preferred_element_type=jnp.float32)
    image_part = jnp.concatenate([image_part, jnp.broadcast_to(loss, (image_count * rows, LOSS_LANES))], 1)
    (halves,) = pair_exchange([(CORE_AXES, image_part.reshape(cores, chips, rows, width + LOSS_LANES), True)], 2)
    chip_sum = jnp.sum(halves, 0)
    image_in, text_in = exchange(chip_sum, text_part.reshape(text_count, rows, width), True, 3)
    image_in = jnp.sum(image_in, 0)
    text_sum = text_in
    image_grad = back_rows(image_in[:, :width], image_unit, image_norm)
    text_grad = back_rows(text_sum, text_unit, text_norm)
    return (image_in[:, width], image_grad, text_grad)


def solution(mesh):
    blk, grp = mesh.devices.shape
    fine = Mesh(mesh.devices.reshape(blk // 2, 2, grp // 16, 8, 2), ROWS_AXES)
    in_specs = (P(ROWS_AXES, None), P(ROWS_AXES, None), P(), P())
    out_specs = (P(ROWS_AXES), P(ROWS_AXES, None), P(ROWS_AXES, None))
    return jax.shard_map(local, mesh=fine, in_specs=in_specs, out_specs=out_specs, check_vma=False)
```

```python
import functools

import jax
import jax.numpy as jnp
from jax import lax
from jax.experimental import pallas as pl
from jax.experimental.pallas import tpu as pltpu
from jax.sharding import Mesh, PartitionSpec as P

ROWS_AXES = ("x", "zh", "y", "zl", "c")
CHIP_AXES = ("x", "y")
CORE_AXES = ("c",)
TEXT_AXES = ("zh", "zl")
MESH_IDS = pl.DeviceIdType.MESH
LOSS_LANES = 128


def unit_rows(values):
    floats = values.astype(jnp.float32)
    norms = jnp.sqrt(jnp.sum(floats * floats, 1, keepdims=True) + 1e-06)
    return (floats / norms, norms)


def back_rows(grads, units, norms):
    return (grads - units * jnp.sum(units * grads, 1, keepdims=True)) / norms


def linear_index(axes):
    index = 0
    for name in axes:
        index = index * lax.axis_size(name) + lax.axis_index(name)
    return index


def group_size(axes):
    size = 1
    for name in axes:
        size *= lax.axis_size(name)
    return size


def member(axes, k):
    coords = {}
    for name in reversed(axes):
        size = lax.axis_size(name)
        coords[name] = k % size
        k = k // size
    return tuple(coords[name] if name in coords else lax.axis_index(name) for name in ROWS_AXES)


def ring_peers():
    count, me = group_size(TEXT_AXES), linear_index(TEXT_AXES)
    return count, me, member(TEXT_AXES, (me + 1) % count), member(TEXT_AXES, (me + count - 1) % count)


def remote(src, dst, send, recv, device):
    return pltpu.make_async_remote_copy(src, dst, send, recv, device_id=device, device_id_type=MESH_IDS)


def greet_all(image_axes, barrier, image_count, image_me, right, left):
    def greet(step, carry):
        pl.semaphore_signal(barrier, 1, device_id=member(image_axes, (image_me + step) % image_count),
                            device_id_type=MESH_IDS)
        return carry

    lax.fori_loop(1, image_count, greet, 0)
    for device in (right, left):
        pl.semaphore_signal(barrier, 1, device_id=device, device_id_type=MESH_IDS)
    pl.semaphore_wait(barrier, image_count + 1)


def image_direct(image_axes, scatter, src, out, send, recv, count, me):
    def start(step, carry):
        peer = (me + step) % count
        remote(src.at[peer] if scatter else src, out.at[me], send.at[peer], recv.at[me],
               member(image_axes, peer)).start()
        return carry

    lax.fori_loop(1, count, start, 0)
    out[me] = src[me] if scatter else src[...]

    def finish(step, carry):
        peer = (me + step) % count
        copy = remote(src.at[peer] if scatter else src, out.at[peer], send.at[peer], recv.at[peer],
                      member(image_axes, peer))
        copy.wait_send()
        copy.wait_recv()
        return carry

    return finish


def gather_kernel(image_axes, image_src, text_src, image_out, text_out, image_send, image_recv, text_send, text_recv):
    image_count, image_me = group_size(image_axes), linear_index(image_axes)
    count, me, right, left = ring_peers()
    half = count // 2
    greet_all(image_axes, pltpu.get_barrier_semaphore(), image_count, image_me, right, left)
    finish = image_direct(image_axes, False, image_src, image_out, image_send, image_recv, image_count, image_me)
    sends = [remote(text_src, text_out.at[me], text_send.at[0], text_recv.at[me], right),
             remote(text_src, text_out.at[me], text_send.at[half], text_recv.at[me], left)]
    for copy in sends:
        copy.start()
    text_out[me] = text_src[...]
    for step in range(1, half):
        for origin, device, slot in (((me + count - step) % count, right, step), ((me + step) % count, left, half + step)):
            if slot >= count - 1:
                continue
            arrived = remote(text_out.at[origin], text_out.at[origin], text_send.at[slot], text_recv.at[origin], device)
            arrived.wait_recv()
            arrived.start()
            sends.append(arrived)
    for origin in ((me + count - half) % count, (me + half - 1) % count):
        remote(text_out.at[origin], text_out.at[origin], text_send.at[0], text_recv.at[origin], right).wait_recv()
    for copy in sends:
        copy.wait_send()
    lax.fori_loop(1, image_count, finish, 0)


def reduce_kernel(image_axes, image_src, text_src, image_out, text_out, image_send, image_recv, text_send, text_recv,
                  inbox, outbox):
    image_count, image_me = group_size(image_axes), linear_index(image_axes)
    count, me, right, left = ring_peers()
    half = count // 2
    greet_all(image_axes, pltpu.get_barrier_semaphore(), image_count, image_me, right, left)
    finish = image_direct(image_axes, True, image_src, image_out, image_send, image_recv, image_count, image_me)
    sends = [remote(text_src.at[(me + half) % count], inbox.at[0], text_send.at[0], text_recv.at[0], right),
             remote(text_src.at[(me + half + 1) % count], inbox.at[half], text_send.at[half], text_recv.at[half], left)]
    for copy in sends:
        copy.start()
    for step in range(1, half):
        chains = ((step, (me + half - step) % count, right), (half + step, (me + half + 1 + step) % count, left))
        for slot, target, device in chains:
            if slot >= count - 1:
                continue
            remote(inbox.at[slot - 1], inbox.at[slot - 1], text_send.at[slot], text_recv.at[slot - 1], device).wait_recv()
            outbox[slot] = inbox[slot - 1] + text_src[target]
            copy = remote(outbox.at[slot], inbox.at[slot], text_send.at[slot], text_recv.at[slot], device)
            copy.start()
            sends.append(copy)
    last_right, last_left = half - 1, count - 2
    for slot in (last_right, last_left):
        remote(inbox.at[slot], inbox.at[slot], text_send.at[0], text_recv.at[slot], right).wait_recv()
    text_out[...] = text_src[me] + inbox[last_right] + inbox[last_left]
    for copy in sends:
        copy.wait_send()
    lax.fori_loop(1, image_count, finish, 0)


def exchange(image_axes, image_src, text_src, scatter, tag):
    image_count, text_count = group_size(image_axes), group_size(TEXT_AXES)
    image_shape = image_src.shape if scatter else (image_count,) + image_src.shape
    text_shape = text_src.shape[1:] if scatter else (text_count,) + text_src.shape
    block = text_src.shape[1:] if scatter else text_src.shape
    vmem = pl.BlockSpec(memory_space=pltpu.VMEM)
    scratch = [
        pltpu.SemaphoreType.DMA((image_count,)),
        pltpu.SemaphoreType.DMA((image_count,)),
        pltpu.SemaphoreType.DMA((text_count,)),
        pltpu.SemaphoreType.DMA((text_count,)),
    ]
    if scatter:
        scratch += [pltpu.VMEM((text_count,) + block, text_src.dtype)] * 2
    return pl.pallas_call(
        functools.partial(reduce_kernel if scatter else gather_kernel, image_axes),
        out_shape=(jax.ShapeDtypeStruct(image_shape, image_src.dtype), jax.ShapeDtypeStruct(text_shape, text_src.dtype)),
        in_specs=[vmem, vmem],
        out_specs=(vmem, vmem),
        scratch_shapes=scratch,
        compiler_params=pltpu.CompilerParams(collective_id=tag, has_side_effects=True),
    )(image_src, text_src)


def pair_kernel(plan, *refs):
    count_groups = len(plan)
    srcs, outs = refs[:count_groups], refs[count_groups:2 * count_groups]
    sems = refs[2 * count_groups:]
    groups = [
        (axes, scatter, srcs[g], outs[g], sems[2 * g], sems[2 * g + 1]) for g, (axes, scatter) in enumerate(plan)
    ]
    barrier = pltpu.get_barrier_semaphore()
    peers = 0
    for axes, scatter, src, out, send, recv in groups:
        count, me = group_size(axes), linear_index(axes)
        peers += count - 1

        def greet(step, carry, axes=axes, count=count, me=me):
            pl.semaphore_signal(barrier, 1, device_id=member(axes, (me + step) % count), device_id_type=MESH_IDS)
            return carry

        lax.fori_loop(1, count, greet, 0)
    pl.semaphore_wait(barrier, peers)

    for axes, scatter, src, out, send, recv in groups:
        count, me = group_size(axes), linear_index(axes)

        def start(step, carry, axes=axes, scatter=scatter, count=count, me=me, src=src, out=out, send=send, recv=recv):
            peer = (me + step) % count
            pltpu.make_async_remote_copy(
                src.at[peer] if scatter else src, out.at[me], send.at[peer], recv.at[me],
                device_id=member(axes, peer), device_id_type=MESH_IDS,
            ).start()
            return carry

        lax.fori_loop(1, count, start, 0)

    for axes, scatter, src, out, send, recv in groups:
        count, me = group_size(axes), linear_index(axes)
        out[me] = src[me] if scatter else src[...]

    for axes, scatter, src, out, send, recv in groups:
        count, me = group_size(axes), linear_index(axes)

        def finish(step, carry, axes=axes, scatter=scatter, count=count, me=me, src=src, out=out, send=send, recv=recv):
            peer = (me + step) % count
            copy = pltpu.make_async_remote_copy(
                src.at[peer] if scatter else src, out.at[peer], send.at[peer], recv.at[peer],
                device_id=member(axes, peer), device_id_type=MESH_IDS,
            )
            copy.wait_send()
            copy.wait_recv()
            return carry

        lax.fori_loop(1, count, finish, 0)


def pair_exchange(routes, tag):
    plan = tuple((axes, scatter) for axes, src, scatter in routes)
    srcs = [src for axes, src, scatter in routes]
    shapes = [
        jax.ShapeDtypeStruct(src.shape if scatter else (group_size(axes),) + src.shape, src.dtype)
        for axes, src, scatter in routes
    ]
    sems = []
    for axes, src, scatter in routes:
        sems += [pltpu.SemaphoreType.DMA((group_size(axes),))] * 2
    vmem = pl.BlockSpec(memory_space=pltpu.VMEM)
    return pl.pallas_call(
        functools.partial(pair_kernel, plan),
        out_shape=tuple(shapes),
        in_specs=[vmem] * len(routes),
        out_specs=tuple([vmem] * len(routes)),
        scratch_shapes=sems,
        compiler_params=pltpu.CompilerParams(collective_id=tag, has_side_effects=True),
    )(*srcs)


def local(images, texts, scale, shift):
    rows, width = images.shape
    image_unit, image_norm = unit_rows(images)
    text_unit, text_norm = unit_rows(texts)
    image_emb = image_unit.astype(jnp.bfloat16)
    text_emb = text_unit.astype(jnp.bfloat16)
    chips = group_size(CHIP_AXES)
    cores = group_size(CORE_AXES)
    image_count = chips * cores
    text_count = group_size(TEXT_AXES)
    total = image_count * text_count * rows
    gathered, seen = exchange(CORE_AXES + CHIP_AXES, image_emb, text_emb, False, 0)
    gathered = gathered.reshape(image_count * rows, width)
    seen = seen.reshape(text_count * rows, width)
    image_ids = jnp.arange(image_count * rows, dtype=jnp.int32)[:, None]
    text_ids = jnp.arange(text_count * rows, dtype=jnp.int32)[None, :]
    mine_i = linear_index(CORE_AXES + CHIP_AXES)
    mine_t = linear_index(TEXT_AXES)
    label = (
        (image_ids // rows == mine_i) & (text_ids // rows == mine_t) & (image_ids % rows == text_ids % rows)
    ).astype(jnp.float32)
    logit = (
        scale
        * lax.dot_general(gathered, seen, (((1,), (1,)), ((), ())), preferred_element_type=jnp.float32)
        + shift
    )
    loss = jnp.sum(jax.nn.softplus(logit * (1.0 - 2.0 * label)), 1, keepdims=True) / total
    coef = ((jax.nn.sigmoid(logit) - label) * scale).astype(jnp.bfloat16)
    image_part = jnp.dot(coef, seen, preferred_element_type=jnp.float32)
    text_part = lax.dot_general(coef, gathered, (((0,), (0,)), ((), ())), preferred_element_type=jnp.float32)
    image_part = jnp.concatenate([image_part, jnp.broadcast_to(loss, (image_count * rows, LOSS_LANES))], 1)
    (halves,) = pair_exchange([(CORE_AXES, image_part.reshape(cores, chips, rows, width + LOSS_LANES), True)], 2)
    chip_sum = jnp.sum(halves, 0)
    image_in, text_in = exchange(CHIP_AXES, chip_sum, text_part.reshape(text_count, rows, width), True, 3)
    image_in = jnp.sum(image_in, 0)
    text_sum = text_in
    image_grad = back_rows(image_in[:, :width], image_unit, image_norm)
    text_grad = back_rows(text_sum, text_unit, text_norm)
    return (image_in[:, width], image_grad, text_grad)


def solution(mesh):
    blk, grp = mesh.devices.shape
    fine = Mesh(mesh.devices.reshape(blk // 2, 2, grp // 16, 8, 2), ROWS_AXES)
    in_specs = (P(ROWS_AXES, None), P(ROWS_AXES, None), P(), P())
    out_specs = (P(ROWS_AXES), P(ROWS_AXES, None), P(ROWS_AXES, None))
    return jax.shard_map(local, mesh=fine, in_specs=in_specs, out_specs=out_specs, check_vma=False)
```

```python
import functools

import jax
import jax.numpy as jnp
from jax import lax
from jax.experimental import pallas as pl
from jax.experimental.pallas import tpu as pltpu
from jax.sharding import Mesh, PartitionSpec as P

ROWS_AXES = ("x", "zh", "y", "zl", "c")
CHIP_AXES = ("x", "y")
CORE_AXES = ("c",)
TEXT_AXES = ("zh", "zl")
MESH_IDS = pl.DeviceIdType.MESH
LOSS_LANES = 128


def unit_rows(values):
    floats = values.astype(jnp.float32)
    norms = jnp.sqrt(jnp.sum(floats * floats, 1, keepdims=True) + 1e-06)
    return (floats / norms, norms)


def back_rows(grads, units, norms):
    return (grads - units * jnp.sum(units * grads, 1, keepdims=True)) / norms


def linear_index(axes):
    index = 0
    for name in axes:
        index = index * lax.axis_size(name) + lax.axis_index(name)
    return index


def group_size(axes):
    size = 1
    for name in axes:
        size *= lax.axis_size(name)
    return size


def member(axes, k):
    coords = {}
    for name in reversed(axes):
        size = lax.axis_size(name)
        coords[name] = k % size
        k = k // size
    return tuple(coords[name] if name in coords else lax.axis_index(name) for name in ROWS_AXES)


def ring_peers():
    count, me = group_size(TEXT_AXES), linear_index(TEXT_AXES)
    return count, me, member(TEXT_AXES, (me + 1) % count), member(TEXT_AXES, (me + count - 1) % count)


def remote(src, dst, send, recv, device):
    return pltpu.make_async_remote_copy(src, dst, send, recv, device_id=device, device_id_type=MESH_IDS)


def greet_all(image_axes, barrier, image_count, image_me, right, left, extra=()):
    def greet(step, carry):
        pl.semaphore_signal(barrier, 1, device_id=member(image_axes, (image_me + step) % image_count),
                            device_id_type=MESH_IDS)
        return carry

    lax.fori_loop(1, image_count, greet, 0)
    for device in (right, left) + tuple(extra):
        pl.semaphore_signal(barrier, 1, device_id=device, device_id_type=MESH_IDS)
    pl.semaphore_wait(barrier, image_count + 1 + len(extra))


def image_direct(image_axes, scatter, src, out, send, recv, count, me):
    def start(step, carry):
        peer = (me + step) % count
        remote(src.at[peer] if scatter else src, out.at[me], send.at[peer], recv.at[me],
               member(image_axes, peer)).start()
        return carry

    lax.fori_loop(1, count, start, 0)
    out[me] = src[me] if scatter else src[...]

    def finish(step, carry):
        peer = (me + step) % count
        copy = remote(src.at[peer] if scatter else src, out.at[peer], send.at[peer], recv.at[peer],
                      member(image_axes, peer))
        copy.wait_send()
        copy.wait_recv()
        return carry

    return finish


def gather_kernel(image_axes, image_src, text_src, image_out, text_out, image_send, image_recv, text_send, text_recv):
    image_count, image_me = group_size(image_axes), linear_index(image_axes)
    count, me, right, left = ring_peers()
    half = count // 2
    greet_all(image_axes, pltpu.get_barrier_semaphore(), image_count, image_me, right, left)
    finish = image_direct(image_axes, False, image_src, image_out, image_send, image_recv, image_count, image_me)
    sends = [remote(text_src, text_out.at[me], text_send.at[0], text_recv.at[me], right),
             remote(text_src, text_out.at[me], text_send.at[half], text_recv.at[me], left)]
    for copy in sends:
        copy.start()
    text_out[me] = text_src[...]
    for step in range(1, half):
        for origin, device, slot in (((me + count - step) % count, right, step), ((me + step) % count, left, half + step)):
            if slot >= count - 1:
                continue
            arrived = remote(text_out.at[origin], text_out.at[origin], text_send.at[slot], text_recv.at[origin], device)
            arrived.wait_recv()
            arrived.start()
            sends.append(arrived)
    for origin in ((me + count - half) % count, (me + half - 1) % count):
        remote(text_out.at[origin], text_out.at[origin], text_send.at[0], text_recv.at[origin], right).wait_recv()
    for copy in sends:
        copy.wait_send()
    lax.fori_loop(1, image_count, finish, 0)


def reduce_kernel(image_axes, image_src, text_src, image_out, text_out, image_send, image_recv, text_send, text_recv,
                  inbox, outbox):
    image_count, image_me = group_size(image_axes), linear_index(image_axes)
    count, me, right, left = ring_peers()
    half = count // 2
    greet_all(image_axes, pltpu.get_barrier_semaphore(), image_count, image_me, right, left)
    finish = image_direct(image_axes, True, image_src, image_out, image_send, image_recv, image_count, image_me)
    sends = [remote(text_src.at[(me + half) % count], inbox.at[0], text_send.at[0], text_recv.at[0], right),
             remote(text_src.at[(me + half + 1) % count], inbox.at[half], text_send.at[half], text_recv.at[half], left)]
    for copy in sends:
        copy.start()
    for step in range(1, half):
        chains = ((step, (me + half - step) % count, right), (half + step, (me + half + 1 + step) % count, left))
        for slot, target, device in chains:
            if slot >= count - 1:
                continue
            remote(inbox.at[slot - 1], inbox.at[slot - 1], text_send.at[slot], text_recv.at[slot - 1], device).wait_recv()
            outbox[slot] = inbox[slot - 1] + text_src[target]
            copy = remote(outbox.at[slot], inbox.at[slot], text_send.at[slot], text_recv.at[slot], device)
            copy.start()
            sends.append(copy)
    last_right, last_left = half - 1, count - 2
    for slot in (last_right, last_left):
        remote(inbox.at[slot], inbox.at[slot], text_send.at[0], text_recv.at[slot], right).wait_recv()
    text_out[...] = text_src[me] + inbox[last_right] + inbox[last_left]
    for copy in sends:
        copy.wait_send()
    lax.fori_loop(1, image_count, finish, 0)


def merged_reduce_kernel(image_axes, image_src, text_src, image_out, text_out, image_send, image_recv, text_send,
                         text_recv, inbox, outbox, halfbox, summed, half_sems):
    image_count, image_me = group_size(image_axes), linear_index(image_axes)
    count, me, right, left = ring_peers()
    half = count // 2
    core = linear_index(CORE_AXES)
    partner = member(CORE_AXES, 1 - core)
    greet_all(image_axes, pltpu.get_barrier_semaphore(), image_count, image_me, right, left, (partner,))
    sends = [remote(text_src.at[(me + half) % count], inbox.at[0], text_send.at[0], text_recv.at[0], right),
             remote(text_src.at[(me + half + 1) % count], inbox.at[half], text_send.at[half], text_recv.at[half], left)]
    for copy in sends:
        copy.start()
    swap = remote(image_src.at[1 - core], halfbox, half_sems.at[0], half_sems.at[1], partner)
    swap.start()
    swap.wait_recv()
    summed[...] = image_src[core] + halfbox[...]
    finish = image_direct(image_axes, True, summed, image_out, image_send, image_recv, image_count, image_me)
    for step in range(1, half):
        chains = ((step, (me + half - step) % count, right), (half + step, (me + half + 1 + step) % count, left))
        for slot, target, device in chains:
            if slot >= count - 1:
                continue
            remote(inbox.at[slot - 1], inbox.at[slot - 1], text_send.at[slot], text_recv.at[slot - 1], device).wait_recv()
            outbox[slot] = inbox[slot - 1] + text_src[target]
            copy = remote(outbox.at[slot], inbox.at[slot], text_send.at[slot], text_recv.at[slot], device)
            copy.start()
            sends.append(copy)
    last_right, last_left = half - 1, count - 2
    for slot in (last_right, last_left):
        remote(inbox.at[slot], inbox.at[slot], text_send.at[0], text_recv.at[slot], right).wait_recv()
    text_out[...] = text_src[me] + inbox[last_right] + inbox[last_left]
    for copy in sends:
        copy.wait_send()
    swap.wait_send()
    lax.fori_loop(1, image_count, finish, 0)


def merged_reduce(image_axes, image_src, text_src, tag):
    image_count, text_count = group_size(image_axes), group_size(TEXT_AXES)
    image_shape = image_src.shape[1:]
    block = text_src.shape[1:]
    vmem = pl.BlockSpec(memory_space=pltpu.VMEM)
    scratch = [
        pltpu.SemaphoreType.DMA((image_count,)),
        pltpu.SemaphoreType.DMA((image_count,)),
        pltpu.SemaphoreType.DMA((text_count,)),
        pltpu.SemaphoreType.DMA((text_count,)),
        pltpu.VMEM((text_count,) + block, text_src.dtype),
        pltpu.VMEM((text_count,) + block, text_src.dtype),
        pltpu.VMEM(image_shape, image_src.dtype),
        pltpu.VMEM(image_shape, image_src.dtype),
        pltpu.SemaphoreType.DMA((2,)),
    ]
    return pl.pallas_call(
        functools.partial(merged_reduce_kernel, image_axes),
        out_shape=(jax.ShapeDtypeStruct(image_shape, image_src.dtype), jax.ShapeDtypeStruct(block, text_src.dtype)),
        in_specs=[vmem, vmem],
        out_specs=(vmem, vmem),
        scratch_shapes=scratch,
        compiler_params=pltpu.CompilerParams(collective_id=tag, has_side_effects=True),
    )(image_src, text_src)


def exchange(image_axes, image_src, text_src, scatter, tag):
    image_count, text_count = group_size(image_axes), group_size(TEXT_AXES)
    image_shape = image_src.shape if scatter else (image_count,) + image_src.shape
    text_shape = text_src.shape[1:] if scatter else (text_count,) + text_src.shape
    block = text_src.shape[1:] if scatter else text_src.shape
    vmem = pl.BlockSpec(memory_space=pltpu.VMEM)
    scratch = [
        pltpu.SemaphoreType.DMA((image_count,)),
        pltpu.SemaphoreType.DMA((image_count,)),
        pltpu.SemaphoreType.DMA((text_count,)),
        pltpu.SemaphoreType.DMA((text_count,)),
    ]
    if scatter:
        scratch += [pltpu.VMEM((text_count,) + block, text_src.dtype)] * 2
    return pl.pallas_call(
        functools.partial(reduce_kernel if scatter else gather_kernel, image_axes),
        out_shape=(jax.ShapeDtypeStruct(image_shape, image_src.dtype), jax.ShapeDtypeStruct(text_shape, text_src.dtype)),
        in_specs=[vmem, vmem],
        out_specs=(vmem, vmem),
        scratch_shapes=scratch,
        compiler_params=pltpu.CompilerParams(collective_id=tag, has_side_effects=True),
    )(image_src, text_src)


def pair_kernel(plan, *refs):
    count_groups = len(plan)
    srcs, outs = refs[:count_groups], refs[count_groups:2 * count_groups]
    sems = refs[2 * count_groups:]
    groups = [
        (axes, scatter, srcs[g], outs[g], sems[2 * g], sems[2 * g + 1]) for g, (axes, scatter) in enumerate(plan)
    ]
    barrier = pltpu.get_barrier_semaphore()
    peers = 0
    for axes, scatter, src, out, send, recv in groups:
        count, me = group_size(axes), linear_index(axes)
        peers += count - 1

        def greet(step, carry, axes=axes, count=count, me=me):
            pl.semaphore_signal(barrier, 1, device_id=member(axes, (me + step) % count), device_id_type=MESH_IDS)
            return carry

        lax.fori_loop(1, count, greet, 0)
    pl.semaphore_wait(barrier, peers)

    for axes, scatter, src, out, send, recv in groups:
        count, me = group_size(axes), linear_index(axes)

        def start(step, carry, axes=axes, scatter=scatter, count=count, me=me, src=src, out=out, send=send, recv=recv):
            peer = (me + step) % count
            pltpu.make_async_remote_copy(
                src.at[peer] if scatter else src, out.at[me], send.at[peer], recv.at[me],
                device_id=member(axes, peer), device_id_type=MESH_IDS,
            ).start()
            return carry

        lax.fori_loop(1, count, start, 0)

    for axes, scatter, src, out, send, recv in groups:
        count, me = group_size(axes), linear_index(axes)
        out[me] = src[me] if scatter else src[...]

    for axes, scatter, src, out, send, recv in groups:
        count, me = group_size(axes), linear_index(axes)

        def finish(step, carry, axes=axes, scatter=scatter, count=count, me=me, src=src, out=out, send=send, recv=recv):
            peer = (me + step) % count
            copy = pltpu.make_async_remote_copy(
                src.at[peer] if scatter else src, out.at[peer], send.at[peer], recv.at[peer],
                device_id=member(axes, peer), device_id_type=MESH_IDS,
            )
            copy.wait_send()
            copy.wait_recv()
            return carry

        lax.fori_loop(1, count, finish, 0)


def pair_exchange(routes, tag):
    plan = tuple((axes, scatter) for axes, src, scatter in routes)
    srcs = [src for axes, src, scatter in routes]
    shapes = [
        jax.ShapeDtypeStruct(src.shape if scatter else (group_size(axes),) + src.shape, src.dtype)
        for axes, src, scatter in routes
    ]
    sems = []
    for axes, src, scatter in routes:
        sems += [pltpu.SemaphoreType.DMA((group_size(axes),))] * 2
    vmem = pl.BlockSpec(memory_space=pltpu.VMEM)
    return pl.pallas_call(
        functools.partial(pair_kernel, plan),
        out_shape=tuple(shapes),
        in_specs=[vmem] * len(routes),
        out_specs=tuple([vmem] * len(routes)),
        scratch_shapes=sems,
        compiler_params=pltpu.CompilerParams(collective_id=tag, has_side_effects=True),
    )(*srcs)


def local(images, texts, scale, shift):
    rows, width = images.shape
    image_unit, image_norm = unit_rows(images)
    text_unit, text_norm = unit_rows(texts)
    image_emb = image_unit.astype(jnp.bfloat16)
    text_emb = text_unit.astype(jnp.bfloat16)
    chips = group_size(CHIP_AXES)
    cores = group_size(CORE_AXES)
    image_count = chips * cores
    text_count = group_size(TEXT_AXES)
    total = image_count * text_count * rows
    gathered, seen = exchange(CORE_AXES + CHIP_AXES, image_emb, text_emb, False, 0)
    gathered = gathered.reshape(image_count * rows, width)
    seen = seen.reshape(text_count * rows, width)
    image_ids = jnp.arange(image_count * rows, dtype=jnp.int32)[:, None]
    text_ids = jnp.arange(text_count * rows, dtype=jnp.int32)[None, :]
    mine_i = linear_index(CORE_AXES + CHIP_AXES)
    mine_t = linear_index(TEXT_AXES)
    label = (
        (image_ids // rows == mine_i) & (text_ids // rows == mine_t) & (image_ids % rows == text_ids % rows)
    ).astype(jnp.float32)
    logit = (
        scale
        * lax.dot_general(gathered, seen, (((1,), (1,)), ((), ())), preferred_element_type=jnp.float32)
        + shift
    )
    loss = jnp.sum(jax.nn.softplus(logit * (1.0 - 2.0 * label)), 1, keepdims=True) / total
    coef = ((jax.nn.sigmoid(logit) - label) * scale).astype(jnp.bfloat16)
    image_part = jnp.dot(coef, seen, preferred_element_type=jnp.float32)
    text_part = lax.dot_general(coef, gathered, (((0,), (0,)), ((), ())), preferred_element_type=jnp.float32)
    image_part = jnp.concatenate([image_part, jnp.broadcast_to(loss, (image_count * rows, LOSS_LANES))], 1)
    image_in, text_in = merged_reduce(
        CHIP_AXES, image_part.reshape(cores, chips, rows, width + LOSS_LANES), text_part.reshape(text_count, rows, width), 3
    )
    image_in = jnp.sum(image_in, 0)
    text_sum = text_in
    image_grad = back_rows(image_in[:, :width], image_unit, image_norm)
    text_grad = back_rows(text_sum, text_unit, text_norm)
    return (image_in[:, width], image_grad, text_grad)


def solution(mesh):
    blk, grp = mesh.devices.shape
    fine = Mesh(mesh.devices.reshape(blk // 2, 2, grp // 16, 8, 2), ROWS_AXES)
    in_specs = (P(ROWS_AXES, None), P(ROWS_AXES, None), P(), P())
    out_specs = (P(ROWS_AXES), P(ROWS_AXES, None), P(ROWS_AXES, None))
    return jax.shard_map(local, mesh=fine, in_specs=in_specs, out_specs=out_specs, check_vma=False)
```

```python
import functools

import jax
import jax.numpy as jnp
from jax import lax
from jax.experimental import pallas as pl
from jax.experimental.pallas import tpu as pltpu
from jax.sharding import Mesh, PartitionSpec as P

ROWS_AXES = ("x", "zh", "y", "zl", "c")
CHIP_AXES = ("x", "y")
CORE_AXES = ("c",)
TEXT_AXES = ("zh", "zl")
MESH_IDS = pl.DeviceIdType.MESH
LOSS_LANES = 128


def unit_rows(values):
    floats = values.astype(jnp.float32)
    norms = jnp.sqrt(jnp.sum(floats * floats, 1, keepdims=True) + 1e-06)
    return (floats / norms, norms)


def back_rows(grads, units, norms):
    return (grads - units * jnp.sum(units * grads, 1, keepdims=True)) / norms


def linear_index(axes):
    index = 0
    for name in axes:
        index = index * lax.axis_size(name) + lax.axis_index(name)
    return index


def group_size(axes):
    size = 1
    for name in axes:
        size *= lax.axis_size(name)
    return size


def member(axes, k):
    coords = {}
    for name in reversed(axes):
        size = lax.axis_size(name)
        coords[name] = k % size
        k = k // size
    return tuple(coords[name] if name in coords else lax.axis_index(name) for name in ROWS_AXES)


def ring_peers():
    count, me = group_size(TEXT_AXES), linear_index(TEXT_AXES)
    return count, me, member(TEXT_AXES, (me + 1) % count), member(TEXT_AXES, (me + count - 1) % count)


def remote(src, dst, send, recv, device):
    return pltpu.make_async_remote_copy(src, dst, send, recv, device_id=device, device_id_type=MESH_IDS)


def greet_all(image_axes, barrier, image_count, image_me, right, left, extra=()):
    def greet(step, carry):
        pl.semaphore_signal(barrier, 1, device_id=member(image_axes, (image_me + step) % image_count),
                            device_id_type=MESH_IDS)
        return carry

    lax.fori_loop(1, image_count, greet, 0)
    for device in (right, left) + tuple(extra):
        pl.semaphore_signal(barrier, 1, device_id=device, device_id_type=MESH_IDS)
    pl.semaphore_wait(barrier, image_count + 1 + len(extra))


def image_direct(image_axes, scatter, src, out, send, recv, count, me):
    def start(lo, hi):
        def one(step, carry):
            peer = (me + step) % count
            remote(src.at[peer] if scatter else src, out.at[me], send.at[peer], recv.at[me],
                   member(image_axes, peer)).start()
            return carry

        if hi > lo:
            lax.fori_loop(lo, hi, one, 0)

    out[me] = src[me] if scatter else src[...]

    def finish(step, carry):
        peer = (me + step) % count
        copy = remote(src.at[peer] if scatter else src, out.at[peer], send.at[peer], recv.at[peer],
                      member(image_axes, peer))
        copy.wait_send()
        copy.wait_recv()
        return carry

    return start, finish


def share(count, steps, step):
    per = -(-(count - 1) // steps)
    return min(count, 1 + per * step), min(count, 1 + per * (step + 1))


def gather_kernel(image_axes, image_src, text_src, image_out, text_out, image_send, image_recv, text_send, text_recv):
    image_count, image_me = group_size(image_axes), linear_index(image_axes)
    count, me, right, left = ring_peers()
    half = count // 2
    greet_all(image_axes, pltpu.get_barrier_semaphore(), image_count, image_me, right, left)
    start, finish = image_direct(image_axes, False, image_src, image_out, image_send, image_recv, image_count, image_me)
    sends = [remote(text_src, text_out.at[me], text_send.at[0], text_recv.at[me], right),
             remote(text_src, text_out.at[me], text_send.at[half], text_recv.at[me], left)]
    for copy in sends:
        copy.start()
    text_out[me] = text_src[...]
    start(*share(image_count, half, 0))
    for step in range(1, half):
        start(*share(image_count, half, step))
        for origin, device, slot in (((me + count - step) % count, right, step), ((me + step) % count, left, half + step)):
            if slot >= count - 1:
                continue
            arrived = remote(text_out.at[origin], text_out.at[origin], text_send.at[slot], text_recv.at[origin], device)
            arrived.wait_recv()
            arrived.start()
            sends.append(arrived)
    for origin in ((me + count - half) % count, (me + half - 1) % count):
        remote(text_out.at[origin], text_out.at[origin], text_send.at[0], text_recv.at[origin], right).wait_recv()
    for copy in sends:
        copy.wait_send()
    lax.fori_loop(1, image_count, finish, 0)


def reduce_kernel(image_axes, image_src, text_src, image_out, text_out, image_send, image_recv, text_send, text_recv,
                  inbox, outbox):
    image_count, image_me = group_size(image_axes), linear_index(image_axes)
    count, me, right, left = ring_peers()
    half = count // 2
    greet_all(image_axes, pltpu.get_barrier_semaphore(), image_count, image_me, right, left)
    start, finish = image_direct(image_axes, True, image_src, image_out, image_send, image_recv, image_count, image_me)
    start(1, image_count)
    sends = [remote(text_src.at[(me + half) % count], inbox.at[0], text_send.at[0], text_recv.at[0], right),
             remote(text_src.at[(me + half + 1) % count], inbox.at[half], text_send.at[half], text_recv.at[half], left)]
    for copy in sends:
        copy.start()
    for step in range(1, half):
        chains = ((step, (me + half - step) % count, right), (half + step, (me + half + 1 + step) % count, left))
        for slot, target, device in chains:
            if slot >= count - 1:
                continue
            remote(inbox.at[slot - 1], inbox.at[slot - 1], text_send.at[slot], text_recv.at[slot - 1], device).wait_recv()
            outbox[slot] = inbox[slot - 1] + text_src[target]
            copy = remote(outbox.at[slot], inbox.at[slot], text_send.at[slot], text_recv.at[slot], device)
            copy.start()
            sends.append(copy)
    last_right, last_left = half - 1, count - 2
    for slot in (last_right, last_left):
        remote(inbox.at[slot], inbox.at[slot], text_send.at[0], text_recv.at[slot], right).wait_recv()
    text_out[...] = text_src[me] + inbox[last_right] + inbox[last_left]
    for copy in sends:
        copy.wait_send()
    lax.fori_loop(1, image_count, finish, 0)


def merged_reduce_kernel(image_axes, image_src, text_src, image_out, text_out, image_send, image_recv, text_send,
                         text_recv, inbox, outbox, halfbox, summed, half_sems):
    image_count, image_me = group_size(image_axes), linear_index(image_axes)
    count, me, right, left = ring_peers()
    half = count // 2
    core = linear_index(CORE_AXES)
    partner = member(CORE_AXES, 1 - core)
    greet_all(image_axes, pltpu.get_barrier_semaphore(), image_count, image_me, right, left, (partner,))
    sends = [remote(text_src.at[(me + half) % count], inbox.at[0], text_send.at[0], text_recv.at[0], right),
             remote(text_src.at[(me + half + 1) % count], inbox.at[half], text_send.at[half], text_recv.at[half], left)]
    for copy in sends:
        copy.start()
    swap = remote(image_src.at[1 - core], halfbox, half_sems.at[0], half_sems.at[1], partner)
    swap.start()
    swap.wait_recv()
    summed[...] = image_src[core] + halfbox[...]
    start, finish = image_direct(image_axes, True, summed, image_out, image_send, image_recv, image_count, image_me)
    start(*share(image_count, half, 0))
    for step in range(1, half):
        start(*share(image_count, half, step))
        chains = ((step, (me + half - step) % count, right), (half + step, (me + half + 1 + step) % count, left))
        for slot, target, device in chains:
            if slot >= count - 1:
                continue
            remote(inbox.at[slot - 1], inbox.at[slot - 1], text_send.at[slot], text_recv.at[slot - 1], device).wait_recv()
            outbox[slot] = inbox[slot - 1] + text_src[target]
            copy = remote(outbox.at[slot], inbox.at[slot], text_send.at[slot], text_recv.at[slot], device)
            copy.start()
            sends.append(copy)
    last_right, last_left = half - 1, count - 2
    for slot in (last_right, last_left):
        remote(inbox.at[slot], inbox.at[slot], text_send.at[0], text_recv.at[slot], right).wait_recv()
    text_out[...] = text_src[me] + inbox[last_right] + inbox[last_left]
    for copy in sends:
        copy.wait_send()
    swap.wait_send()
    lax.fori_loop(1, image_count, finish, 0)


def merged_reduce(image_axes, image_src, text_src, tag):
    image_count, text_count = group_size(image_axes), group_size(TEXT_AXES)
    image_shape = image_src.shape[1:]
    block = text_src.shape[1:]
    vmem = pl.BlockSpec(memory_space=pltpu.VMEM)
    scratch = [
        pltpu.SemaphoreType.DMA((image_count,)),
        pltpu.SemaphoreType.DMA((image_count,)),
        pltpu.SemaphoreType.DMA((text_count,)),
        pltpu.SemaphoreType.DMA((text_count,)),
        pltpu.VMEM((text_count,) + block, text_src.dtype),
        pltpu.VMEM((text_count,) + block, text_src.dtype),
        pltpu.VMEM(image_shape, image_src.dtype),
        pltpu.VMEM(image_shape, image_src.dtype),
        pltpu.SemaphoreType.DMA((2,)),
    ]
    return pl.pallas_call(
        functools.partial(merged_reduce_kernel, image_axes),
        out_shape=(jax.ShapeDtypeStruct(image_shape, image_src.dtype), jax.ShapeDtypeStruct(block, text_src.dtype)),
        in_specs=[vmem, vmem],
        out_specs=(vmem, vmem),
        scratch_shapes=scratch,
        compiler_params=pltpu.CompilerParams(collective_id=tag, has_side_effects=True),
    )(image_src, text_src)


def exchange(image_axes, image_src, text_src, scatter, tag):
    image_count, text_count = group_size(image_axes), group_size(TEXT_AXES)
    image_shape = image_src.shape if scatter else (image_count,) + image_src.shape
    text_shape = text_src.shape[1:] if scatter else (text_count,) + text_src.shape
    block = text_src.shape[1:] if scatter else text_src.shape
    vmem = pl.BlockSpec(memory_space=pltpu.VMEM)
    scratch = [
        pltpu.SemaphoreType.DMA((image_count,)),
        pltpu.SemaphoreType.DMA((image_count,)),
        pltpu.SemaphoreType.DMA((text_count,)),
        pltpu.SemaphoreType.DMA((text_count,)),
    ]
    if scatter:
        scratch += [pltpu.VMEM((text_count,) + block, text_src.dtype)] * 2
    return pl.pallas_call(
        functools.partial(reduce_kernel if scatter else gather_kernel, image_axes),
        out_shape=(jax.ShapeDtypeStruct(image_shape, image_src.dtype), jax.ShapeDtypeStruct(text_shape, text_src.dtype)),
        in_specs=[vmem, vmem],
        out_specs=(vmem, vmem),
        scratch_shapes=scratch,
        compiler_params=pltpu.CompilerParams(collective_id=tag, has_side_effects=True),
    )(image_src, text_src)


def pair_kernel(plan, *refs):
    count_groups = len(plan)
    srcs, outs = refs[:count_groups], refs[count_groups:2 * count_groups]
    sems = refs[2 * count_groups:]
    groups = [
        (axes, scatter, srcs[g], outs[g], sems[2 * g], sems[2 * g + 1]) for g, (axes, scatter) in enumerate(plan)
    ]
    barrier = pltpu.get_barrier_semaphore()
    peers = 0
    for axes, scatter, src, out, send, recv in groups:
        count, me = group_size(axes), linear_index(axes)
        peers += count - 1

        def greet(step, carry, axes=axes, count=count, me=me):
            pl.semaphore_signal(barrier, 1, device_id=member(axes, (me + step) % count), device_id_type=MESH_IDS)
            return carry

        lax.fori_loop(1, count, greet, 0)
    pl.semaphore_wait(barrier, peers)

    for axes, scatter, src, out, send, recv in groups:
        count, me = group_size(axes), linear_index(axes)

        def start(step, carry, axes=axes, scatter=scatter, count=count, me=me, src=src, out=out, send=send, recv=recv):
            peer = (me + step) % count
            pltpu.make_async_remote_copy(
                src.at[peer] if scatter else src, out.at[me], send.at[peer], recv.at[me],
                device_id=member(axes, peer), device_id_type=MESH_IDS,
            ).start()
            return carry

        lax.fori_loop(1, count, start, 0)

    for axes, scatter, src, out, send, recv in groups:
        count, me = group_size(axes), linear_index(axes)
        out[me] = src[me] if scatter else src[...]

    for axes, scatter, src, out, send, recv in groups:
        count, me = group_size(axes), linear_index(axes)

        def finish(step, carry, axes=axes, scatter=scatter, count=count, me=me, src=src, out=out, send=send, recv=recv):
            peer = (me + step) % count
            copy = pltpu.make_async_remote_copy(
                src.at[peer] if scatter else src, out.at[peer], send.at[peer], recv.at[peer],
                device_id=member(axes, peer), device_id_type=MESH_IDS,
            )
            copy.wait_send()
            copy.wait_recv()
            return carry

        lax.fori_loop(1, count, finish, 0)


def pair_exchange(routes, tag):
    plan = tuple((axes, scatter) for axes, src, scatter in routes)
    srcs = [src for axes, src, scatter in routes]
    shapes = [
        jax.ShapeDtypeStruct(src.shape if scatter else (group_size(axes),) + src.shape, src.dtype)
        for axes, src, scatter in routes
    ]
    sems = []
    for axes, src, scatter in routes:
        sems += [pltpu.SemaphoreType.DMA((group_size(axes),))] * 2
    vmem = pl.BlockSpec(memory_space=pltpu.VMEM)
    return pl.pallas_call(
        functools.partial(pair_kernel, plan),
        out_shape=tuple(shapes),
        in_specs=[vmem] * len(routes),
        out_specs=tuple([vmem] * len(routes)),
        scratch_shapes=sems,
        compiler_params=pltpu.CompilerParams(collective_id=tag, has_side_effects=True),
    )(*srcs)


def local(images, texts, scale, shift):
    rows, width = images.shape
    image_unit, image_norm = unit_rows(images)
    text_unit, text_norm = unit_rows(texts)
    image_emb = image_unit.astype(jnp.bfloat16)
    text_emb = text_unit.astype(jnp.bfloat16)
    chips = group_size(CHIP_AXES)
    cores = group_size(CORE_AXES)
    image_count = chips * cores
    text_count = group_size(TEXT_AXES)
    total = image_count * text_count * rows
    gathered, seen = exchange(CORE_AXES + CHIP_AXES, image_emb, text_emb, False, 0)
    gathered = gathered.reshape(image_count * rows, width)
    seen = seen.reshape(text_count * rows, width)
    image_ids = jnp.arange(image_count * rows, dtype=jnp.int32)[:, None]
    text_ids = jnp.arange(text_count * rows, dtype=jnp.int32)[None, :]
    mine_i = linear_index(CORE_AXES + CHIP_AXES)
    mine_t = linear_index(TEXT_AXES)
    label = (
        (image_ids // rows == mine_i) & (text_ids // rows == mine_t) & (image_ids % rows == text_ids % rows)
    ).astype(jnp.float32)
    logit = (
        scale
        * lax.dot_general(gathered, seen, (((1,), (1,)), ((), ())), preferred_element_type=jnp.float32)
        + shift
    )
    loss = jnp.sum(jax.nn.softplus(logit * (1.0 - 2.0 * label)), 1, keepdims=True) / total
    coef = ((jax.nn.sigmoid(logit) - label) * scale).astype(jnp.bfloat16)
    image_part = jnp.dot(coef, seen, preferred_element_type=jnp.float32)
    text_part = lax.dot_general(coef, gathered, (((0,), (0,)), ((), ())), preferred_element_type=jnp.float32)
    image_part = jnp.concatenate([image_part, jnp.broadcast_to(loss, (image_count * rows, LOSS_LANES))], 1)
    image_in, text_in = merged_reduce(
        CHIP_AXES, image_part.reshape(cores, chips, rows, width + LOSS_LANES), text_part.reshape(text_count, rows, width), 3
    )
    image_in = jnp.sum(image_in, 0)
    text_sum = text_in
    image_grad = back_rows(image_in[:, :width], image_unit, image_norm)
    text_grad = back_rows(text_sum, text_unit, text_norm)
    return (image_in[:, width], image_grad, text_grad)


def solution(mesh):
    blk, grp = mesh.devices.shape
    fine = Mesh(mesh.devices.reshape(blk // 2, 2, grp // 16, 8, 2), ROWS_AXES)
    in_specs = (P(ROWS_AXES, None), P(ROWS_AXES, None), P(), P())
    out_specs = (P(ROWS_AXES), P(ROWS_AXES, None), P(ROWS_AXES, None))
    return jax.shard_map(local, mesh=fine, in_specs=in_specs, out_specs=out_specs, check_vma=False)
```

```python
import functools

import jax
import jax.numpy as jnp
from jax import lax
from jax.experimental import pallas as pl
from jax.experimental.pallas import tpu as pltpu
from jax.sharding import Mesh, PartitionSpec as P

ROWS_AXES = ("x", "zh", "y", "zl", "c")
CHIP_AXES = ("x", "y")
CORE_AXES = ("c",)
TEXT_AXES = ("zh", "zl")
MESH_IDS = pl.DeviceIdType.MESH
LOSS_LANES = 128


def unit_rows(values):
    floats = values.astype(jnp.float32)
    norms = jnp.sqrt(jnp.sum(floats * floats, 1, keepdims=True) + 1e-06)
    return (floats / norms, norms)


def back_rows(grads, units, norms):
    return (grads - units * jnp.sum(units * grads, 1, keepdims=True)) / norms


def linear_index(axes):
    index = 0
    for name in axes:
        index = index * lax.axis_size(name) + lax.axis_index(name)
    return index


def group_size(axes):
    size = 1
    for name in axes:
        size *= lax.axis_size(name)
    return size


def member(axes, k):
    coords = {}
    for name in reversed(axes):
        size = lax.axis_size(name)
        coords[name] = k % size
        k = k // size
    return tuple(coords[name] if name in coords else lax.axis_index(name) for name in ROWS_AXES)


def ring_peers():
    count, me = group_size(TEXT_AXES), linear_index(TEXT_AXES)
    return count, me, member(TEXT_AXES, (me + 1) % count), member(TEXT_AXES, (me + count - 1) % count)


def remote(src, dst, send, recv, device):
    return pltpu.make_async_remote_copy(src, dst, send, recv, device_id=device, device_id_type=MESH_IDS)


def greet_all(image_axes, barrier, image_count, image_me, right, left, extra=()):
    def greet(step, carry):
        pl.semaphore_signal(barrier, 1, device_id=member(image_axes, (image_me + step) % image_count),
                            device_id_type=MESH_IDS)
        return carry

    lax.fori_loop(1, image_count, greet, 0)
    for device in (right, left) + tuple(extra):
        pl.semaphore_signal(barrier, 1, device_id=device, device_id_type=MESH_IDS)
    pl.semaphore_wait(barrier, image_count + 1 + len(extra))


def image_direct(image_axes, scatter, src, out, send, recv, count, me):
    def start(step, carry):
        peer = (me + step) % count
        remote(src.at[peer] if scatter else src, out.at[me], send.at[peer], recv.at[me],
               member(image_axes, peer)).start()
        return carry

    lax.fori_loop(1, count, start, 0)
    out[me] = src[me] if scatter else src[...]

    def finish(step, carry):
        peer = (me + step) % count
        copy = remote(src.at[peer] if scatter else src, out.at[peer], send.at[peer], recv.at[peer],
                      member(image_axes, peer))
        copy.wait_send()
        copy.wait_recv()
        return carry

    return finish


def gather_kernel(image_axes, image_src, text_src, image_out, text_out, image_send, image_recv, text_send, text_recv):
    image_count, image_me = group_size(image_axes), linear_index(image_axes)
    count, me, right, left = ring_peers()
    right2 = member(TEXT_AXES, (me + 2) % count)
    left2 = member(TEXT_AXES, (me + count - 2) % count)
    greet_all(image_axes, pltpu.get_barrier_semaphore(), image_count, image_me, right, left, (right2, left2))
    finish = image_direct(image_axes, False, image_src, image_out, image_send, image_recv, image_count, image_me)
    sends = []

    def send(src, origin, device, slot):
        copy = remote(src, text_out.at[origin], text_send.at[slot], text_recv.at[origin], device)
        copy.start()
        sends.append(copy)

    def arrive(origin):
        remote(text_out.at[origin], text_out.at[origin], text_send.at[0], text_recv.at[origin], right).wait_recv()

    half = count // 2
    for slot, device in ((0, right), (1, right2), (half, left), (half + 1, left2)):
        send(text_src, me, device, slot)
    text_out[me] = text_src[...]
    slot_right, slot_left = 2, half + 2
    for step in range(2, half // 2 + 1):
        for distance in (2 * step - 3, 2 * step - 2):
            origin = (me + count - distance) % count
            arrive(origin)
            send(text_out.at[origin], origin, right2, slot_right)
            slot_right += 1
        for distance in (2 * step - 3, 2 * step - 2):
            if distance > half - 3:
                continue
            origin = (me + distance) % count
            arrive(origin)
            send(text_out.at[origin], origin, left2, slot_left)
            slot_left += 1
    for distance in (half - 1, half):
        arrive((me + count - distance) % count)
    for distance in (half - 2, half - 1):
        arrive((me + distance) % count)
    for copy in sends:
        copy.wait_send()
    lax.fori_loop(1, image_count, finish, 0)


def reduce_kernel(image_axes, image_src, text_src, image_out, text_out, image_send, image_recv, text_send, text_recv,
                  inbox, outbox):
    image_count, image_me = group_size(image_axes), linear_index(image_axes)
    count, me, right, left = ring_peers()
    half = count // 2
    greet_all(image_axes, pltpu.get_barrier_semaphore(), image_count, image_me, right, left)
    finish = image_direct(image_axes, True, image_src, image_out, image_send, image_recv, image_count, image_me)
    sends = [remote(text_src.at[(me + half) % count], inbox.at[0], text_send.at[0], text_recv.at[0], right),
             remote(text_src.at[(me + half + 1) % count], inbox.at[half], text_send.at[half], text_recv.at[half], left)]
    for copy in sends:
        copy.start()
    for step in range(1, half):
        chains = ((step, (me + half - step) % count, right), (half + step, (me + half + 1 + step) % count, left))
        for slot, target, device in chains:
            if slot >= count - 1:
                continue
            remote(inbox.at[slot - 1], inbox.at[slot - 1], text_send.at[slot], text_recv.at[slot - 1], device).wait_recv()
            outbox[slot] = inbox[slot - 1] + text_src[target]
            copy = remote(outbox.at[slot], inbox.at[slot], text_send.at[slot], text_recv.at[slot], device)
            copy.start()
            sends.append(copy)
    last_right, last_left = half - 1, count - 2
    for slot in (last_right, last_left):
        remote(inbox.at[slot], inbox.at[slot], text_send.at[0], text_recv.at[slot], right).wait_recv()
    text_out[...] = text_src[me] + inbox[last_right] + inbox[last_left]
    for copy in sends:
        copy.wait_send()
    lax.fori_loop(1, image_count, finish, 0)


def merged_reduce_kernel(image_axes, image_src, text_src, image_out, text_out, image_send, image_recv, text_send,
                         text_recv, inbox, outbox, halfbox, summed, half_sems):
    image_count, image_me = group_size(image_axes), linear_index(image_axes)
    count, me, right, left = ring_peers()
    half = count // 2
    core = linear_index(CORE_AXES)
    partner = member(CORE_AXES, 1 - core)
    greet_all(image_axes, pltpu.get_barrier_semaphore(), image_count, image_me, right, left, (partner,))
    sends = [remote(text_src.at[(me + half) % count], inbox.at[0], text_send.at[0], text_recv.at[0], right),
             remote(text_src.at[(me + half + 1) % count], inbox.at[half], text_send.at[half], text_recv.at[half], left)]
    for copy in sends:
        copy.start()
    swap = remote(image_src.at[1 - core], halfbox, half_sems.at[0], half_sems.at[1], partner)
    swap.start()
    swap.wait_recv()
    summed[...] = image_src[core] + halfbox[...]
    finish = image_direct(image_axes, True, summed, image_out, image_send, image_recv, image_count, image_me)
    for step in range(1, half):
        chains = ((step, (me + half - step) % count, right), (half + step, (me + half + 1 + step) % count, left))
        for slot, target, device in chains:
            if slot >= count - 1:
                continue
            remote(inbox.at[slot - 1], inbox.at[slot - 1], text_send.at[slot], text_recv.at[slot - 1], device).wait_recv()
            outbox[slot] = inbox[slot - 1] + text_src[target]
            copy = remote(outbox.at[slot], inbox.at[slot], text_send.at[slot], text_recv.at[slot], device)
            copy.start()
            sends.append(copy)
    last_right, last_left = half - 1, count - 2
    for slot in (last_right, last_left):
        remote(inbox.at[slot], inbox.at[slot], text_send.at[0], text_recv.at[slot], right).wait_recv()
    text_out[...] = text_src[me] + inbox[last_right] + inbox[last_left]
    for copy in sends:
        copy.wait_send()
    swap.wait_send()
    lax.fori_loop(1, image_count, finish, 0)


def merged_reduce(image_axes, image_src, text_src, tag):
    image_count, text_count = group_size(image_axes), group_size(TEXT_AXES)
    image_shape = image_src.shape[1:]
    block = text_src.shape[1:]
    vmem = pl.BlockSpec(memory_space=pltpu.VMEM)
    scratch = [
        pltpu.SemaphoreType.DMA((image_count,)),
        pltpu.SemaphoreType.DMA((image_count,)),
        pltpu.SemaphoreType.DMA((text_count,)),
        pltpu.SemaphoreType.DMA((text_count,)),
        pltpu.VMEM((text_count,) + block, text_src.dtype),
        pltpu.VMEM((text_count,) + block, text_src.dtype),
        pltpu.VMEM(image_shape, image_src.dtype),
        pltpu.VMEM(image_shape, image_src.dtype),
        pltpu.SemaphoreType.DMA((2,)),
    ]
    return pl.pallas_call(
        functools.partial(merged_reduce_kernel, image_axes),
        out_shape=(jax.ShapeDtypeStruct(image_shape, image_src.dtype), jax.ShapeDtypeStruct(block, text_src.dtype)),
        in_specs=[vmem, vmem],
        out_specs=(vmem, vmem),
        scratch_shapes=scratch,
        compiler_params=pltpu.CompilerParams(collective_id=tag, has_side_effects=True),
    )(image_src, text_src)


def exchange(image_axes, image_src, text_src, scatter, tag):
    image_count, text_count = group_size(image_axes), group_size(TEXT_AXES)
    image_shape = image_src.shape if scatter else (image_count,) + image_src.shape
    text_shape = text_src.shape[1:] if scatter else (text_count,) + text_src.shape
    block = text_src.shape[1:] if scatter else text_src.shape
    vmem = pl.BlockSpec(memory_space=pltpu.VMEM)
    scratch = [
        pltpu.SemaphoreType.DMA((image_count,)),
        pltpu.SemaphoreType.DMA((image_count,)),
        pltpu.SemaphoreType.DMA((text_count,)),
        pltpu.SemaphoreType.DMA((text_count,)),
    ]
    if scatter:
        scratch += [pltpu.VMEM((text_count,) + block, text_src.dtype)] * 2
    return pl.pallas_call(
        functools.partial(reduce_kernel if scatter else gather_kernel, image_axes),
        out_shape=(jax.ShapeDtypeStruct(image_shape, image_src.dtype), jax.ShapeDtypeStruct(text_shape, text_src.dtype)),
        in_specs=[vmem, vmem],
        out_specs=(vmem, vmem),
        scratch_shapes=scratch,
        compiler_params=pltpu.CompilerParams(collective_id=tag, has_side_effects=True),
    )(image_src, text_src)


def pair_kernel(plan, *refs):
    count_groups = len(plan)
    srcs, outs = refs[:count_groups], refs[count_groups:2 * count_groups]
    sems = refs[2 * count_groups:]
    groups = [
        (axes, scatter, srcs[g], outs[g], sems[2 * g], sems[2 * g + 1]) for g, (axes, scatter) in enumerate(plan)
    ]
    barrier = pltpu.get_barrier_semaphore()
    peers = 0
    for axes, scatter, src, out, send, recv in groups:
        count, me = group_size(axes), linear_index(axes)
        peers += count - 1

        def greet(step, carry, axes=axes, count=count, me=me):
            pl.semaphore_signal(barrier, 1, device_id=member(axes, (me + step) % count), device_id_type=MESH_IDS)
            return carry

        lax.fori_loop(1, count, greet, 0)
    pl.semaphore_wait(barrier, peers)

    for axes, scatter, src, out, send, recv in groups:
        count, me = group_size(axes), linear_index(axes)

        def start(step, carry, axes=axes, scatter=scatter, count=count, me=me, src=src, out=out, send=send, recv=recv):
            peer = (me + step) % count
            pltpu.make_async_remote_copy(
                src.at[peer] if scatter else src, out.at[me], send.at[peer], recv.at[me],
                device_id=member(axes, peer), device_id_type=MESH_IDS,
            ).start()
            return carry

        lax.fori_loop(1, count, start, 0)

    for axes, scatter, src, out, send, recv in groups:
        count, me = group_size(axes), linear_index(axes)
        out[me] = src[me] if scatter else src[...]

    for axes, scatter, src, out, send, recv in groups:
        count, me = group_size(axes), linear_index(axes)

        def finish(step, carry, axes=axes, scatter=scatter, count=count, me=me, src=src, out=out, send=send, recv=recv):
            peer = (me + step) % count
            copy = pltpu.make_async_remote_copy(
                src.at[peer] if scatter else src, out.at[peer], send.at[peer], recv.at[peer],
                device_id=member(axes, peer), device_id_type=MESH_IDS,
            )
            copy.wait_send()
            copy.wait_recv()
            return carry

        lax.fori_loop(1, count, finish, 0)


def pair_exchange(routes, tag):
    plan = tuple((axes, scatter) for axes, src, scatter in routes)
    srcs = [src for axes, src, scatter in routes]
    shapes = [
        jax.ShapeDtypeStruct(src.shape if scatter else (group_size(axes),) + src.shape, src.dtype)
        for axes, src, scatter in routes
    ]
    sems = []
    for axes, src, scatter in routes:
        sems += [pltpu.SemaphoreType.DMA((group_size(axes),))] * 2
    vmem = pl.BlockSpec(memory_space=pltpu.VMEM)
    return pl.pallas_call(
        functools.partial(pair_kernel, plan),
        out_shape=tuple(shapes),
        in_specs=[vmem] * len(routes),
        out_specs=tuple([vmem] * len(routes)),
        scratch_shapes=sems,
        compiler_params=pltpu.CompilerParams(collective_id=tag, has_side_effects=True),
    )(*srcs)


def local(images, texts, scale, shift):
    rows, width = images.shape
    image_unit, image_norm = unit_rows(images)
    text_unit, text_norm = unit_rows(texts)
    image_emb = image_unit.astype(jnp.bfloat16)
    text_emb = text_unit.astype(jnp.bfloat16)
    chips = group_size(CHIP_AXES)
    cores = group_size(CORE_AXES)
    image_count = chips * cores
    text_count = group_size(TEXT_AXES)
    total = image_count * text_count * rows
    gathered, seen = exchange(CORE_AXES + CHIP_AXES, image_emb, text_emb, False, 0)
    gathered = gathered.reshape(image_count * rows, width)
    seen = seen.reshape(text_count * rows, width)
    image_ids = jnp.arange(image_count * rows, dtype=jnp.int32)[:, None]
    text_ids = jnp.arange(text_count * rows, dtype=jnp.int32)[None, :]
    mine_i = linear_index(CORE_AXES + CHIP_AXES)
    mine_t = linear_index(TEXT_AXES)
    label = (
        (image_ids // rows == mine_i) & (text_ids // rows == mine_t) & (image_ids % rows == text_ids % rows)
    ).astype(jnp.float32)
    logit = (
        scale
        * lax.dot_general(gathered, seen, (((1,), (1,)), ((), ())), preferred_element_type=jnp.float32)
        + shift
    )
    loss = jnp.sum(jax.nn.softplus(logit * (1.0 - 2.0 * label)), 1, keepdims=True) / total
    coef = ((jax.nn.sigmoid(logit) - label) * scale).astype(jnp.bfloat16)
    image_part = jnp.dot(coef, seen, preferred_element_type=jnp.float32)
    text_part = lax.dot_general(coef, gathered, (((0,), (0,)), ((), ())), preferred_element_type=jnp.float32)
    image_part = jnp.concatenate([image_part, jnp.broadcast_to(loss, (image_count * rows, LOSS_LANES))], 1)
    image_in, text_in = merged_reduce(
        CHIP_AXES, image_part.reshape(cores, chips, rows, width + LOSS_LANES), text_part.reshape(text_count, rows, width), 3
    )
    image_in = jnp.sum(image_in, 0)
    text_sum = text_in
    image_grad = back_rows(image_in[:, :width], image_unit, image_norm)
    text_grad = back_rows(text_sum, text_unit, text_norm)
    return (image_in[:, width], image_grad, text_grad)


def solution(mesh):
    blk, grp = mesh.devices.shape
    fine = Mesh(mesh.devices.reshape(blk // 2, 2, grp // 16, 8, 2), ROWS_AXES)
    in_specs = (P(ROWS_AXES, None), P(ROWS_AXES, None), P(), P())
    out_specs = (P(ROWS_AXES), P(ROWS_AXES, None), P(ROWS_AXES, None))
    return jax.shard_map(local, mesh=fine, in_specs=in_specs, out_specs=out_specs, check_vma=False)
```

```python
import functools

import jax
import jax.numpy as jnp
from jax import lax
from jax.experimental import pallas as pl
from jax.experimental.pallas import tpu as pltpu
from jax.sharding import Mesh, PartitionSpec as P

ROWS_AXES = ("x", "zh", "y", "zl", "c")
CHIP_AXES = ("x", "y")
CORE_AXES = ("c",)
TEXT_AXES = ("zh", "zl")
MESH_IDS = pl.DeviceIdType.MESH
LOSS_LANES = 128


def unit_rows(values):
    floats = values.astype(jnp.float32)
    norms = jnp.sqrt(jnp.sum(floats * floats, 1, keepdims=True) + 1e-06)
    return (floats / norms, norms)


def back_rows(grads, units, norms):
    return (grads - units * jnp.sum(units * grads, 1, keepdims=True)) / norms


def linear_index(axes):
    index = 0
    for name in axes:
        index = index * lax.axis_size(name) + lax.axis_index(name)
    return index


def group_size(axes):
    size = 1
    for name in axes:
        size *= lax.axis_size(name)
    return size


def member(axes, k):
    coords = {}
    for name in reversed(axes):
        size = lax.axis_size(name)
        coords[name] = k % size
        k = k // size
    return tuple(coords[name] if name in coords else lax.axis_index(name) for name in ROWS_AXES)


def ring_peers():
    count, me = group_size(TEXT_AXES), linear_index(TEXT_AXES)
    return count, me, member(TEXT_AXES, (me + 1) % count), member(TEXT_AXES, (me + count - 1) % count)


def remote(src, dst, send, recv, device):
    return pltpu.make_async_remote_copy(src, dst, send, recv, device_id=device, device_id_type=MESH_IDS)


def greet_all(image_axes, barrier, image_count, image_me, right, left, extra=()):
    def greet(step, carry):
        pl.semaphore_signal(barrier, 1, device_id=member(image_axes, (image_me + step) % image_count),
                            device_id_type=MESH_IDS)
        return carry

    lax.fori_loop(1, image_count, greet, 0)
    for device in (right, left) + tuple(extra):
        pl.semaphore_signal(barrier, 1, device_id=device, device_id_type=MESH_IDS)
    pl.semaphore_wait(barrier, image_count + 1 + len(extra))


def image_direct(image_axes, scatter, src, out, send, recv, count, me):
    def start(step, carry):
        peer = (me + step) % count
        remote(src.at[peer] if scatter else src, out.at[me], send.at[peer], recv.at[me],
               member(image_axes, peer)).start()
        return carry

    lax.fori_loop(1, count, start, 0)
    out[me] = src[me] if scatter else src[...]

    def finish(step, carry):
        peer = (me + step) % count
        copy = remote(src.at[peer] if scatter else src, out.at[peer], send.at[peer], recv.at[peer],
                      member(image_axes, peer))
        copy.wait_send()
        copy.wait_recv()
        return carry

    return finish


def gather_kernel(image_axes, image_src, text_src, image_out, text_out, image_send, image_recv, text_send, text_recv):
    image_count, image_me = group_size(image_axes), linear_index(image_axes)
    count, me, right, left = ring_peers()
    right2 = member(TEXT_AXES, (me + 2) % count)
    left2 = member(TEXT_AXES, (me + count - 2) % count)
    greet_all(image_axes, pltpu.get_barrier_semaphore(), image_count, image_me, right, left, (right2, left2))
    finish = image_direct(image_axes, False, image_src, image_out, image_send, image_recv, image_count, image_me)
    sends = []

    def send(src, origin, device, slot):
        copy = remote(src, text_out.at[origin], text_send.at[slot], text_recv.at[origin], device)
        copy.start()
        sends.append(copy)

    def arrive(origin):
        remote(text_out.at[origin], text_out.at[origin], text_send.at[0], text_recv.at[origin], right).wait_recv()

    half = count // 2
    for slot, device in ((0, right), (1, right2), (half, left), (half + 1, left2)):
        send(text_src, me, device, slot)
    text_out[me] = text_src[...]
    slot_right, slot_left = 2, half + 2
    for step in range(2, half // 2 + 1):
        for distance in (2 * step - 3, 2 * step - 2):
            origin = (me + count - distance) % count
            arrive(origin)
            send(text_out.at[origin], origin, right2, slot_right)
            slot_right += 1
        for distance in (2 * step - 3, 2 * step - 2):
            if distance > half - 3:
                continue
            origin = (me + distance) % count
            arrive(origin)
            send(text_out.at[origin], origin, left2, slot_left)
            slot_left += 1
    for distance in (half - 1, half):
        arrive((me + count - distance) % count)
    for distance in (half - 2, half - 1):
        arrive((me + distance) % count)
    for copy in sends:
        copy.wait_send()
    lax.fori_loop(1, image_count, finish, 0)


def reduce_kernel(image_axes, image_src, text_src, image_out, text_out, image_send, image_recv, text_send, text_recv,
                  inbox, outbox):
    image_count, image_me = group_size(image_axes), linear_index(image_axes)
    count, me, right, left = ring_peers()
    half = count // 2
    greet_all(image_axes, pltpu.get_barrier_semaphore(), image_count, image_me, right, left)
    finish = image_direct(image_axes, True, image_src, image_out, image_send, image_recv, image_count, image_me)
    sends = [remote(text_src.at[(me + half) % count], inbox.at[0], text_send.at[0], text_recv.at[0], right),
             remote(text_src.at[(me + half + 1) % count], inbox.at[half], text_send.at[half], text_recv.at[half], left)]
    for copy in sends:
        copy.start()
    for step in range(1, half):
        chains = ((step, (me + half - step) % count, right), (half + step, (me + half + 1 + step) % count, left))
        for slot, target, device in chains:
            if slot >= count - 1:
                continue
            remote(inbox.at[slot - 1], inbox.at[slot - 1], text_send.at[slot], text_recv.at[slot - 1], device).wait_recv()
            outbox[slot] = inbox[slot - 1] + text_src[target]
            copy = remote(outbox.at[slot], inbox.at[slot], text_send.at[slot], text_recv.at[slot], device)
            copy.start()
            sends.append(copy)
    last_right, last_left = half - 1, count - 2
    for slot in (last_right, last_left):
        remote(inbox.at[slot], inbox.at[slot], text_send.at[0], text_recv.at[slot], right).wait_recv()
    text_out[...] = text_src[me] + inbox[last_right] + inbox[last_left]
    for copy in sends:
        copy.wait_send()
    lax.fori_loop(1, image_count, finish, 0)


def merged_reduce_kernel(image_axes, image_src, text_src, image_out, text_out, image_send, image_recv, text_send,
                         text_recv, inbox, outbox, halfbox, summed, half_sems):
    image_count, image_me = group_size(image_axes), linear_index(image_axes)
    count, me, right, left = ring_peers()
    right2 = member(TEXT_AXES, (me + 2) % count)
    left2 = member(TEXT_AXES, (me + count - 2) % count)
    core = linear_index(CORE_AXES)
    partner = member(CORE_AXES, 1 - core)
    greet_all(image_axes, pltpu.get_barrier_semaphore(), image_count, image_me, right, left, (right2, left2, partner))
    chains = (
        (0, 4, lambda step: right2, lambda step: 10 - 2 * step),
        (4, 4, lambda step: right2 if step < 4 else right, lambda step: 9 - 2 * step),
        (8, 3, lambda step: left2, lambda step: 2 * step - 8),
        (11, 4, lambda step: left2 if step < 4 else left, lambda step: 2 * step - 9),
    )
    sends = []

    def step_sends(step):
        for base, steps, device, offset in chains:
            if step > steps:
                continue
            slot = base + step - 1
            target = (me + count + offset(step)) % count
            if step == 1:
                source = text_src.at[target]
            else:
                remote(inbox.at[slot - 1], inbox.at[slot - 1], text_send.at[slot], text_recv.at[slot - 1],
                       right).wait_recv()
                outbox[slot] = inbox[slot - 1] + text_src[target]
                source = outbox.at[slot]
            copy = remote(source, inbox.at[slot], text_send.at[slot], text_recv.at[slot], device(step))
            copy.start()
            sends.append(copy)

    step_sends(1)
    swap = remote(image_src.at[1 - core], halfbox, half_sems.at[0], half_sems.at[1], partner)
    swap.start()
    swap.wait_recv()
    summed[...] = image_src[core] + halfbox[...]
    finish = image_direct(image_axes, True, summed, image_out, image_send, image_recv, image_count, image_me)
    for step in range(2, 5):
        step_sends(step)
    finals = (3, 7, 10, 14)
    for slot in finals:
        remote(inbox.at[slot], inbox.at[slot], text_send.at[0], text_recv.at[slot], right).wait_recv()
    text_out[...] = text_src[me] + inbox[finals[0]] + inbox[finals[1]] + inbox[finals[2]] + inbox[finals[3]]
    for copy in sends:
        copy.wait_send()
    swap.wait_send()
    lax.fori_loop(1, image_count, finish, 0)


def merged_reduce(image_axes, image_src, text_src, tag):
    image_count, text_count = group_size(image_axes), group_size(TEXT_AXES)
    image_shape = image_src.shape[1:]
    block = text_src.shape[1:]
    vmem = pl.BlockSpec(memory_space=pltpu.VMEM)
    scratch = [
        pltpu.SemaphoreType.DMA((image_count,)),
        pltpu.SemaphoreType.DMA((image_count,)),
        pltpu.SemaphoreType.DMA((text_count,)),
        pltpu.SemaphoreType.DMA((text_count,)),
        pltpu.VMEM((text_count,) + block, text_src.dtype),
        pltpu.VMEM((text_count,) + block, text_src.dtype),
        pltpu.VMEM(image_shape, image_src.dtype),
        pltpu.VMEM(image_shape, image_src.dtype),
        pltpu.SemaphoreType.DMA((2,)),
    ]
    return pl.pallas_call(
        functools.partial(merged_reduce_kernel, image_axes),
        out_shape=(jax.ShapeDtypeStruct(image_shape, image_src.dtype), jax.ShapeDtypeStruct(block, text_src.dtype)),
        in_specs=[vmem, vmem],
        out_specs=(vmem, vmem),
        scratch_shapes=scratch,
        compiler_params=pltpu.CompilerParams(collective_id=tag, has_side_effects=True),
    )(image_src, text_src)


def exchange(image_axes, image_src, text_src, scatter, tag):
    image_count, text_count = group_size(image_axes), group_size(TEXT_AXES)
    image_shape = image_src.shape if scatter else (image_count,) + image_src.shape
    text_shape = text_src.shape[1:] if scatter else (text_count,) + text_src.shape
    block = text_src.shape[1:] if scatter else text_src.shape
    vmem = pl.BlockSpec(memory_space=pltpu.VMEM)
    scratch = [
        pltpu.SemaphoreType.DMA((image_count,)),
        pltpu.SemaphoreType.DMA((image_count,)),
        pltpu.SemaphoreType.DMA((text_count,)),
        pltpu.SemaphoreType.DMA((text_count,)),
    ]
    if scatter:
        scratch += [pltpu.VMEM((text_count,) + block, text_src.dtype)] * 2
    return pl.pallas_call(
        functools.partial(reduce_kernel if scatter else gather_kernel, image_axes),
        out_shape=(jax.ShapeDtypeStruct(image_shape, image_src.dtype), jax.ShapeDtypeStruct(text_shape, text_src.dtype)),
        in_specs=[vmem, vmem],
        out_specs=(vmem, vmem),
        scratch_shapes=scratch,
        compiler_params=pltpu.CompilerParams(collective_id=tag, has_side_effects=True),
    )(image_src, text_src)


def pair_kernel(plan, *refs):
    count_groups = len(plan)
    srcs, outs = refs[:count_groups], refs[count_groups:2 * count_groups]
    sems = refs[2 * count_groups:]
    groups = [
        (axes, scatter, srcs[g], outs[g], sems[2 * g], sems[2 * g + 1]) for g, (axes, scatter) in enumerate(plan)
    ]
    barrier = pltpu.get_barrier_semaphore()
    peers = 0
    for axes, scatter, src, out, send, recv in groups:
        count, me = group_size(axes), linear_index(axes)
        peers += count - 1

        def greet(step, carry, axes=axes, count=count, me=me):
            pl.semaphore_signal(barrier, 1, device_id=member(axes, (me + step) % count), device_id_type=MESH_IDS)
            return carry

        lax.fori_loop(1, count, greet, 0)
    pl.semaphore_wait(barrier, peers)

    for axes, scatter, src, out, send, recv in groups:
        count, me = group_size(axes), linear_index(axes)

        def start(step, carry, axes=axes, scatter=scatter, count=count, me=me, src=src, out=out, send=send, recv=recv):
            peer = (me + step) % count
            pltpu.make_async_remote_copy(
                src.at[peer] if scatter else src, out.at[me], send.at[peer], recv.at[me],
                device_id=member(axes, peer), device_id_type=MESH_IDS,
            ).start()
            return carry

        lax.fori_loop(1, count, start, 0)

    for axes, scatter, src, out, send, recv in groups:
        count, me = group_size(axes), linear_index(axes)
        out[me] = src[me] if scatter else src[...]

    for axes, scatter, src, out, send, recv in groups:
        count, me = group_size(axes), linear_index(axes)

        def finish(step, carry, axes=axes, scatter=scatter, count=count, me=me, src=src, out=out, send=send, recv=recv):
            peer = (me + step) % count
            copy = pltpu.make_async_remote_copy(
                src.at[peer] if scatter else src, out.at[peer], send.at[peer], recv.at[peer],
                device_id=member(axes, peer), device_id_type=MESH_IDS,
            )
            copy.wait_send()
            copy.wait_recv()
            return carry

        lax.fori_loop(1, count, finish, 0)


def pair_exchange(routes, tag):
    plan = tuple((axes, scatter) for axes, src, scatter in routes)
    srcs = [src for axes, src, scatter in routes]
    shapes = [
        jax.ShapeDtypeStruct(src.shape if scatter else (group_size(axes),) + src.shape, src.dtype)
        for axes, src, scatter in routes
    ]
    sems = []
    for axes, src, scatter in routes:
        sems += [pltpu.SemaphoreType.DMA((group_size(axes),))] * 2
    vmem = pl.BlockSpec(memory_space=pltpu.VMEM)
    return pl.pallas_call(
        functools.partial(pair_kernel, plan),
        out_shape=tuple(shapes),
        in_specs=[vmem] * len(routes),
        out_specs=tuple([vmem] * len(routes)),
        scratch_shapes=sems,
        compiler_params=pltpu.CompilerParams(collective_id=tag, has_side_effects=True),
    )(*srcs)


def local(images, texts, scale, shift):
    rows, width = images.shape
    image_unit, image_norm = unit_rows(images)
    text_unit, text_norm = unit_rows(texts)
    image_emb = image_unit.astype(jnp.bfloat16)
    text_emb = text_unit.astype(jnp.bfloat16)
    chips = group_size(CHIP_AXES)
    cores = group_size(CORE_AXES)
    image_count = chips * cores
    text_count = group_size(TEXT_AXES)
    total = image_count * text_count * rows
    gathered, seen = exchange(CORE_AXES + CHIP_AXES, image_emb, text_emb, False, 0)
    gathered = gathered.reshape(image_count * rows, width)
    seen = seen.reshape(text_count * rows, width)
    image_ids = jnp.arange(image_count * rows, dtype=jnp.int32)[:, None]
    text_ids = jnp.arange(text_count * rows, dtype=jnp.int32)[None, :]
    mine_i = linear_index(CORE_AXES + CHIP_AXES)
    mine_t = linear_index(TEXT_AXES)
    label = (
        (image_ids // rows == mine_i) & (text_ids // rows == mine_t) & (image_ids % rows == text_ids % rows)
    ).astype(jnp.float32)
    logit = (
        scale
        * lax.dot_general(gathered, seen, (((1,), (1,)), ((), ())), preferred_element_type=jnp.float32)
        + shift
    )
    loss = jnp.sum(jax.nn.softplus(logit * (1.0 - 2.0 * label)), 1, keepdims=True) / total
    coef = ((jax.nn.sigmoid(logit) - label) * scale).astype(jnp.bfloat16)
    image_part = jnp.dot(coef, seen, preferred_element_type=jnp.float32)
    text_part = lax.dot_general(coef, gathered, (((0,), (0,)), ((), ())), preferred_element_type=jnp.float32)
    image_part = jnp.concatenate([image_part, jnp.broadcast_to(loss, (image_count * rows, LOSS_LANES))], 1)
    image_in, text_in = merged_reduce(
        CHIP_AXES, image_part.reshape(cores, chips, rows, width + LOSS_LANES), text_part.reshape(text_count, rows, width), 3
    )
    image_in = jnp.sum(image_in, 0)
    text_sum = text_in
    image_grad = back_rows(image_in[:, :width], image_unit, image_norm)
    text_grad = back_rows(text_sum, text_unit, text_norm)
    return (image_in[:, width], image_grad, text_grad)


def solution(mesh):
    blk, grp = mesh.devices.shape
    fine = Mesh(mesh.devices.reshape(blk // 2, 2, grp // 16, 8, 2), ROWS_AXES)
    in_specs = (P(ROWS_AXES, None), P(ROWS_AXES, None), P(), P())
    out_specs = (P(ROWS_AXES), P(ROWS_AXES, None), P(ROWS_AXES, None))
    return jax.shard_map(local, mesh=fine, in_specs=in_specs, out_specs=out_specs, check_vma=False)
```

```python
import functools

import jax
import jax.numpy as jnp
from jax import lax
from jax.experimental import pallas as pl
from jax.experimental.pallas import tpu as pltpu
from jax.sharding import Mesh, PartitionSpec as P

ROWS_AXES = ("x", "zh", "y", "zl", "c")
CHIP_AXES = ("x", "y")
CORE_AXES = ("c",)
TEXT_AXES = ("zh", "zl")
MESH_IDS = pl.DeviceIdType.MESH
LOSS_LANES = 128


def unit_rows(values):
    floats = values.astype(jnp.float32)
    norms = jnp.sqrt(jnp.sum(floats * floats, 1, keepdims=True) + 1e-06)
    return (floats / norms, norms)


def back_rows(grads, units, norms):
    return (grads - units * jnp.sum(units * grads, 1, keepdims=True)) / norms


def linear_index(axes):
    index = 0
    for name in axes:
        index = index * lax.axis_size(name) + lax.axis_index(name)
    return index


def group_size(axes):
    size = 1
    for name in axes:
        size *= lax.axis_size(name)
    return size


def member(axes, k):
    coords = {}
    for name in reversed(axes):
        size = lax.axis_size(name)
        coords[name] = k % size
        k = k // size
    return tuple(coords[name] if name in coords else lax.axis_index(name) for name in ROWS_AXES)


def ring_peers():
    count, me = group_size(TEXT_AXES), linear_index(TEXT_AXES)
    return count, me, member(TEXT_AXES, (me + 1) % count), member(TEXT_AXES, (me + count - 1) % count)


def remote(src, dst, send, recv, device):
    return pltpu.make_async_remote_copy(src, dst, send, recv, device_id=device, device_id_type=MESH_IDS)


def greet_all(image_axes, barrier, image_count, image_me, right, left, extra=()):
    def greet(step, carry):
        pl.semaphore_signal(barrier, 1, device_id=member(image_axes, (image_me + step) % image_count),
                            device_id_type=MESH_IDS)
        return carry

    lax.fori_loop(1, image_count, greet, 0)
    for device in (right, left) + tuple(extra):
        pl.semaphore_signal(barrier, 1, device_id=device, device_id_type=MESH_IDS)
    pl.semaphore_wait(barrier, image_count + 1 + len(extra))


def image_direct(image_axes, scatter, src, out, send, recv, count, me):
    def start(step, carry):
        peer = (me + step) % count
        remote(src.at[peer] if scatter else src, out.at[me], send.at[peer], recv.at[me],
               member(image_axes, peer)).start()
        return carry

    lax.fori_loop(1, count, start, 0)
    out[me] = src[me] if scatter else src[...]

    def finish(step, carry):
        peer = (me + step) % count
        copy = remote(src.at[peer] if scatter else src, out.at[peer], send.at[peer], recv.at[peer],
                      member(image_axes, peer))
        copy.wait_send()
        copy.wait_recv()
        return carry

    return finish


def gather_kernel(image_axes, image_src, text_src, image_out, text_out, image_send, image_recv, text_send, text_recv):
    image_count, image_me = group_size(image_axes), linear_index(image_axes)
    count, me, right, left = ring_peers()
    right2 = member(TEXT_AXES, (me + 2) % count)
    left2 = member(TEXT_AXES, (me + count - 2) % count)
    greet_all(image_axes, pltpu.get_barrier_semaphore(), image_count, image_me, right, left, (right2, left2))
    finish = image_direct(image_axes, False, image_src, image_out, image_send, image_recv, image_count, image_me)
    sends = []

    def send(src, origin, device, slot):
        copy = remote(src, text_out.at[origin], text_send.at[slot], text_recv.at[origin], device)
        copy.start()
        sends.append(copy)

    def arrive(origin):
        remote(text_out.at[origin], text_out.at[origin], text_send.at[0], text_recv.at[origin], right).wait_recv()

    half = count // 2
    for slot, device in ((0, right), (1, right2), (half, left), (half + 1, left2)):
        send(text_src, me, device, slot)
    text_out[me] = text_src[...]
    slot_right, slot_left = 2, half + 2
    for step in range(2, half // 2 + 1):
        for distance in (2 * step - 3, 2 * step - 2):
            origin = (me + count - distance) % count
            arrive(origin)
            send(text_out.at[origin], origin, right2, slot_right)
            slot_right += 1
        for distance in (2 * step - 3, 2 * step - 2):
            if distance > half - 3:
                continue
            origin = (me + distance) % count
            arrive(origin)
            send(text_out.at[origin], origin, left2, slot_left)
            slot_left += 1
    for distance in (half - 1, half):
        arrive((me + count - distance) % count)
    for distance in (half - 2, half - 1):
        arrive((me + distance) % count)
    for copy in sends:
        copy.wait_send()
    lax.fori_loop(1, image_count, finish, 0)


def reduce_kernel(image_axes, image_src, text_src, image_out, text_out, image_send, image_recv, text_send, text_recv,
                  inbox, outbox):
    image_count, image_me = group_size(image_axes), linear_index(image_axes)
    count, me, right, left = ring_peers()
    half = count // 2
    greet_all(image_axes, pltpu.get_barrier_semaphore(), image_count, image_me, right, left)
    finish = image_direct(image_axes, True, image_src, image_out, image_send, image_recv, image_count, image_me)
    sends = [remote(text_src.at[(me + half) % count], inbox.at[0], text_send.at[0], text_recv.at[0], right),
             remote(text_src.at[(me + half + 1) % count], inbox.at[half], text_send.at[half], text_recv.at[half], left)]
    for copy in sends:
        copy.start()
    for step in range(1, half):
        chains = ((step, (me + half - step) % count, right), (half + step, (me + half + 1 + step) % count, left))
        for slot, target, device in chains:
            if slot >= count - 1:
                continue
            remote(inbox.at[slot - 1], inbox.at[slot - 1], text_send.at[slot], text_recv.at[slot - 1], device).wait_recv()
            outbox[slot] = inbox[slot - 1] + text_src[target]
            copy = remote(outbox.at[slot], inbox.at[slot], text_send.at[slot], text_recv.at[slot], device)
            copy.start()
            sends.append(copy)
    last_right, last_left = half - 1, count - 2
    for slot in (last_right, last_left):
        remote(inbox.at[slot], inbox.at[slot], text_send.at[0], text_recv.at[slot], right).wait_recv()
    text_out[...] = text_src[me] + inbox[last_right] + inbox[last_left]
    for copy in sends:
        copy.wait_send()
    lax.fori_loop(1, image_count, finish, 0)


def merged_reduce_kernel(image_axes, image_src, text_src, image_out, text_out, image_send, image_recv, text_send,
                         text_recv, inbox, outbox, halfbox, summed, half_sems):
    image_count, image_me = group_size(image_axes), linear_index(image_axes)
    count, me, right, left = ring_peers()
    right2 = member(TEXT_AXES, (me + 2) % count)
    left2 = member(TEXT_AXES, (me + count - 2) % count)
    core = linear_index(CORE_AXES)
    partner = member(CORE_AXES, 1 - core)
    greet_all(image_axes, pltpu.get_barrier_semaphore(), image_count, image_me, right, left, (right2, left2, partner))
    chains = (
        (0, 4, lambda step: right2, lambda step: 10 - 2 * step),
        (4, 4, lambda step: right2 if step < 4 else right, lambda step: 9 - 2 * step),
        (8, 3, lambda step: left2, lambda step: 2 * step - 8),
        (11, 4, lambda step: left2 if step < 4 else left, lambda step: 2 * step - 9),
    )
    sends = []

    def step_sends(step):
        for base, steps, device, offset in chains:
            if step > steps:
                continue
            slot = base + step - 1
            target = (me + count + offset(step)) % count
            if step == 1:
                source = text_src.at[target]
            else:
                remote(inbox.at[slot - 1], inbox.at[slot - 1], text_send.at[slot], text_recv.at[slot - 1],
                       right).wait_recv()
                outbox[slot] = inbox[slot - 1] + text_src[target]
                source = outbox.at[slot]
            copy = remote(source, inbox.at[slot], text_send.at[slot], text_recv.at[slot], device(step))
            copy.start()
            sends.append(copy)

    swap = remote(image_src.at[1 - core], halfbox, half_sems.at[0], half_sems.at[1], partner)
    swap.start()
    step_sends(1)
    step_sends(2)
    swap.wait_recv()
    summed[...] = image_src[core] + halfbox[...]
    finish = image_direct(image_axes, True, summed, image_out, image_send, image_recv, image_count, image_me)
    for step in range(3, 5):
        step_sends(step)
    finals = (3, 7, 10, 14)
    for slot in finals:
        remote(inbox.at[slot], inbox.at[slot], text_send.at[0], text_recv.at[slot], right).wait_recv()
    text_out[...] = text_src[me] + inbox[finals[0]] + inbox[finals[1]] + inbox[finals[2]] + inbox[finals[3]]
    for copy in sends:
        copy.wait_send()
    swap.wait_send()
    lax.fori_loop(1, image_count, finish, 0)


def merged_reduce(image_axes, image_src, text_src, tag):
    image_count, text_count = group_size(image_axes), group_size(TEXT_AXES)
    image_shape = image_src.shape[1:]
    block = text_src.shape[1:]
    vmem = pl.BlockSpec(memory_space=pltpu.VMEM)
    scratch = [
        pltpu.SemaphoreType.DMA((image_count,)),
        pltpu.SemaphoreType.DMA((image_count,)),
        pltpu.SemaphoreType.DMA((text_count,)),
        pltpu.SemaphoreType.DMA((text_count,)),
        pltpu.VMEM((text_count,) + block, text_src.dtype),
        pltpu.VMEM((text_count,) + block, text_src.dtype),
        pltpu.VMEM(image_shape, image_src.dtype),
        pltpu.VMEM(image_shape, image_src.dtype),
        pltpu.SemaphoreType.DMA((2,)),
    ]
    return pl.pallas_call(
        functools.partial(merged_reduce_kernel, image_axes),
        out_shape=(jax.ShapeDtypeStruct(image_shape, image_src.dtype), jax.ShapeDtypeStruct(block, text_src.dtype)),
        in_specs=[vmem, vmem],
        out_specs=(vmem, vmem),
        scratch_shapes=scratch,
        compiler_params=pltpu.CompilerParams(collective_id=tag, has_side_effects=True),
    )(image_src, text_src)


def exchange(image_axes, image_src, text_src, scatter, tag):
    image_count, text_count = group_size(image_axes), group_size(TEXT_AXES)
    image_shape = image_src.shape if scatter else (image_count,) + image_src.shape
    text_shape = text_src.shape[1:] if scatter else (text_count,) + text_src.shape
    block = text_src.shape[1:] if scatter else text_src.shape
    vmem = pl.BlockSpec(memory_space=pltpu.VMEM)
    scratch = [
        pltpu.SemaphoreType.DMA((image_count,)),
        pltpu.SemaphoreType.DMA((image_count,)),
        pltpu.SemaphoreType.DMA((text_count,)),
        pltpu.SemaphoreType.DMA((text_count,)),
    ]
    if scatter:
        scratch += [pltpu.VMEM((text_count,) + block, text_src.dtype)] * 2
    return pl.pallas_call(
        functools.partial(reduce_kernel if scatter else gather_kernel, image_axes),
        out_shape=(jax.ShapeDtypeStruct(image_shape, image_src.dtype), jax.ShapeDtypeStruct(text_shape, text_src.dtype)),
        in_specs=[vmem, vmem],
        out_specs=(vmem, vmem),
        scratch_shapes=scratch,
        compiler_params=pltpu.CompilerParams(collective_id=tag, has_side_effects=True),
    )(image_src, text_src)


def pair_kernel(plan, *refs):
    count_groups = len(plan)
    srcs, outs = refs[:count_groups], refs[count_groups:2 * count_groups]
    sems = refs[2 * count_groups:]
    groups = [
        (axes, scatter, srcs[g], outs[g], sems[2 * g], sems[2 * g + 1]) for g, (axes, scatter) in enumerate(plan)
    ]
    barrier = pltpu.get_barrier_semaphore()
    peers = 0
    for axes, scatter, src, out, send, recv in groups:
        count, me = group_size(axes), linear_index(axes)
        peers += count - 1

        def greet(step, carry, axes=axes, count=count, me=me):
            pl.semaphore_signal(barrier, 1, device_id=member(axes, (me + step) % count), device_id_type=MESH_IDS)
            return carry

        lax.fori_loop(1, count, greet, 0)
    pl.semaphore_wait(barrier, peers)

    for axes, scatter, src, out, send, recv in groups:
        count, me = group_size(axes), linear_index(axes)

        def start(step, carry, axes=axes, scatter=scatter, count=count, me=me, src=src, out=out, send=send, recv=recv):
            peer = (me + step) % count
            pltpu.make_async_remote_copy(
                src.at[peer] if scatter else src, out.at[me], send.at[peer], recv.at[me],
                device_id=member(axes, peer), device_id_type=MESH_IDS,
            ).start()
            return carry

        lax.fori_loop(1, count, start, 0)

    for axes, scatter, src, out, send, recv in groups:
        count, me = group_size(axes), linear_index(axes)
        out[me] = src[me] if scatter else src[...]

    for axes, scatter, src, out, send, recv in groups:
        count, me = group_size(axes), linear_index(axes)

        def finish(step, carry, axes=axes, scatter=scatter, count=count, me=me, src=src, out=out, send=send, recv=recv):
            peer = (me + step) % count
            copy = pltpu.make_async_remote_copy(
                src.at[peer] if scatter else src, out.at[peer], send.at[peer], recv.at[peer],
                device_id=member(axes, peer), device_id_type=MESH_IDS,
            )
            copy.wait_send()
            copy.wait_recv()
            return carry

        lax.fori_loop(1, count, finish, 0)


def pair_exchange(routes, tag):
    plan = tuple((axes, scatter) for axes, src, scatter in routes)
    srcs = [src for axes, src, scatter in routes]
    shapes = [
        jax.ShapeDtypeStruct(src.shape if scatter else (group_size(axes),) + src.shape, src.dtype)
        for axes, src, scatter in routes
    ]
    sems = []
    for axes, src, scatter in routes:
        sems += [pltpu.SemaphoreType.DMA((group_size(axes),))] * 2
    vmem = pl.BlockSpec(memory_space=pltpu.VMEM)
    return pl.pallas_call(
        functools.partial(pair_kernel, plan),
        out_shape=tuple(shapes),
        in_specs=[vmem] * len(routes),
        out_specs=tuple([vmem] * len(routes)),
        scratch_shapes=sems,
        compiler_params=pltpu.CompilerParams(collective_id=tag, has_side_effects=True),
    )(*srcs)


def local(images, texts, scale, shift):
    rows, width = images.shape
    image_unit, image_norm = unit_rows(images)
    text_unit, text_norm = unit_rows(texts)
    image_emb = image_unit.astype(jnp.bfloat16)
    text_emb = text_unit.astype(jnp.bfloat16)
    chips = group_size(CHIP_AXES)
    cores = group_size(CORE_AXES)
    image_count = chips * cores
    text_count = group_size(TEXT_AXES)
    total = image_count * text_count * rows
    gathered, seen = exchange(CORE_AXES + CHIP_AXES, image_emb, text_emb, False, 0)
    gathered = gathered.reshape(image_count * rows, width)
    seen = seen.reshape(text_count * rows, width)
    image_ids = jnp.arange(image_count * rows, dtype=jnp.int32)[:, None]
    text_ids = jnp.arange(text_count * rows, dtype=jnp.int32)[None, :]
    mine_i = linear_index(CORE_AXES + CHIP_AXES)
    mine_t = linear_index(TEXT_AXES)
    label = (
        (image_ids // rows == mine_i) & (text_ids // rows == mine_t) & (image_ids % rows == text_ids % rows)
    ).astype(jnp.float32)
    logit = (
        scale
        * lax.dot_general(gathered, seen, (((1,), (1,)), ((), ())), preferred_element_type=jnp.float32)
        + shift
    )
    loss = jnp.sum(jax.nn.softplus(logit * (1.0 - 2.0 * label)), 1, keepdims=True) / total
    coef = ((jax.nn.sigmoid(logit) - label) * scale).astype(jnp.bfloat16)
    image_part = jnp.dot(coef, seen, preferred_element_type=jnp.float32)
    text_part = lax.dot_general(coef, gathered, (((0,), (0,)), ((), ())), preferred_element_type=jnp.float32)
    image_part = jnp.concatenate([image_part, jnp.broadcast_to(loss, (image_count * rows, LOSS_LANES))], 1)
    image_in, text_in = merged_reduce(
        CHIP_AXES, image_part.reshape(cores, chips, rows, width + LOSS_LANES), text_part.reshape(text_count, rows, width), 3
    )
    image_in = jnp.sum(image_in, 0)
    text_sum = text_in
    image_grad = back_rows(image_in[:, :width], image_unit, image_norm)
    text_grad = back_rows(text_sum, text_unit, text_norm)
    return (image_in[:, width], image_grad, text_grad)


def solution(mesh):
    blk, grp = mesh.devices.shape
    fine = Mesh(mesh.devices.reshape(blk // 2, 2, grp // 16, 8, 2), ROWS_AXES)
    in_specs = (P(ROWS_AXES, None), P(ROWS_AXES, None), P(), P())
    out_specs = (P(ROWS_AXES), P(ROWS_AXES, None), P(ROWS_AXES, None))
    return jax.shard_map(local, mesh=fine, in_specs=in_specs, out_specs=out_specs, check_vma=False)
```

```python
import functools

import jax
import jax.numpy as jnp
from jax import lax
from jax.experimental import pallas as pl
from jax.experimental.pallas import tpu as pltpu
from jax.sharding import Mesh, PartitionSpec as P

ROWS_AXES = ("x", "zh", "y", "zl", "c")
CHIP_AXES = ("x", "y")
CORE_AXES = ("c",)
TEXT_AXES = ("zh", "zl")
MESH_IDS = pl.DeviceIdType.MESH
LOSS_LANES = 128


def unit_rows(values):
    floats = values.astype(jnp.float32)
    norms = jnp.sqrt(jnp.sum(floats * floats, 1, keepdims=True) + 1e-06)
    return (floats / norms, norms)


def back_rows(grads, units, norms):
    return (grads - units * jnp.sum(units * grads, 1, keepdims=True)) / norms


def linear_index(axes):
    index = 0
    for name in axes:
        index = index * lax.axis_size(name) + lax.axis_index(name)
    return index


def group_size(axes):
    size = 1
    for name in axes:
        size *= lax.axis_size(name)
    return size


def member(axes, k):
    coords = {}
    for name in reversed(axes):
        size = lax.axis_size(name)
        coords[name] = k % size
        k = k // size
    return tuple(coords[name] if name in coords else lax.axis_index(name) for name in ROWS_AXES)


def ring_peers():
    count, me = group_size(TEXT_AXES), linear_index(TEXT_AXES)
    return count, me, member(TEXT_AXES, (me + 1) % count), member(TEXT_AXES, (me + count - 1) % count)


def remote(src, dst, send, recv, device):
    return pltpu.make_async_remote_copy(src, dst, send, recv, device_id=device, device_id_type=MESH_IDS)


def greet_all(image_axes, barrier, image_count, image_me, right, left, extra=()):
    def greet(step, carry):
        pl.semaphore_signal(barrier, 1, device_id=member(image_axes, (image_me + step) % image_count),
                            device_id_type=MESH_IDS)
        return carry

    lax.fori_loop(1, image_count, greet, 0)
    for device in (right, left) + tuple(extra):
        pl.semaphore_signal(barrier, 1, device_id=device, device_id_type=MESH_IDS)
    pl.semaphore_wait(barrier, image_count + 1 + len(extra))


def image_direct(image_axes, scatter, src, out, send, recv, count, me):
    def start(step, carry):
        peer = (me + step) % count
        remote(src.at[peer] if scatter else src, out.at[me], send.at[peer], recv.at[me],
               member(image_axes, peer)).start()
        return carry

    lax.fori_loop(1, count, start, 0)
    out[me] = src[me] if scatter else src[...]

    def finish(step, carry):
        peer = (me + step) % count
        copy = remote(src.at[peer] if scatter else src, out.at[peer], send.at[peer], recv.at[peer],
                      member(image_axes, peer))
        copy.wait_send()
        copy.wait_recv()
        return carry

    return finish


def gather_kernel(image_axes, image_src, text_src, image_out, text_out, image_send, image_recv, text_send, text_recv):
    image_count, image_me = group_size(image_axes), linear_index(image_axes)
    count, me, right, left = ring_peers()
    half = count // 2
    reach = half // 2
    near = [(member(TEXT_AXES, (me + d) % count), member(TEXT_AXES, (me + count - d) % count)) for d in range(1, reach + 1)]
    extra = tuple(device for pair in near[1:] for device in pair)
    greet_all(image_axes, pltpu.get_barrier_semaphore(), image_count, image_me, right, left, extra)
    finish = image_direct(image_axes, False, image_src, image_out, image_send, image_recv, image_count, image_me)
    sends = []

    def send(src, origin, device, slot):
        copy = remote(src, text_out.at[origin], text_send.at[slot], text_recv.at[origin], device)
        copy.start()
        sends.append(copy)

    def arrive(origin):
        remote(text_out.at[origin], text_out.at[origin], text_send.at[0], text_recv.at[origin], right).wait_recv()

    for d in range(1, reach + 1):
        send(text_src, me, near[d - 1][0], d - 1)
        send(text_src, me, near[d - 1][1], half + d - 1)
    text_out[me] = text_src[...]
    far_right, far_left = near[reach - 1]
    for d in range(1, reach + 1):
        origin = (me + count - d) % count
        arrive(origin)
        send(text_out.at[origin], origin, far_right, reach + d - 1)
    for d in range(1, reach):
        origin = (me + d) % count
        arrive(origin)
        send(text_out.at[origin], origin, far_left, half + reach + d - 1)
    arrive((me + reach) % count)
    for d in range(reach + 1, half + 1):
        arrive((me + count - d) % count)
    for d in range(reach + 1, half):
        arrive((me + d) % count)
    for copy in sends:
        copy.wait_send()
    lax.fori_loop(1, image_count, finish, 0)


def reduce_kernel(image_axes, image_src, text_src, image_out, text_out, image_send, image_recv, text_send, text_recv,
                  inbox, outbox):
    image_count, image_me = group_size(image_axes), linear_index(image_axes)
    count, me, right, left = ring_peers()
    half = count // 2
    greet_all(image_axes, pltpu.get_barrier_semaphore(), image_count, image_me, right, left)
    finish = image_direct(image_axes, True, image_src, image_out, image_send, image_recv, image_count, image_me)
    sends = [remote(text_src.at[(me + half) % count], inbox.at[0], text_send.at[0], text_recv.at[0], right),
             remote(text_src.at[(me + half + 1) % count], inbox.at[half], text_send.at[half], text_recv.at[half], left)]
    for copy in sends:
        copy.start()
    for step in range(1, half):
        chains = ((step, (me + half - step) % count, right), (half + step, (me + half + 1 + step) % count, left))
        for slot, target, device in chains:
            if slot >= count - 1:
                continue
            remote(inbox.at[slot - 1], inbox.at[slot - 1], text_send.at[slot], text_recv.at[slot - 1], device).wait_recv()
            outbox[slot] = inbox[slot - 1] + text_src[target]
            copy = remote(outbox.at[slot], inbox.at[slot], text_send.at[slot], text_recv.at[slot], device)
            copy.start()
            sends.append(copy)
    last_right, last_left = half - 1, count - 2
    for slot in (last_right, last_left):
        remote(inbox.at[slot], inbox.at[slot], text_send.at[0], text_recv.at[slot], right).wait_recv()
    text_out[...] = text_src[me] + inbox[last_right] + inbox[last_left]
    for copy in sends:
        copy.wait_send()
    lax.fori_loop(1, image_count, finish, 0)


def merged_reduce_kernel(image_axes, image_src, text_src, image_out, text_out, image_send, image_recv, text_send,
                         text_recv, inbox, outbox, halfbox, summed, half_sems):
    image_count, image_me = group_size(image_axes), linear_index(image_axes)
    count, me, right, left = ring_peers()
    right2 = member(TEXT_AXES, (me + 2) % count)
    left2 = member(TEXT_AXES, (me + count - 2) % count)
    core = linear_index(CORE_AXES)
    partner = member(CORE_AXES, 1 - core)
    greet_all(image_axes, pltpu.get_barrier_semaphore(), image_count, image_me, right, left, (right2, left2, partner))
    chains = (
        (0, 4, lambda step: right2, lambda step: 10 - 2 * step),
        (4, 4, lambda step: right2 if step < 4 else right, lambda step: 9 - 2 * step),
        (8, 3, lambda step: left2, lambda step: 2 * step - 8),
        (11, 4, lambda step: left2 if step < 4 else left, lambda step: 2 * step - 9),
    )
    sends = []

    def step_sends(step):
        for base, steps, device, offset in chains:
            if step > steps:
                continue
            slot = base + step - 1
            target = (me + count + offset(step)) % count
            if step == 1:
                source = text_src.at[target]
            else:
                remote(inbox.at[slot - 1], inbox.at[slot - 1], text_send.at[slot], text_recv.at[slot - 1],
                       right).wait_recv()
                outbox[slot] = inbox[slot - 1] + text_src[target]
                source = outbox.at[slot]
            copy = remote(source, inbox.at[slot], text_send.at[slot], text_recv.at[slot], device(step))
            copy.start()
            sends.append(copy)

    swap = remote(image_src.at[1 - core], halfbox, half_sems.at[0], half_sems.at[1], partner)
    swap.start()
    step_sends(1)
    step_sends(2)
    swap.wait_recv()
    summed[...] = image_src[core] + halfbox[...]
    finish = image_direct(image_axes, True, summed, image_out, image_send, image_recv, image_count, image_me)
    for step in range(3, 5):
        step_sends(step)
    finals = (3, 7, 10, 14)
    for slot in finals:
        remote(inbox.at[slot], inbox.at[slot], text_send.at[0], text_recv.at[slot], right).wait_recv()
    text_out[...] = text_src[me] + inbox[finals[0]] + inbox[finals[1]] + inbox[finals[2]] + inbox[finals[3]]
    for copy in sends:
        copy.wait_send()
    swap.wait_send()
    lax.fori_loop(1, image_count, finish, 0)


def merged_reduce(image_axes, image_src, text_src, tag):
    image_count, text_count = group_size(image_axes), group_size(TEXT_AXES)
    image_shape = image_src.shape[1:]
    block = text_src.shape[1:]
    vmem = pl.BlockSpec(memory_space=pltpu.VMEM)
    scratch = [
        pltpu.SemaphoreType.DMA((image_count,)),
        pltpu.SemaphoreType.DMA((image_count,)),
        pltpu.SemaphoreType.DMA((text_count,)),
        pltpu.SemaphoreType.DMA((text_count,)),
        pltpu.VMEM((text_count,) + block, text_src.dtype),
        pltpu.VMEM((text_count,) + block, text_src.dtype),
        pltpu.VMEM(image_shape, image_src.dtype),
        pltpu.VMEM(image_shape, image_src.dtype),
        pltpu.SemaphoreType.DMA((2,)),
    ]
    return pl.pallas_call(
        functools.partial(merged_reduce_kernel, image_axes),
        out_shape=(jax.ShapeDtypeStruct(image_shape, image_src.dtype), jax.ShapeDtypeStruct(block, text_src.dtype)),
        in_specs=[vmem, vmem],
        out_specs=(vmem, vmem),
        scratch_shapes=scratch,
        compiler_params=pltpu.CompilerParams(collective_id=tag, has_side_effects=True),
    )(image_src, text_src)


def exchange(image_axes, image_src, text_src, scatter, tag):
    image_count, text_count = group_size(image_axes), group_size(TEXT_AXES)
    image_shape = image_src.shape if scatter else (image_count,) + image_src.shape
    text_shape = text_src.shape[1:] if scatter else (text_count,) + text_src.shape
    block = text_src.shape[1:] if scatter else text_src.shape
    vmem = pl.BlockSpec(memory_space=pltpu.VMEM)
    scratch = [
        pltpu.SemaphoreType.DMA((image_count,)),
        pltpu.SemaphoreType.DMA((image_count,)),
        pltpu.SemaphoreType.DMA((text_count,)),
        pltpu.SemaphoreType.DMA((text_count,)),
    ]
    if scatter:
        scratch += [pltpu.VMEM((text_count,) + block, text_src.dtype)] * 2
    return pl.pallas_call(
        functools.partial(reduce_kernel if scatter else gather_kernel, image_axes),
        out_shape=(jax.ShapeDtypeStruct(image_shape, image_src.dtype), jax.ShapeDtypeStruct(text_shape, text_src.dtype)),
        in_specs=[vmem, vmem],
        out_specs=(vmem, vmem),
        scratch_shapes=scratch,
        compiler_params=pltpu.CompilerParams(collective_id=tag, has_side_effects=True),
    )(image_src, text_src)


def pair_kernel(plan, *refs):
    count_groups = len(plan)
    srcs, outs = refs[:count_groups], refs[count_groups:2 * count_groups]
    sems = refs[2 * count_groups:]
    groups = [
        (axes, scatter, srcs[g], outs[g], sems[2 * g], sems[2 * g + 1]) for g, (axes, scatter) in enumerate(plan)
    ]
    barrier = pltpu.get_barrier_semaphore()
    peers = 0
    for axes, scatter, src, out, send, recv in groups:
        count, me = group_size(axes), linear_index(axes)
        peers += count - 1

        def greet(step, carry, axes=axes, count=count, me=me):
            pl.semaphore_signal(barrier, 1, device_id=member(axes, (me + step) % count), device_id_type=MESH_IDS)
            return carry

        lax.fori_loop(1, count, greet, 0)
    pl.semaphore_wait(barrier, peers)

    for axes, scatter, src, out, send, recv in groups:
        count, me = group_size(axes), linear_index(axes)

        def start(step, carry, axes=axes, scatter=scatter, count=count, me=me, src=src, out=out, send=send, recv=recv):
            peer = (me + step) % count
            pltpu.make_async_remote_copy(
                src.at[peer] if scatter else src, out.at[me], send.at[peer], recv.at[me],
                device_id=member(axes, peer), device_id_type=MESH_IDS,
            ).start()
            return carry

        lax.fori_loop(1, count, start, 0)

    for axes, scatter, src, out, send, recv in groups:
        count, me = group_size(axes), linear_index(axes)
        out[me] = src[me] if scatter else src[...]

    for axes, scatter, src, out, send, recv in groups:
        count, me = group_size(axes), linear_index(axes)

        def finish(step, carry, axes=axes, scatter=scatter, count=count, me=me, src=src, out=out, send=send, recv=recv):
            peer = (me + step) % count
            copy = pltpu.make_async_remote_copy(
                src.at[peer] if scatter else src, out.at[peer], send.at[peer], recv.at[peer],
                device_id=member(axes, peer), device_id_type=MESH_IDS,
            )
            copy.wait_send()
            copy.wait_recv()
            return carry

        lax.fori_loop(1, count, finish, 0)


def pair_exchange(routes, tag):
    plan = tuple((axes, scatter) for axes, src, scatter in routes)
    srcs = [src for axes, src, scatter in routes]
    shapes = [
        jax.ShapeDtypeStruct(src.shape if scatter else (group_size(axes),) + src.shape, src.dtype)
        for axes, src, scatter in routes
    ]
    sems = []
    for axes, src, scatter in routes:
        sems += [pltpu.SemaphoreType.DMA((group_size(axes),))] * 2
    vmem = pl.BlockSpec(memory_space=pltpu.VMEM)
    return pl.pallas_call(
        functools.partial(pair_kernel, plan),
        out_shape=tuple(shapes),
        in_specs=[vmem] * len(routes),
        out_specs=tuple([vmem] * len(routes)),
        scratch_shapes=sems,
        compiler_params=pltpu.CompilerParams(collective_id=tag, has_side_effects=True),
    )(*srcs)


def local(images, texts, scale, shift):
    rows, width = images.shape
    image_unit, image_norm = unit_rows(images)
    text_unit, text_norm = unit_rows(texts)
    image_emb = image_unit.astype(jnp.bfloat16)
    text_emb = text_unit.astype(jnp.bfloat16)
    chips = group_size(CHIP_AXES)
    cores = group_size(CORE_AXES)
    image_count = chips * cores
    text_count = group_size(TEXT_AXES)
    total = image_count * text_count * rows
    gathered, seen = exchange(CORE_AXES + CHIP_AXES, image_emb, text_emb, False, 0)
    gathered = gathered.reshape(image_count * rows, width)
    seen = seen.reshape(text_count * rows, width)
    image_ids = jnp.arange(image_count * rows, dtype=jnp.int32)[:, None]
    text_ids = jnp.arange(text_count * rows, dtype=jnp.int32)[None, :]
    mine_i = linear_index(CORE_AXES + CHIP_AXES)
    mine_t = linear_index(TEXT_AXES)
    label = (
        (image_ids // rows == mine_i) & (text_ids // rows == mine_t) & (image_ids % rows == text_ids % rows)
    ).astype(jnp.float32)
    logit = (
        scale
        * lax.dot_general(gathered, seen, (((1,), (1,)), ((), ())), preferred_element_type=jnp.float32)
        + shift
    )
    loss = jnp.sum(jax.nn.softplus(logit * (1.0 - 2.0 * label)), 1, keepdims=True) / total
    coef = ((jax.nn.sigmoid(logit) - label) * scale).astype(jnp.bfloat16)
    image_part = jnp.dot(coef, seen, preferred_element_type=jnp.float32)
    text_part = lax.dot_general(coef, gathered, (((0,), (0,)), ((), ())), preferred_element_type=jnp.float32)
    image_part = jnp.concatenate([image_part, jnp.broadcast_to(loss, (image_count * rows, LOSS_LANES))], 1)
    image_in, text_in = merged_reduce(
        CHIP_AXES, image_part.reshape(cores, chips, rows, width + LOSS_LANES), text_part.reshape(text_count, rows, width), 3
    )
    image_in = jnp.sum(image_in, 0)
    text_sum = text_in
    image_grad = back_rows(image_in[:, :width], image_unit, image_norm)
    text_grad = back_rows(text_sum, text_unit, text_norm)
    return (image_in[:, width], image_grad, text_grad)


def solution(mesh):
    blk, grp = mesh.devices.shape
    fine = Mesh(mesh.devices.reshape(blk // 2, 2, grp // 16, 8, 2), ROWS_AXES)
    in_specs = (P(ROWS_AXES, None), P(ROWS_AXES, None), P(), P())
    out_specs = (P(ROWS_AXES), P(ROWS_AXES, None), P(ROWS_AXES, None))
    return jax.shard_map(local, mesh=fine, in_specs=in_specs, out_specs=out_specs, check_vma=False)
```

```python
import functools

import jax
import jax.numpy as jnp
from jax import lax
from jax.experimental import pallas as pl
from jax.experimental.pallas import tpu as pltpu
from jax.sharding import Mesh, PartitionSpec as P

ROWS_AXES = ("x", "zh", "y", "zl", "c")
CHIP_AXES = ("x", "y")
CORE_AXES = ("c",)
TEXT_AXES = ("zh", "zl")
MESH_IDS = pl.DeviceIdType.MESH
LOSS_LANES = 128


def unit_rows(values):
    floats = values.astype(jnp.float32)
    norms = jnp.sqrt(jnp.sum(floats * floats, 1, keepdims=True) + 1e-06)
    return (floats / norms, norms)


def back_rows(grads, units, norms):
    return (grads - units * jnp.sum(units * grads, 1, keepdims=True)) / norms


def linear_index(axes):
    index = 0
    for name in axes:
        index = index * lax.axis_size(name) + lax.axis_index(name)
    return index


def group_size(axes):
    size = 1
    for name in axes:
        size *= lax.axis_size(name)
    return size


def member(axes, k):
    coords = {}
    for name in reversed(axes):
        size = lax.axis_size(name)
        coords[name] = k % size
        k = k // size
    return tuple(coords[name] if name in coords else lax.axis_index(name) for name in ROWS_AXES)


def ring_peers():
    count, me = group_size(TEXT_AXES), linear_index(TEXT_AXES)
    return count, me, member(TEXT_AXES, (me + 1) % count), member(TEXT_AXES, (me + count - 1) % count)


def remote(src, dst, send, recv, device):
    return pltpu.make_async_remote_copy(src, dst, send, recv, device_id=device, device_id_type=MESH_IDS)


def greet_all(image_axes, barrier, image_count, image_me, right, left, extra=()):
    def greet(step, carry):
        pl.semaphore_signal(barrier, 1, device_id=member(image_axes, (image_me + step) % image_count),
                            device_id_type=MESH_IDS)
        return carry

    lax.fori_loop(1, image_count, greet, 0)
    for device in (right, left) + tuple(extra):
        pl.semaphore_signal(barrier, 1, device_id=device, device_id_type=MESH_IDS)
    pl.semaphore_wait(barrier, image_count + 1 + len(extra))


def image_direct(image_axes, scatter, src, out, send, recv, count, me):
    def start(step, carry):
        peer = (me + step) % count
        remote(src.at[peer] if scatter else src, out.at[me], send.at[peer], recv.at[me],
               member(image_axes, peer)).start()
        return carry

    lax.fori_loop(1, count, start, 0)
    out[me] = src[me] if scatter else src[...]

    def finish(step, carry):
        peer = (me + step) % count
        copy = remote(src.at[peer] if scatter else src, out.at[peer], send.at[peer], recv.at[peer],
                      member(image_axes, peer))
        copy.wait_send()
        copy.wait_recv()
        return carry

    return finish


def gather_kernel(image_axes, image_src, text_src, image_out, text_out, image_send, image_recv, text_send, text_recv):
    image_count, image_me = group_size(image_axes), linear_index(image_axes)
    count, me, right, left = ring_peers()
    right2 = member(TEXT_AXES, (me + 2) % count)
    left2 = member(TEXT_AXES, (me + count - 2) % count)
    greet_all(image_axes, pltpu.get_barrier_semaphore(), image_count, image_me, right, left, (right2, left2))
    finish = image_direct(image_axes, False, image_src, image_out, image_send, image_recv, image_count, image_me)
    sends = []

    def send(src, origin, device, slot):
        copy = remote(src, text_out.at[origin], text_send.at[slot], text_recv.at[origin], device)
        copy.start()
        sends.append(copy)

    def arrive(origin):
        remote(text_out.at[origin], text_out.at[origin], text_send.at[0], text_recv.at[origin], right).wait_recv()

    half = count // 2
    for slot, device in ((0, right), (1, right2), (half, left), (half + 1, left2)):
        send(text_src, me, device, slot)
    text_out[me] = text_src[...]
    slot_right, slot_left = 2, half + 2
    for step in range(2, half // 2 + 1):
        for distance in (2 * step - 3, 2 * step - 2):
            origin = (me + count - distance) % count
            arrive(origin)
            send(text_out.at[origin], origin, right2, slot_right)
            slot_right += 1
        for distance in (2 * step - 3, 2 * step - 2):
            if distance > half - 3:
                continue
            origin = (me + distance) % count
            arrive(origin)
            send(text_out.at[origin], origin, left2, slot_left)
            slot_left += 1
    for distance in (half - 1, half):
        arrive((me + count - distance) % count)
    for distance in (half - 2, half - 1):
        arrive((me + distance) % count)
    for copy in sends:
        copy.wait_send()
    lax.fori_loop(1, image_count, finish, 0)


def reduce_kernel(image_axes, image_src, text_src, image_out, text_out, image_send, image_recv, text_send, text_recv,
                  inbox, outbox):
    image_count, image_me = group_size(image_axes), linear_index(image_axes)
    count, me, right, left = ring_peers()
    half = count // 2
    greet_all(image_axes, pltpu.get_barrier_semaphore(), image_count, image_me, right, left)
    finish = image_direct(image_axes, True, image_src, image_out, image_send, image_recv, image_count, image_me)
    sends = [remote(text_src.at[(me + half) % count], inbox.at[0], text_send.at[0], text_recv.at[0], right),
             remote(text_src.at[(me + half + 1) % count], inbox.at[half], text_send.at[half], text_recv.at[half], left)]
    for copy in sends:
        copy.start()
    for step in range(1, half):
        chains = ((step, (me + half - step) % count, right), (half + step, (me + half + 1 + step) % count, left))
        for slot, target, device in chains:
            if slot >= count - 1:
                continue
            remote(inbox.at[slot - 1], inbox.at[slot - 1], text_send.at[slot], text_recv.at[slot - 1], device).wait_recv()
            outbox[slot] = inbox[slot - 1] + text_src[target]
            copy = remote(outbox.at[slot], inbox.at[slot], text_send.at[slot], text_recv.at[slot], device)
            copy.start()
            sends.append(copy)
    last_right, last_left = half - 1, count - 2
    for slot in (last_right, last_left):
        remote(inbox.at[slot], inbox.at[slot], text_send.at[0], text_recv.at[slot], right).wait_recv()
    text_out[...] = text_src[me] + inbox[last_right] + inbox[last_left]
    for copy in sends:
        copy.wait_send()
    lax.fori_loop(1, image_count, finish, 0)


def merged_reduce_kernel(image_axes, image_src, text_src, image_unit, image_norm, text_unit, text_norm, loss_out,
                         image_grad, text_grad, image_send, image_recv, text_send, text_recv, inbox, outbox, halfbox,
                         summed, half_sems, image_out):
    image_count, image_me = group_size(image_axes), linear_index(image_axes)
    count, me, right, left = ring_peers()
    right2 = member(TEXT_AXES, (me + 2) % count)
    left2 = member(TEXT_AXES, (me + count - 2) % count)
    core = linear_index(CORE_AXES)
    partner = member(CORE_AXES, 1 - core)
    greet_all(image_axes, pltpu.get_barrier_semaphore(), image_count, image_me, right, left, (right2, left2, partner))
    chains = (
        (0, 4, lambda step: right2, lambda step: 10 - 2 * step),
        (4, 4, lambda step: right2 if step < 4 else right, lambda step: 9 - 2 * step),
        (8, 3, lambda step: left2, lambda step: 2 * step - 8),
        (11, 4, lambda step: left2 if step < 4 else left, lambda step: 2 * step - 9),
    )
    sends = []

    def step_sends(step):
        for base, steps, device, offset in chains:
            if step > steps:
                continue
            slot = base + step - 1
            target = (me + count + offset(step)) % count
            if step == 1:
                source = text_src.at[target]
            else:
                remote(inbox.at[slot - 1], inbox.at[slot - 1], text_send.at[slot], text_recv.at[slot - 1],
                       right).wait_recv()
                outbox[slot] = inbox[slot - 1] + text_src[target]
                source = outbox.at[slot]
            copy = remote(source, inbox.at[slot], text_send.at[slot], text_recv.at[slot], device(step))
            copy.start()
            sends.append(copy)

    swap = remote(image_src.at[1 - core], halfbox, half_sems.at[0], half_sems.at[1], partner)
    swap.start()
    step_sends(1)
    step_sends(2)
    swap.wait_recv()
    summed[...] = image_src[core] + halfbox[...]
    finish = image_direct(image_axes, True, summed, image_out, image_send, image_recv, image_count, image_me)
    for step in range(3, 5):
        step_sends(step)
    finals = (3, 7, 10, 14)
    for slot in finals:
        remote(inbox.at[slot], inbox.at[slot], text_send.at[0], text_recv.at[slot], right).wait_recv()
    text_sum = text_src[me] + inbox[finals[0]] + inbox[finals[1]] + inbox[finals[2]] + inbox[finals[3]]
    text_grad[...] = back_rows(text_sum, text_unit[...], text_norm[...])
    for copy in sends:
        copy.wait_send()
    swap.wait_send()
    lax.fori_loop(1, image_count, finish, 0)
    width = image_grad.shape[1]
    image_sum = jnp.sum(image_out[...], 0)
    image_grad[...] = back_rows(image_sum[:, :width], image_unit[...], image_norm[...])
    loss_out[...] = image_sum[:, width:]


def merged_reduce(image_axes, image_src, text_src, units, tag):
    image_count, text_count = group_size(image_axes), group_size(TEXT_AXES)
    image_shape = image_src.shape[1:]
    block = text_src.shape[1:]
    rows, lanes = image_shape[1:]
    vmem = pl.BlockSpec(memory_space=pltpu.VMEM)
    scratch = [
        pltpu.SemaphoreType.DMA((image_count,)),
        pltpu.SemaphoreType.DMA((image_count,)),
        pltpu.SemaphoreType.DMA((text_count,)),
        pltpu.SemaphoreType.DMA((text_count,)),
        pltpu.VMEM((text_count,) + block, text_src.dtype),
        pltpu.VMEM((text_count,) + block, text_src.dtype),
        pltpu.VMEM(image_shape, image_src.dtype),
        pltpu.VMEM(image_shape, image_src.dtype),
        pltpu.SemaphoreType.DMA((2,)),
        pltpu.VMEM(image_shape, image_src.dtype),
    ]
    return pl.pallas_call(
        functools.partial(merged_reduce_kernel, image_axes),
        out_shape=(
            jax.ShapeDtypeStruct((rows, lanes - block[1]), jnp.float32),
            jax.ShapeDtypeStruct(block, jnp.float32),
            jax.ShapeDtypeStruct(block, jnp.float32),
        ),
        in_specs=[vmem] * 6,
        out_specs=(vmem, vmem, vmem),
        scratch_shapes=scratch,
        compiler_params=pltpu.CompilerParams(collective_id=tag, has_side_effects=True),
    )(image_src, text_src, *units)


def exchange(image_axes, image_src, text_src, scatter, tag):
    image_count, text_count = group_size(image_axes), group_size(TEXT_AXES)
    image_shape = image_src.shape if scatter else (image_count,) + image_src.shape
    text_shape = text_src.shape[1:] if scatter else (text_count,) + text_src.shape
    block = text_src.shape[1:] if scatter else text_src.shape
    vmem = pl.BlockSpec(memory_space=pltpu.VMEM)
    scratch = [
        pltpu.SemaphoreType.DMA((image_count,)),
        pltpu.SemaphoreType.DMA((image_count,)),
        pltpu.SemaphoreType.DMA((text_count,)),
        pltpu.SemaphoreType.DMA((text_count,)),
    ]
    if scatter:
        scratch += [pltpu.VMEM((text_count,) + block, text_src.dtype)] * 2
    return pl.pallas_call(
        functools.partial(reduce_kernel if scatter else gather_kernel, image_axes),
        out_shape=(jax.ShapeDtypeStruct(image_shape, image_src.dtype), jax.ShapeDtypeStruct(text_shape, text_src.dtype)),
        in_specs=[vmem, vmem],
        out_specs=(vmem, vmem),
        scratch_shapes=scratch,
        compiler_params=pltpu.CompilerParams(collective_id=tag, has_side_effects=True),
    )(image_src, text_src)


def pair_kernel(plan, *refs):
    count_groups = len(plan)
    srcs, outs = refs[:count_groups], refs[count_groups:2 * count_groups]
    sems = refs[2 * count_groups:]
    groups = [
        (axes, scatter, srcs[g], outs[g], sems[2 * g], sems[2 * g + 1]) for g, (axes, scatter) in enumerate(plan)
    ]
    barrier = pltpu.get_barrier_semaphore()
    peers = 0
    for axes, scatter, src, out, send, recv in groups:
        count, me = group_size(axes), linear_index(axes)
        peers += count - 1

        def greet(step, carry, axes=axes, count=count, me=me):
            pl.semaphore_signal(barrier, 1, device_id=member(axes, (me + step) % count), device_id_type=MESH_IDS)
            return carry

        lax.fori_loop(1, count, greet, 0)
    pl.semaphore_wait(barrier, peers)

    for axes, scatter, src, out, send, recv in groups:
        count, me = group_size(axes), linear_index(axes)

        def start(step, carry, axes=axes, scatter=scatter, count=count, me=me, src=src, out=out, send=send, recv=recv):
            peer = (me + step) % count
            pltpu.make_async_remote_copy(
                src.at[peer] if scatter else src, out.at[me], send.at[peer], recv.at[me],
                device_id=member(axes, peer), device_id_type=MESH_IDS,
            ).start()
            return carry

        lax.fori_loop(1, count, start, 0)

    for axes, scatter, src, out, send, recv in groups:
        count, me = group_size(axes), linear_index(axes)
        out[me] = src[me] if scatter else src[...]

    for axes, scatter, src, out, send, recv in groups:
        count, me = group_size(axes), linear_index(axes)

        def finish(step, carry, axes=axes, scatter=scatter, count=count, me=me, src=src, out=out, send=send, recv=recv):
            peer = (me + step) % count
            copy = pltpu.make_async_remote_copy(
                src.at[peer] if scatter else src, out.at[peer], send.at[peer], recv.at[peer],
                device_id=member(axes, peer), device_id_type=MESH_IDS,
            )
            copy.wait_send()
            copy.wait_recv()
            return carry

        lax.fori_loop(1, count, finish, 0)


def pair_exchange(routes, tag):
    plan = tuple((axes, scatter) for axes, src, scatter in routes)
    srcs = [src for axes, src, scatter in routes]
    shapes = [
        jax.ShapeDtypeStruct(src.shape if scatter else (group_size(axes),) + src.shape, src.dtype)
        for axes, src, scatter in routes
    ]
    sems = []
    for axes, src, scatter in routes:
        sems += [pltpu.SemaphoreType.DMA((group_size(axes),))] * 2
    vmem = pl.BlockSpec(memory_space=pltpu.VMEM)
    return pl.pallas_call(
        functools.partial(pair_kernel, plan),
        out_shape=tuple(shapes),
        in_specs=[vmem] * len(routes),
        out_specs=tuple([vmem] * len(routes)),
        scratch_shapes=sems,
        compiler_params=pltpu.CompilerParams(collective_id=tag, has_side_effects=True),
    )(*srcs)


def local(images, texts, scale, shift):
    rows, width = images.shape
    image_unit, image_norm = unit_rows(images)
    text_unit, text_norm = unit_rows(texts)
    image_emb = image_unit.astype(jnp.bfloat16)
    text_emb = text_unit.astype(jnp.bfloat16)
    chips = group_size(CHIP_AXES)
    cores = group_size(CORE_AXES)
    image_count = chips * cores
    text_count = group_size(TEXT_AXES)
    total = image_count * text_count * rows
    gathered, seen = exchange(CORE_AXES + CHIP_AXES, image_emb, text_emb, False, 0)
    gathered = gathered.reshape(image_count * rows, width)
    seen = seen.reshape(text_count * rows, width)
    image_ids = jnp.arange(image_count * rows, dtype=jnp.int32)[:, None]
    text_ids = jnp.arange(text_count * rows, dtype=jnp.int32)[None, :]
    mine_i = linear_index(CORE_AXES + CHIP_AXES)
    mine_t = linear_index(TEXT_AXES)
    label = (
        (image_ids // rows == mine_i) & (text_ids // rows == mine_t) & (image_ids % rows == text_ids % rows)
    ).astype(jnp.float32)
    logit = (
        scale
        * lax.dot_general(gathered, seen, (((1,), (1,)), ((), ())), preferred_element_type=jnp.float32)
        + shift
    )
    loss = jnp.sum(jax.nn.softplus(logit * (1.0 - 2.0 * label)), 1, keepdims=True) / total
    coef = ((jax.nn.sigmoid(logit) - label) * scale).astype(jnp.bfloat16)
    image_part = jnp.dot(coef, seen, preferred_element_type=jnp.float32)
    text_part = lax.dot_general(coef, gathered, (((0,), (0,)), ((), ())), preferred_element_type=jnp.float32)
    image_part = jnp.concatenate([image_part, jnp.broadcast_to(loss, (image_count * rows, LOSS_LANES))], 1)
    loss_lanes, image_grad, text_grad = merged_reduce(
        CHIP_AXES, image_part.reshape(cores, chips, rows, width + LOSS_LANES), text_part.reshape(text_count, rows, width),
        (image_unit, image_norm, text_unit, text_norm), 3
    )
    return (loss_lanes[:, 0], image_grad, text_grad)


def solution(mesh):
    blk, grp = mesh.devices.shape
    fine = Mesh(mesh.devices.reshape(blk // 2, 2, grp // 16, 8, 2), ROWS_AXES)
    in_specs = (P(ROWS_AXES, None), P(ROWS_AXES, None), P(), P())
    out_specs = (P(ROWS_AXES), P(ROWS_AXES, None), P(ROWS_AXES, None))
    return jax.shard_map(local, mesh=fine, in_specs=in_specs, out_specs=out_specs, check_vma=False)
```

```python
import functools

import jax
import jax.numpy as jnp
from jax import lax
from jax.experimental import pallas as pl
from jax.experimental.pallas import tpu as pltpu
from jax.sharding import Mesh, PartitionSpec as P

ROWS_AXES = ("x", "zh", "y", "zl", "c")
CHIP_AXES = ("x", "y")
CORE_AXES = ("c",)
TEXT_AXES = ("zh", "zl")
MESH_IDS = pl.DeviceIdType.MESH
LOSS_LANES = 128


def unit_rows(values):
    floats = values.astype(jnp.float32)
    norms = jnp.sqrt(jnp.sum(floats * floats, 1, keepdims=True) + 1e-06)
    return (floats / norms, norms)


def back_rows(grads, units, norms):
    return (grads - units * jnp.sum(units * grads, 1, keepdims=True)) / norms


def linear_index(axes):
    index = 0
    for name in axes:
        index = index * lax.axis_size(name) + lax.axis_index(name)
    return index


def group_size(axes):
    size = 1
    for name in axes:
        size *= lax.axis_size(name)
    return size


def member(axes, k):
    coords = {}
    for name in reversed(axes):
        size = lax.axis_size(name)
        coords[name] = k % size
        k = k // size
    return tuple(coords[name] if name in coords else lax.axis_index(name) for name in ROWS_AXES)


def ring_peers():
    count, me = group_size(TEXT_AXES), linear_index(TEXT_AXES)
    return count, me, member(TEXT_AXES, (me + 1) % count), member(TEXT_AXES, (me + count - 1) % count)


def remote(src, dst, send, recv, device):
    return pltpu.make_async_remote_copy(src, dst, send, recv, device_id=device, device_id_type=MESH_IDS)


def greet_all(image_axes, barrier, image_count, image_me, right, left, extra=()):
    def greet(step, carry):
        pl.semaphore_signal(barrier, 1, device_id=member(image_axes, (image_me + step) % image_count),
                            device_id_type=MESH_IDS)
        return carry

    lax.fori_loop(1, image_count, greet, 0)
    for device in (right, left) + tuple(extra):
        pl.semaphore_signal(barrier, 1, device_id=device, device_id_type=MESH_IDS)
    pl.semaphore_wait(barrier, image_count + 1 + len(extra))


def image_direct(image_axes, scatter, src, out, send, recv, count, me):
    def start(step, carry):
        peer = (me + step) % count
        remote(src.at[peer] if scatter else src, out.at[me], send.at[peer], recv.at[me],
               member(image_axes, peer)).start()
        return carry

    lax.fori_loop(1, count, start, 0)
    out[me] = src[me] if scatter else src[...]

    def finish(step, carry):
        peer = (me + step) % count
        copy = remote(src.at[peer] if scatter else src, out.at[peer], send.at[peer], recv.at[peer],
                      member(image_axes, peer))
        copy.wait_send()
        copy.wait_recv()
        return carry

    return finish


def gather_kernel(image_axes, image_src, text_src, image_out, text_out, image_send, image_recv, text_send, text_recv):
    image_count, image_me = group_size(image_axes), linear_index(image_axes)
    count, me, right, left = ring_peers()
    right2 = member(TEXT_AXES, (me + 2) % count)
    left2 = member(TEXT_AXES, (me + count - 2) % count)
    greet_all(image_axes, pltpu.get_barrier_semaphore(), image_count, image_me, right, left, (right2, left2))
    finish = image_direct(image_axes, False, image_src, image_out, image_send, image_recv, image_count, image_me)
    sends = []

    def send(src, origin, device, slot):
        copy = remote(src, text_out.at[origin], text_send.at[slot], text_recv.at[origin], device)
        copy.start()
        sends.append(copy)

    def arrive(origin):
        remote(text_out.at[origin], text_out.at[origin], text_send.at[0], text_recv.at[origin], right).wait_recv()

    half = count // 2
    for slot, device in ((0, right), (1, right2), (half, left), (half + 1, left2)):
        send(text_src, me, device, slot)
    text_out[me] = text_src[...]
    slot_right, slot_left = 2, half + 2
    for step in range(2, half // 2 + 1):
        for distance in (2 * step - 3, 2 * step - 2):
            origin = (me + count - distance) % count
            arrive(origin)
            send(text_out.at[origin], origin, right2, slot_right)
            slot_right += 1
        for distance in (2 * step - 3, 2 * step - 2):
            if distance > half - 3:
                continue
            origin = (me + distance) % count
            arrive(origin)
            send(text_out.at[origin], origin, left2, slot_left)
            slot_left += 1
    for distance in (half - 1, half):
        arrive((me + count - distance) % count)
    for distance in (half - 2, half - 1):
        arrive((me + distance) % count)
    for copy in sends:
        copy.wait_send()
    lax.fori_loop(1, image_count, finish, 0)


def reduce_kernel(image_axes, image_src, text_src, image_out, text_out, image_send, image_recv, text_send, text_recv,
                  inbox, outbox):
    image_count, image_me = group_size(image_axes), linear_index(image_axes)
    count, me, right, left = ring_peers()
    half = count // 2
    greet_all(image_axes, pltpu.get_barrier_semaphore(), image_count, image_me, right, left)
    finish = image_direct(image_axes, True, image_src, image_out, image_send, image_recv, image_count, image_me)
    sends = [remote(text_src.at[(me + half) % count], inbox.at[0], text_send.at[0], text_recv.at[0], right),
             remote(text_src.at[(me + half + 1) % count], inbox.at[half], text_send.at[half], text_recv.at[half], left)]
    for copy in sends:
        copy.start()
    for step in range(1, half):
        chains = ((step, (me + half - step) % count, right), (half + step, (me + half + 1 + step) % count, left))
        for slot, target, device in chains:
            if slot >= count - 1:
                continue
            remote(inbox.at[slot - 1], inbox.at[slot - 1], text_send.at[slot], text_recv.at[slot - 1], device).wait_recv()
            outbox[slot] = inbox[slot - 1] + text_src[target]
            copy = remote(outbox.at[slot], inbox.at[slot], text_send.at[slot], text_recv.at[slot], device)
            copy.start()
            sends.append(copy)
    last_right, last_left = half - 1, count - 2
    for slot in (last_right, last_left):
        remote(inbox.at[slot], inbox.at[slot], text_send.at[0], text_recv.at[slot], right).wait_recv()
    text_out[...] = text_src[me] + inbox[last_right] + inbox[last_left]
    for copy in sends:
        copy.wait_send()
    lax.fori_loop(1, image_count, finish, 0)


def merged_reduce_kernel(image_axes, image_src, text_src, image_unit, text_unit, loss_out,
                         image_grad, text_grad, image_send, image_recv, text_send, text_recv, inbox, outbox, halfbox,
                         summed, half_sems, image_out):
    image_count, image_me = group_size(image_axes), linear_index(image_axes)
    count, me, right, left = ring_peers()
    right2 = member(TEXT_AXES, (me + 2) % count)
    left2 = member(TEXT_AXES, (me + count - 2) % count)
    core = linear_index(CORE_AXES)
    partner = member(CORE_AXES, 1 - core)
    greet_all(image_axes, pltpu.get_barrier_semaphore(), image_count, image_me, right, left, (right2, left2, partner))
    chains = (
        (0, 4, lambda step: right2, lambda step: 10 - 2 * step),
        (4, 4, lambda step: right2 if step < 4 else right, lambda step: 9 - 2 * step),
        (8, 3, lambda step: left2, lambda step: 2 * step - 8),
        (11, 4, lambda step: left2 if step < 4 else left, lambda step: 2 * step - 9),
    )
    sends = []

    def step_sends(step):
        for base, steps, device, offset in chains:
            if step > steps:
                continue
            slot = base + step - 1
            target = (me + count + offset(step)) % count
            if step == 1:
                source = text_src.at[target]
            else:
                remote(inbox.at[slot - 1], inbox.at[slot - 1], text_send.at[slot], text_recv.at[slot - 1],
                       right).wait_recv()
                outbox[slot] = inbox[slot - 1] + text_src[target]
                source = outbox.at[slot]
            copy = remote(source, inbox.at[slot], text_send.at[slot], text_recv.at[slot], device(step))
            copy.start()
            sends.append(copy)

    swap = remote(image_src.at[1 - core], halfbox, half_sems.at[0], half_sems.at[1], partner)
    swap.start()
    step_sends(1)
    step_sends(2)
    swap.wait_recv()
    summed[...] = image_src[core] + halfbox[...]
    finish = image_direct(image_axes, True, summed, image_out, image_send, image_recv, image_count, image_me)
    for step in range(3, 5):
        step_sends(step)
    finals = (3, 7, 10, 14)
    for slot in finals:
        remote(inbox.at[slot], inbox.at[slot], text_send.at[0], text_recv.at[slot], right).wait_recv()
    text_sum = text_src[me] + inbox[finals[0]] + inbox[finals[1]] + inbox[finals[2]] + inbox[finals[3]]
    text_grad[...] = text_sum - text_unit[...] * jnp.sum(text_unit[...] * text_sum, 1, keepdims=True)
    for copy in sends:
        copy.wait_send()
    swap.wait_send()
    lax.fori_loop(1, image_count, finish, 0)
    width = image_grad.shape[1]
    image_sum = jnp.sum(image_out[...], 0)
    image_part = image_sum[:, :width]
    image_grad[...] = image_part - image_unit[...] * jnp.sum(image_unit[...] * image_part, 1, keepdims=True)
    loss_out[...] = image_sum[:, width:]


def merged_reduce(image_axes, image_src, text_src, units, tag):
    image_count, text_count = group_size(image_axes), group_size(TEXT_AXES)
    image_shape = image_src.shape[1:]
    block = text_src.shape[1:]
    rows, lanes = image_shape[1:]
    vmem = pl.BlockSpec(memory_space=pltpu.VMEM)
    scratch = [
        pltpu.SemaphoreType.DMA((image_count,)),
        pltpu.SemaphoreType.DMA((image_count,)),
        pltpu.SemaphoreType.DMA((text_count,)),
        pltpu.SemaphoreType.DMA((text_count,)),
        pltpu.VMEM((text_count,) + block, text_src.dtype),
        pltpu.VMEM((text_count,) + block, text_src.dtype),
        pltpu.VMEM(image_shape, image_src.dtype),
        pltpu.VMEM(image_shape, image_src.dtype),
        pltpu.SemaphoreType.DMA((2,)),
        pltpu.VMEM(image_shape, image_src.dtype),
    ]
    return pl.pallas_call(
        functools.partial(merged_reduce_kernel, image_axes),
        out_shape=(
            jax.ShapeDtypeStruct((rows, lanes - block[1]), jnp.float32),
            jax.ShapeDtypeStruct(block, jnp.float32),
            jax.ShapeDtypeStruct(block, jnp.float32),
        ),
        in_specs=[vmem] * 4,
        out_specs=(vmem, vmem, vmem),
        scratch_shapes=scratch,
        compiler_params=pltpu.CompilerParams(collective_id=tag, has_side_effects=True),
    )(image_src, text_src, *units)


def exchange(image_axes, image_src, text_src, scatter, tag):
    image_count, text_count = group_size(image_axes), group_size(TEXT_AXES)
    image_shape = image_src.shape if scatter else (image_count,) + image_src.shape
    text_shape = text_src.shape[1:] if scatter else (text_count,) + text_src.shape
    block = text_src.shape[1:] if scatter else text_src.shape
    vmem = pl.BlockSpec(memory_space=pltpu.VMEM)
    scratch = [
        pltpu.SemaphoreType.DMA((image_count,)),
        pltpu.SemaphoreType.DMA((image_count,)),
        pltpu.SemaphoreType.DMA((text_count,)),
        pltpu.SemaphoreType.DMA((text_count,)),
    ]
    if scatter:
        scratch += [pltpu.VMEM((text_count,) + block, text_src.dtype)] * 2
    return pl.pallas_call(
        functools.partial(reduce_kernel if scatter else gather_kernel, image_axes),
        out_shape=(jax.ShapeDtypeStruct(image_shape, image_src.dtype), jax.ShapeDtypeStruct(text_shape, text_src.dtype)),
        in_specs=[vmem, vmem],
        out_specs=(vmem, vmem),
        scratch_shapes=scratch,
        compiler_params=pltpu.CompilerParams(collective_id=tag, has_side_effects=True),
    )(image_src, text_src)


def pair_kernel(plan, *refs):
    count_groups = len(plan)
    srcs, outs = refs[:count_groups], refs[count_groups:2 * count_groups]
    sems = refs[2 * count_groups:]
    groups = [
        (axes, scatter, srcs[g], outs[g], sems[2 * g], sems[2 * g + 1]) for g, (axes, scatter) in enumerate(plan)
    ]
    barrier = pltpu.get_barrier_semaphore()
    peers = 0
    for axes, scatter, src, out, send, recv in groups:
        count, me = group_size(axes), linear_index(axes)
        peers += count - 1

        def greet(step, carry, axes=axes, count=count, me=me):
            pl.semaphore_signal(barrier, 1, device_id=member(axes, (me + step) % count), device_id_type=MESH_IDS)
            return carry

        lax.fori_loop(1, count, greet, 0)
    pl.semaphore_wait(barrier, peers)

    for axes, scatter, src, out, send, recv in groups:
        count, me = group_size(axes), linear_index(axes)

        def start(step, carry, axes=axes, scatter=scatter, count=count, me=me, src=src, out=out, send=send, recv=recv):
            peer = (me + step) % count
            pltpu.make_async_remote_copy(
                src.at[peer] if scatter else src, out.at[me], send.at[peer], recv.at[me],
                device_id=member(axes, peer), device_id_type=MESH_IDS,
            ).start()
            return carry

        lax.fori_loop(1, count, start, 0)

    for axes, scatter, src, out, send, recv in groups:
        count, me = group_size(axes), linear_index(axes)
        out[me] = src[me] if scatter else src[...]

    for axes, scatter, src, out, send, recv in groups:
        count, me = group_size(axes), linear_index(axes)

        def finish(step, carry, axes=axes, scatter=scatter, count=count, me=me, src=src, out=out, send=send, recv=recv):
            peer = (me + step) % count
            copy = pltpu.make_async_remote_copy(
                src.at[peer] if scatter else src, out.at[peer], send.at[peer], recv.at[peer],
                device_id=member(axes, peer), device_id_type=MESH_IDS,
            )
            copy.wait_send()
            copy.wait_recv()
            return carry

        lax.fori_loop(1, count, finish, 0)


def pair_exchange(routes, tag):
    plan = tuple((axes, scatter) for axes, src, scatter in routes)
    srcs = [src for axes, src, scatter in routes]
    shapes = [
        jax.ShapeDtypeStruct(src.shape if scatter else (group_size(axes),) + src.shape, src.dtype)
        for axes, src, scatter in routes
    ]
    sems = []
    for axes, src, scatter in routes:
        sems += [pltpu.SemaphoreType.DMA((group_size(axes),))] * 2
    vmem = pl.BlockSpec(memory_space=pltpu.VMEM)
    return pl.pallas_call(
        functools.partial(pair_kernel, plan),
        out_shape=tuple(shapes),
        in_specs=[vmem] * len(routes),
        out_specs=tuple([vmem] * len(routes)),
        scratch_shapes=sems,
        compiler_params=pltpu.CompilerParams(collective_id=tag, has_side_effects=True),
    )(*srcs)


def local(images, texts, scale, shift):
    rows, width = images.shape
    image_unit, image_norm = unit_rows(images)
    text_unit, text_norm = unit_rows(texts)
    image_emb = image_unit.astype(jnp.bfloat16)
    text_emb = text_unit.astype(jnp.bfloat16)
    chips = group_size(CHIP_AXES)
    cores = group_size(CORE_AXES)
    image_count = chips * cores
    text_count = group_size(TEXT_AXES)
    total = image_count * text_count * rows
    gathered, seen = exchange(CORE_AXES + CHIP_AXES, image_emb, text_emb, False, 0)
    gathered = gathered.reshape(image_count * rows, width)
    seen = seen.reshape(text_count * rows, width)
    image_ids = jnp.arange(image_count * rows, dtype=jnp.int32)[:, None]
    text_ids = jnp.arange(text_count * rows, dtype=jnp.int32)[None, :]
    mine_i = linear_index(CORE_AXES + CHIP_AXES)
    mine_t = linear_index(TEXT_AXES)
    label = (
        (image_ids // rows == mine_i) & (text_ids // rows == mine_t) & (image_ids % rows == text_ids % rows)
    ).astype(jnp.float32)
    logit = (
        scale
        * lax.dot_general(gathered, seen, (((1,), (1,)), ((), ())), preferred_element_type=jnp.float32)
        + shift
    )
    loss = jnp.sum(jax.nn.softplus(logit * (1.0 - 2.0 * label)), 1, keepdims=True) / total
    coef = ((jax.nn.sigmoid(logit) - label) * scale).astype(jnp.bfloat16)
    image_part = jnp.dot(coef, seen, preferred_element_type=jnp.float32)
    text_part = lax.dot_general(coef, gathered, (((0,), (0,)), ((), ())), preferred_element_type=jnp.float32)
    image_part = jnp.concatenate([image_part, jnp.broadcast_to(loss, (image_count * rows, LOSS_LANES))], 1)
    loss_lanes, image_grad, text_grad = merged_reduce(
        CHIP_AXES, image_part.reshape(cores, chips, rows, width + LOSS_LANES), text_part.reshape(text_count, rows, width),
        (image_unit, text_unit), 3
    )
    return (loss_lanes[:, 0], image_grad / image_norm, text_grad / text_norm)


def solution(mesh):
    blk, grp = mesh.devices.shape
    fine = Mesh(mesh.devices.reshape(blk // 2, 2, grp // 16, 8, 2), ROWS_AXES)
    in_specs = (P(ROWS_AXES, None), P(ROWS_AXES, None), P(), P())
    out_specs = (P(ROWS_AXES), P(ROWS_AXES, None), P(ROWS_AXES, None))
    return jax.shard_map(local, mesh=fine, in_specs=in_specs, out_specs=out_specs, check_vma=False)
```

```python
import functools

import jax
import jax.numpy as jnp
from jax import lax
from jax.experimental import pallas as pl
from jax.experimental.pallas import tpu as pltpu
from jax.sharding import Mesh, PartitionSpec as P

ROWS_AXES = ("x", "zh", "y", "zl", "c")
CHIP_AXES = ("x", "y")
CORE_AXES = ("c",)
TEXT_AXES = ("zh", "zl")
MESH_IDS = pl.DeviceIdType.MESH
LOSS_LANES = 128


def unit_rows(values):
    floats = values.astype(jnp.float32)
    norms = jnp.sqrt(jnp.sum(floats * floats, 1, keepdims=True) + 1e-06)
    return (floats / norms, norms)


def back_rows(grads, units, norms):
    return (grads - units * jnp.sum(units * grads, 1, keepdims=True)) / norms


def linear_index(axes):
    index = 0
    for name in axes:
        index = index * lax.axis_size(name) + lax.axis_index(name)
    return index


def group_size(axes):
    size = 1
    for name in axes:
        size *= lax.axis_size(name)
    return size


def member(axes, k):
    coords = {}
    for name in reversed(axes):
        size = lax.axis_size(name)
        coords[name] = k % size
        k = k // size
    return tuple(coords[name] if name in coords else lax.axis_index(name) for name in ROWS_AXES)


def ring_peers():
    count, me = group_size(TEXT_AXES), linear_index(TEXT_AXES)
    return count, me, member(TEXT_AXES, (me + 1) % count), member(TEXT_AXES, (me + count - 1) % count)


def remote(src, dst, send, recv, device):
    return pltpu.make_async_remote_copy(src, dst, send, recv, device_id=device, device_id_type=MESH_IDS)


def greet_all(image_axes, barrier, image_count, image_me, right, left, extra=()):
    def greet(step, carry):
        pl.semaphore_signal(barrier, 1, device_id=member(image_axes, (image_me + step) % image_count),
                            device_id_type=MESH_IDS)
        return carry

    lax.fori_loop(1, image_count, greet, 0)
    for device in (right, left) + tuple(extra):
        pl.semaphore_signal(barrier, 1, device_id=device, device_id_type=MESH_IDS)
    pl.semaphore_wait(barrier, image_count + 1 + len(extra))


def image_direct(image_axes, scatter, src, out, send, recv, count, me):
    def start(step, carry):
        peer = (me + step) % count
        remote(src.at[peer] if scatter else src, out.at[me], send.at[peer], recv.at[me],
               member(image_axes, peer)).start()
        return carry

    lax.fori_loop(1, count, start, 0)
    out[me] = src[me] if scatter else src[...]

    def finish(step, carry):
        peer = (me + step) % count
        copy = remote(src.at[peer] if scatter else src, out.at[peer], send.at[peer], recv.at[peer],
                      member(image_axes, peer))
        copy.wait_send()
        copy.wait_recv()
        return carry

    return finish


def gather_kernel(image_axes, image_src, text_src, scale_ref, shift_ref, image_part_out, text_part_out, image_send,
                  image_recv, text_send, text_recv, image_out, text_out):
    image_count, image_me = group_size(image_axes), linear_index(image_axes)
    count, me, right, left = ring_peers()
    right2 = member(TEXT_AXES, (me + 2) % count)
    left2 = member(TEXT_AXES, (me + count - 2) % count)
    greet_all(image_axes, pltpu.get_barrier_semaphore(), image_count, image_me, right, left, (right2, left2))
    finish = image_direct(image_axes, False, image_src, image_out, image_send, image_recv, image_count, image_me)
    sends = []

    def send(src, origin, device, slot):
        copy = remote(src, text_out.at[origin], text_send.at[slot], text_recv.at[origin], device)
        copy.start()
        sends.append(copy)

    def arrive(origin):
        remote(text_out.at[origin], text_out.at[origin], text_send.at[0], text_recv.at[origin], right).wait_recv()

    half = count // 2
    for slot, device in ((0, right), (1, right2), (half, left), (half + 1, left2)):
        send(text_src, me, device, slot)
    text_out[me] = text_src[...]
    slot_right, slot_left = 2, half + 2
    for step in range(2, half // 2 + 1):
        for distance in (2 * step - 3, 2 * step - 2):
            origin = (me + count - distance) % count
            arrive(origin)
            send(text_out.at[origin], origin, right2, slot_right)
            slot_right += 1
        for distance in (2 * step - 3, 2 * step - 2):
            if distance > half - 3:
                continue
            origin = (me + distance) % count
            arrive(origin)
            send(text_out.at[origin], origin, left2, slot_left)
            slot_left += 1
    for distance in (half - 1, half):
        arrive((me + count - distance) % count)
    for distance in (half - 2, half - 1):
        arrive((me + distance) % count)
    for copy in sends:
        copy.wait_send()
    lax.fori_loop(1, image_count, finish, 0)
    rows, width = image_src.shape
    gathered = image_out[...].reshape(image_count * rows, width)
    seen = text_out[...].reshape(count * rows, width)
    scale, shift = scale_ref[...], shift_ref[...]
    shape = (image_count * rows, count * rows)
    image_ids = lax.broadcasted_iota(jnp.int32, shape, 0)
    text_ids = lax.broadcasted_iota(jnp.int32, shape, 1)
    label = ((image_ids // rows == image_me) & (text_ids // rows == me) & (image_ids % rows == text_ids % rows)).astype(
        jnp.float32)
    logit = scale * lax.dot_general(gathered, seen, (((1,), (1,)), ((), ())), preferred_element_type=jnp.float32) + shift
    total = image_count * count * rows
    loss = jnp.sum(jax.nn.softplus(logit * (1.0 - 2.0 * label)), 1, keepdims=True) / total
    coef = ((jax.nn.sigmoid(logit) - label) * scale).astype(jnp.bfloat16)
    image_part_out[:, :width] = jnp.dot(coef, seen, preferred_element_type=jnp.float32)
    image_part_out[:, width:] = jnp.broadcast_to(loss, (image_count * rows, LOSS_LANES))
    text_part_out[...] = lax.dot_general(coef, gathered, (((0,), (0,)), ((), ())), preferred_element_type=jnp.float32)


def reduce_kernel(image_axes, image_src, text_src, image_out, text_out, image_send, image_recv, text_send, text_recv,
                  inbox, outbox):
    image_count, image_me = group_size(image_axes), linear_index(image_axes)
    count, me, right, left = ring_peers()
    half = count // 2
    greet_all(image_axes, pltpu.get_barrier_semaphore(), image_count, image_me, right, left)
    finish = image_direct(image_axes, True, image_src, image_out, image_send, image_recv, image_count, image_me)
    sends = [remote(text_src.at[(me + half) % count], inbox.at[0], text_send.at[0], text_recv.at[0], right),
             remote(text_src.at[(me + half + 1) % count], inbox.at[half], text_send.at[half], text_recv.at[half], left)]
    for copy in sends:
        copy.start()
    for step in range(1, half):
        chains = ((step, (me + half - step) % count, right), (half + step, (me + half + 1 + step) % count, left))
        for slot, target, device in chains:
            if slot >= count - 1:
                continue
            remote(inbox.at[slot - 1], inbox.at[slot - 1], text_send.at[slot], text_recv.at[slot - 1], device).wait_recv()
            outbox[slot] = inbox[slot - 1] + text_src[target]
            copy = remote(outbox.at[slot], inbox.at[slot], text_send.at[slot], text_recv.at[slot], device)
            copy.start()
            sends.append(copy)
    last_right, last_left = half - 1, count - 2
    for slot in (last_right, last_left):
        remote(inbox.at[slot], inbox.at[slot], text_send.at[0], text_recv.at[slot], right).wait_recv()
    text_out[...] = text_src[me] + inbox[last_right] + inbox[last_left]
    for copy in sends:
        copy.wait_send()
    lax.fori_loop(1, image_count, finish, 0)


def merged_reduce_kernel(image_axes, image_src, text_src, image_out, text_out, image_send, image_recv, text_send,
                         text_recv, inbox, outbox, halfbox, summed, half_sems):
    image_count, image_me = group_size(image_axes), linear_index(image_axes)
    count, me, right, left = ring_peers()
    right2 = member(TEXT_AXES, (me + 2) % count)
    left2 = member(TEXT_AXES, (me + count - 2) % count)
    core = linear_index(CORE_AXES)
    partner = member(CORE_AXES, 1 - core)
    greet_all(image_axes, pltpu.get_barrier_semaphore(), image_count, image_me, right, left, (right2, left2, partner))
    chains = (
        (0, 4, lambda step: right2, lambda step: 10 - 2 * step),
        (4, 4, lambda step: right2 if step < 4 else right, lambda step: 9 - 2 * step),
        (8, 3, lambda step: left2, lambda step: 2 * step - 8),
        (11, 4, lambda step: left2 if step < 4 else left, lambda step: 2 * step - 9),
    )
    sends = []

    def step_sends(step):
        for base, steps, device, offset in chains:
            if step > steps:
                continue
            slot = base + step - 1
            target = (me + count + offset(step)) % count
            if step == 1:
                source = text_src.at[target]
            else:
                remote(inbox.at[slot - 1], inbox.at[slot - 1], text_send.at[slot], text_recv.at[slot - 1],
                       right).wait_recv()
                outbox[slot] = inbox[slot - 1] + text_src[target]
                source = outbox.at[slot]
            copy = remote(source, inbox.at[slot], text_send.at[slot], text_recv.at[slot], device(step))
            copy.start()
            sends.append(copy)

    swap = remote(image_src.at[1 - core], halfbox, half_sems.at[0], half_sems.at[1], partner)
    swap.start()
    step_sends(1)
    step_sends(2)
    swap.wait_recv()
    summed[...] = image_src[core] + halfbox[...]
    finish = image_direct(image_axes, True, summed, image_out, image_send, image_recv, image_count, image_me)
    for step in range(3, 5):
        step_sends(step)
    finals = (3, 7, 10, 14)
    for slot in finals:
        remote(inbox.at[slot], inbox.at[slot], text_send.at[0], text_recv.at[slot], right).wait_recv()
    text_out[...] = text_src[me] + inbox[finals[0]] + inbox[finals[1]] + inbox[finals[2]] + inbox[finals[3]]
    for copy in sends:
        copy.wait_send()
    swap.wait_send()
    lax.fori_loop(1, image_count, finish, 0)


def merged_reduce(image_axes, image_src, text_src, tag):
    image_count, text_count = group_size(image_axes), group_size(TEXT_AXES)
    image_shape = image_src.shape[1:]
    block = text_src.shape[1:]
    vmem = pl.BlockSpec(memory_space=pltpu.VMEM)
    scratch = [
        pltpu.SemaphoreType.DMA((image_count,)),
        pltpu.SemaphoreType.DMA((image_count,)),
        pltpu.SemaphoreType.DMA((text_count,)),
        pltpu.SemaphoreType.DMA((text_count,)),
        pltpu.VMEM((text_count,) + block, text_src.dtype),
        pltpu.VMEM((text_count,) + block, text_src.dtype),
        pltpu.VMEM(image_shape, image_src.dtype),
        pltpu.VMEM(image_shape, image_src.dtype),
        pltpu.SemaphoreType.DMA((2,)),
    ]
    return pl.pallas_call(
        functools.partial(merged_reduce_kernel, image_axes),
        out_shape=(jax.ShapeDtypeStruct(image_shape, image_src.dtype), jax.ShapeDtypeStruct(block, text_src.dtype)),
        in_specs=[vmem, vmem],
        out_specs=(vmem, vmem),
        scratch_shapes=scratch,
        compiler_params=pltpu.CompilerParams(collective_id=tag, has_side_effects=True),
    )(image_src, text_src)


def gather_compute(image_axes, image_src, text_src, scale, shift, tag):
    image_count, text_count = group_size(image_axes), group_size(TEXT_AXES)
    rows, width = image_src.shape
    vmem = pl.BlockSpec(memory_space=pltpu.VMEM)
    scratch = [
        pltpu.SemaphoreType.DMA((image_count,)),
        pltpu.SemaphoreType.DMA((image_count,)),
        pltpu.SemaphoreType.DMA((text_count,)),
        pltpu.SemaphoreType.DMA((text_count,)),
        pltpu.VMEM((image_count,) + image_src.shape, image_src.dtype),
        pltpu.VMEM((text_count,) + text_src.shape, text_src.dtype),
    ]
    return pl.pallas_call(
        functools.partial(gather_kernel, image_axes),
        out_shape=(
            jax.ShapeDtypeStruct((image_count * rows, width + LOSS_LANES), jnp.float32),
            jax.ShapeDtypeStruct((text_count * rows, width), jnp.float32),
        ),
        in_specs=[vmem] * 4,
        out_specs=(vmem, vmem),
        scratch_shapes=scratch,
        compiler_params=pltpu.CompilerParams(collective_id=tag, has_side_effects=True),
    )(image_src, text_src, scale.reshape(1, 1), shift.reshape(1, 1))


def exchange(image_axes, image_src, text_src, scatter, tag):
    image_count, text_count = group_size(image_axes), group_size(TEXT_AXES)
    image_shape = image_src.shape if scatter else (image_count,) + image_src.shape
    text_shape = text_src.shape[1:] if scatter else (text_count,) + text_src.shape
    block = text_src.shape[1:] if scatter else text_src.shape
    vmem = pl.BlockSpec(memory_space=pltpu.VMEM)
    scratch = [
        pltpu.SemaphoreType.DMA((image_count,)),
        pltpu.SemaphoreType.DMA((image_count,)),
        pltpu.SemaphoreType.DMA((text_count,)),
        pltpu.SemaphoreType.DMA((text_count,)),
    ]
    if scatter:
        scratch += [pltpu.VMEM((text_count,) + block, text_src.dtype)] * 2
    return pl.pallas_call(
        functools.partial(reduce_kernel if scatter else gather_kernel, image_axes),
        out_shape=(jax.ShapeDtypeStruct(image_shape, image_src.dtype), jax.ShapeDtypeStruct(text_shape, text_src.dtype)),
        in_specs=[vmem, vmem],
        out_specs=(vmem, vmem),
        scratch_shapes=scratch,
        compiler_params=pltpu.CompilerParams(collective_id=tag, has_side_effects=True),
    )(image_src, text_src)


def pair_kernel(plan, *refs):
    count_groups = len(plan)
    srcs, outs = refs[:count_groups], refs[count_groups:2 * count_groups]
    sems = refs[2 * count_groups:]
    groups = [
        (axes, scatter, srcs[g], outs[g], sems[2 * g], sems[2 * g + 1]) for g, (axes, scatter) in enumerate(plan)
    ]
    barrier = pltpu.get_barrier_semaphore()
    peers = 0
    for axes, scatter, src, out, send, recv in groups:
        count, me = group_size(axes), linear_index(axes)
        peers += count - 1

        def greet(step, carry, axes=axes, count=count, me=me):
            pl.semaphore_signal(barrier, 1, device_id=member(axes, (me + step) % count), device_id_type=MESH_IDS)
            return carry

        lax.fori_loop(1, count, greet, 0)
    pl.semaphore_wait(barrier, peers)

    for axes, scatter, src, out, send, recv in groups:
        count, me = group_size(axes), linear_index(axes)

        def start(step, carry, axes=axes, scatter=scatter, count=count, me=me, src=src, out=out, send=send, recv=recv):
            peer = (me + step) % count
            pltpu.make_async_remote_copy(
                src.at[peer] if scatter else src, out.at[me], send.at[peer], recv.at[me],
                device_id=member(axes, peer), device_id_type=MESH_IDS,
            ).start()
            return carry

        lax.fori_loop(1, count, start, 0)

    for axes, scatter, src, out, send, recv in groups:
        count, me = group_size(axes), linear_index(axes)
        out[me] = src[me] if scatter else src[...]

    for axes, scatter, src, out, send, recv in groups:
        count, me = group_size(axes), linear_index(axes)

        def finish(step, carry, axes=axes, scatter=scatter, count=count, me=me, src=src, out=out, send=send, recv=recv):
            peer = (me + step) % count
            copy = pltpu.make_async_remote_copy(
                src.at[peer] if scatter else src, out.at[peer], send.at[peer], recv.at[peer],
                device_id=member(axes, peer), device_id_type=MESH_IDS,
            )
            copy.wait_send()
            copy.wait_recv()
            return carry

        lax.fori_loop(1, count, finish, 0)


def pair_exchange(routes, tag):
    plan = tuple((axes, scatter) for axes, src, scatter in routes)
    srcs = [src for axes, src, scatter in routes]
    shapes = [
        jax.ShapeDtypeStruct(src.shape if scatter else (group_size(axes),) + src.shape, src.dtype)
        for axes, src, scatter in routes
    ]
    sems = []
    for axes, src, scatter in routes:
        sems += [pltpu.SemaphoreType.DMA((group_size(axes),))] * 2
    vmem = pl.BlockSpec(memory_space=pltpu.VMEM)
    return pl.pallas_call(
        functools.partial(pair_kernel, plan),
        out_shape=tuple(shapes),
        in_specs=[vmem] * len(routes),
        out_specs=tuple([vmem] * len(routes)),
        scratch_shapes=sems,
        compiler_params=pltpu.CompilerParams(collective_id=tag, has_side_effects=True),
    )(*srcs)


def local(images, texts, scale, shift):
    rows, width = images.shape
    image_unit, image_norm = unit_rows(images)
    text_unit, text_norm = unit_rows(texts)
    image_emb = image_unit.astype(jnp.bfloat16)
    text_emb = text_unit.astype(jnp.bfloat16)
    chips = group_size(CHIP_AXES)
    cores = group_size(CORE_AXES)
    image_count = chips * cores
    text_count = group_size(TEXT_AXES)
    total = image_count * text_count * rows
    image_part, text_part = gather_compute(CORE_AXES + CHIP_AXES, image_emb, text_emb, scale, shift, 0)
    image_in, text_in = merged_reduce(
        CHIP_AXES, image_part.reshape(cores, chips, rows, width + LOSS_LANES), text_part.reshape(text_count, rows, width), 3
    )
    image_in = jnp.sum(image_in, 0)
    text_sum = text_in
    image_grad = back_rows(image_in[:, :width], image_unit, image_norm)
    text_grad = back_rows(text_sum, text_unit, text_norm)
    return (image_in[:, width], image_grad, text_grad)


def solution(mesh):
    blk, grp = mesh.devices.shape
    fine = Mesh(mesh.devices.reshape(blk // 2, 2, grp // 16, 8, 2), ROWS_AXES)
    in_specs = (P(ROWS_AXES, None), P(ROWS_AXES, None), P(), P())
    out_specs = (P(ROWS_AXES), P(ROWS_AXES, None), P(ROWS_AXES, None))
    return jax.shard_map(local, mesh=fine, in_specs=in_specs, out_specs=out_specs, check_vma=False)
```

```python
import functools

import jax
import jax.numpy as jnp
from jax import lax
from jax.experimental import pallas as pl
from jax.experimental.pallas import tpu as pltpu
from jax.sharding import Mesh, PartitionSpec as P

ROWS_AXES = ("x", "zh", "y", "zl", "c")
CHIP_AXES = ("x", "y")
CORE_AXES = ("c",)
TEXT_AXES = ("zh", "zl")
MESH_IDS = pl.DeviceIdType.MESH
LOSS_LANES = 128


def unit_rows(values):
    floats = values.astype(jnp.float32)
    norms = jnp.sqrt(jnp.sum(floats * floats, 1, keepdims=True) + 1e-06)
    return (floats / norms, norms)


def back_rows(grads, units, norms):
    return (grads - units * jnp.sum(units * grads, 1, keepdims=True)) / norms


def linear_index(axes):
    index = 0
    for name in axes:
        index = index * lax.axis_size(name) + lax.axis_index(name)
    return index


def group_size(axes):
    size = 1
    for name in axes:
        size *= lax.axis_size(name)
    return size


def member(axes, k):
    coords = {}
    for name in reversed(axes):
        size = lax.axis_size(name)
        coords[name] = k % size
        k = k // size
    return tuple(coords[name] if name in coords else lax.axis_index(name) for name in ROWS_AXES)


def ring_peers():
    count, me = group_size(TEXT_AXES), linear_index(TEXT_AXES)
    return count, me, member(TEXT_AXES, (me + 1) % count), member(TEXT_AXES, (me + count - 1) % count)


def remote(src, dst, send, recv, device):
    return pltpu.make_async_remote_copy(src, dst, send, recv, device_id=device, device_id_type=MESH_IDS)


def greet_all(image_axes, barrier, image_count, image_me, right, left, extra=()):
    def greet(step, carry):
        pl.semaphore_signal(barrier, 1, device_id=member(image_axes, (image_me + step) % image_count),
                            device_id_type=MESH_IDS)
        return carry

    lax.fori_loop(1, image_count, greet, 0)
    for device in (right, left) + tuple(extra):
        pl.semaphore_signal(barrier, 1, device_id=device, device_id_type=MESH_IDS)
    pl.semaphore_wait(barrier, image_count + 1 + len(extra))


def image_direct(image_axes, scatter, src, out, send, recv, count, me):
    def start(step, carry):
        peer = (me + step) % count
        remote(src.at[peer] if scatter else src, out.at[me], send.at[peer], recv.at[me],
               member(image_axes, peer)).start()
        return carry

    lax.fori_loop(1, count, start, 0)
    out[me] = src[me] if scatter else src[...]

    def finish(step, carry):
        peer = (me + step) % count
        copy = remote(src.at[peer] if scatter else src, out.at[peer], send.at[peer], recv.at[peer],
                      member(image_axes, peer))
        copy.wait_send()
        copy.wait_recv()
        return carry

    return finish


def gather_kernel(image_axes, image_raw, text_raw, scale_ref, shift_ref, image_part_out, text_part_out,
                  image_unit_out, image_norm_out, text_unit_out, text_norm_out, image_send, image_recv, text_send,
                  text_recv, image_out, text_out, image_src, text_src):
    for raw, unit_out, norm_out, emb in ((image_raw, image_unit_out, image_norm_out, image_src),
                                         (text_raw, text_unit_out, text_norm_out, text_src)):
        floats = raw[...].astype(jnp.float32)
        norms = jnp.sqrt(jnp.sum(floats * floats, 1, keepdims=True) + 1e-06)
        units = floats / norms
        unit_out[...] = units
        norm_out[...] = jnp.broadcast_to(norms, norm_out.shape)
        emb[...] = units.astype(jnp.bfloat16)
    image_count, image_me = group_size(image_axes), linear_index(image_axes)
    count, me, right, left = ring_peers()
    right2 = member(TEXT_AXES, (me + 2) % count)
    left2 = member(TEXT_AXES, (me + count - 2) % count)
    greet_all(image_axes, pltpu.get_barrier_semaphore(), image_count, image_me, right, left, (right2, left2))
    finish = image_direct(image_axes, False, image_src, image_out, image_send, image_recv, image_count, image_me)
    sends = []

    def send(src, origin, device, slot):
        copy = remote(src, text_out.at[origin], text_send.at[slot], text_recv.at[origin], device)
        copy.start()
        sends.append(copy)

    def arrive(origin):
        remote(text_out.at[origin], text_out.at[origin], text_send.at[0], text_recv.at[origin], right).wait_recv()

    half = count // 2
    for slot, device in ((0, right), (1, right2), (half, left), (half + 1, left2)):
        send(text_src, me, device, slot)
    text_out[me] = text_src[...]
    slot_right, slot_left = 2, half + 2
    for step in range(2, half // 2 + 1):
        for distance in (2 * step - 3, 2 * step - 2):
            origin = (me + count - distance) % count
            arrive(origin)
            send(text_out.at[origin], origin, right2, slot_right)
            slot_right += 1
        for distance in (2 * step - 3, 2 * step - 2):
            if distance > half - 3:
                continue
            origin = (me + distance) % count
            arrive(origin)
            send(text_out.at[origin], origin, left2, slot_left)
            slot_left += 1
    for distance in (half - 1, half):
        arrive((me + count - distance) % count)
    for distance in (half - 2, half - 1):
        arrive((me + distance) % count)
    for copy in sends:
        copy.wait_send()
    lax.fori_loop(1, image_count, finish, 0)
    rows, width = image_src.shape
    gathered = image_out[...].reshape(image_count * rows, width)
    seen = text_out[...].reshape(count * rows, width)
    scale, shift = scale_ref[...], shift_ref[...]
    shape = (image_count * rows, count * rows)
    image_ids = lax.broadcasted_iota(jnp.int32, shape, 0)
    text_ids = lax.broadcasted_iota(jnp.int32, shape, 1)
    label = ((image_ids // rows == image_me) & (text_ids // rows == me) & (image_ids % rows == text_ids % rows)).astype(
        jnp.float32)
    logit = scale * lax.dot_general(gathered, seen, (((1,), (1,)), ((), ())), preferred_element_type=jnp.float32) + shift
    total = image_count * count * rows
    loss = jnp.sum(jax.nn.softplus(logit * (1.0 - 2.0 * label)), 1, keepdims=True) / total
    coef = ((jax.nn.sigmoid(logit) - label) * scale).astype(jnp.bfloat16)
    image_part_out[:, :width] = jnp.dot(coef, seen, preferred_element_type=jnp.float32)
    image_part_out[:, width:] = jnp.broadcast_to(loss, (image_count * rows, LOSS_LANES))
    text_part_out[...] = lax.dot_general(coef, gathered, (((0,), (0,)), ((), ())), preferred_element_type=jnp.float32)


def reduce_kernel(image_axes, image_src, text_src, image_out, text_out, image_send, image_recv, text_send, text_recv,
                  inbox, outbox):
    image_count, image_me = group_size(image_axes), linear_index(image_axes)
    count, me, right, left = ring_peers()
    half = count // 2
    greet_all(image_axes, pltpu.get_barrier_semaphore(), image_count, image_me, right, left)
    finish = image_direct(image_axes, True, image_src, image_out, image_send, image_recv, image_count, image_me)
    sends = [remote(text_src.at[(me + half) % count], inbox.at[0], text_send.at[0], text_recv.at[0], right),
             remote(text_src.at[(me + half + 1) % count], inbox.at[half], text_send.at[half], text_recv.at[half], left)]
    for copy in sends:
        copy.start()
    for step in range(1, half):
        chains = ((step, (me + half - step) % count, right), (half + step, (me + half + 1 + step) % count, left))
        for slot, target, device in chains:
            if slot >= count - 1:
                continue
            remote(inbox.at[slot - 1], inbox.at[slot - 1], text_send.at[slot], text_recv.at[slot - 1], device).wait_recv()
            outbox[slot] = inbox[slot - 1] + text_src[target]
            copy = remote(outbox.at[slot], inbox.at[slot], text_send.at[slot], text_recv.at[slot], device)
            copy.start()
            sends.append(copy)
    last_right, last_left = half - 1, count - 2
    for slot in (last_right, last_left):
        remote(inbox.at[slot], inbox.at[slot], text_send.at[0], text_recv.at[slot], right).wait_recv()
    text_out[...] = text_src[me] + inbox[last_right] + inbox[last_left]
    for copy in sends:
        copy.wait_send()
    lax.fori_loop(1, image_count, finish, 0)


def merged_reduce_kernel(image_axes, image_src, text_src, image_out, text_out, image_send, image_recv, text_send,
                         text_recv, inbox, outbox, halfbox, summed, half_sems):
    image_count, image_me = group_size(image_axes), linear_index(image_axes)
    count, me, right, left = ring_peers()
    right2 = member(TEXT_AXES, (me + 2) % count)
    left2 = member(TEXT_AXES, (me + count - 2) % count)
    core = linear_index(CORE_AXES)
    partner = member(CORE_AXES, 1 - core)
    greet_all(image_axes, pltpu.get_barrier_semaphore(), image_count, image_me, right, left, (right2, left2, partner))
    chains = (
        (0, 4, lambda step: right2, lambda step: 10 - 2 * step),
        (4, 4, lambda step: right2 if step < 4 else right, lambda step: 9 - 2 * step),
        (8, 3, lambda step: left2, lambda step: 2 * step - 8),
        (11, 4, lambda step: left2 if step < 4 else left, lambda step: 2 * step - 9),
    )
    sends = []

    def step_sends(step):
        for base, steps, device, offset in chains:
            if step > steps:
                continue
            slot = base + step - 1
            target = (me + count + offset(step)) % count
            if step == 1:
                source = text_src.at[target]
            else:
                remote(inbox.at[slot - 1], inbox.at[slot - 1], text_send.at[slot], text_recv.at[slot - 1],
                       right).wait_recv()
                outbox[slot] = inbox[slot - 1] + text_src[target]
                source = outbox.at[slot]
            copy = remote(source, inbox.at[slot], text_send.at[slot], text_recv.at[slot], device(step))
            copy.start()
            sends.append(copy)

    swap = remote(image_src.at[1 - core], halfbox, half_sems.at[0], half_sems.at[1], partner)
    swap.start()
    step_sends(1)
    step_sends(2)
    swap.wait_recv()
    summed[...] = image_src[core] + halfbox[...]
    finish = image_direct(image_axes, True, summed, image_out, image_send, image_recv, image_count, image_me)
    for step in range(3, 5):
        step_sends(step)
    finals = (3, 7, 10, 14)
    for slot in finals:
        remote(inbox.at[slot], inbox.at[slot], text_send.at[0], text_recv.at[slot], right).wait_recv()
    text_out[...] = text_src[me] + inbox[finals[0]] + inbox[finals[1]] + inbox[finals[2]] + inbox[finals[3]]
    for copy in sends:
        copy.wait_send()
    swap.wait_send()
    lax.fori_loop(1, image_count, finish, 0)


def merged_reduce(image_axes, image_src, text_src, tag):
    image_count, text_count = group_size(image_axes), group_size(TEXT_AXES)
    image_shape = image_src.shape[1:]
    block = text_src.shape[1:]
    vmem = pl.BlockSpec(memory_space=pltpu.VMEM)
    scratch = [
        pltpu.SemaphoreType.DMA((image_count,)),
        pltpu.SemaphoreType.DMA((image_count,)),
        pltpu.SemaphoreType.DMA((text_count,)),
        pltpu.SemaphoreType.DMA((text_count,)),
        pltpu.VMEM((text_count,) + block, text_src.dtype),
        pltpu.VMEM((text_count,) + block, text_src.dtype),
        pltpu.VMEM(image_shape, image_src.dtype),
        pltpu.VMEM(image_shape, image_src.dtype),
        pltpu.SemaphoreType.DMA((2,)),
    ]
    return pl.pallas_call(
        functools.partial(merged_reduce_kernel, image_axes),
        out_shape=(jax.ShapeDtypeStruct(image_shape, image_src.dtype), jax.ShapeDtypeStruct(block, text_src.dtype)),
        in_specs=[vmem, vmem],
        out_specs=(vmem, vmem),
        scratch_shapes=scratch,
        compiler_params=pltpu.CompilerParams(collective_id=tag, has_side_effects=True),
    )(image_src, text_src)


def gather_compute(image_axes, image_src, text_src, scale, shift, tag):
    image_count, text_count = group_size(image_axes), group_size(TEXT_AXES)
    rows, width = image_src.shape
    vmem = pl.BlockSpec(memory_space=pltpu.VMEM)
    scratch = [
        pltpu.SemaphoreType.DMA((image_count,)),
        pltpu.SemaphoreType.DMA((image_count,)),
        pltpu.SemaphoreType.DMA((text_count,)),
        pltpu.SemaphoreType.DMA((text_count,)),
        pltpu.VMEM((image_count,) + image_src.shape, jnp.bfloat16),
        pltpu.VMEM((text_count,) + text_src.shape, jnp.bfloat16),
        pltpu.VMEM(image_src.shape, jnp.bfloat16),
        pltpu.VMEM(text_src.shape, jnp.bfloat16),
    ]
    return pl.pallas_call(
        functools.partial(gather_kernel, image_axes),
        out_shape=(
            jax.ShapeDtypeStruct((image_count * rows, width + LOSS_LANES), jnp.float32),
            jax.ShapeDtypeStruct((text_count * rows, width), jnp.float32),
            jax.ShapeDtypeStruct((rows, width), jnp.float32),
            jax.ShapeDtypeStruct((rows, LOSS_LANES), jnp.float32),
            jax.ShapeDtypeStruct((rows, width), jnp.float32),
            jax.ShapeDtypeStruct((rows, LOSS_LANES), jnp.float32),
        ),
        in_specs=[vmem] * 4,
        out_specs=tuple([vmem] * 6),
        scratch_shapes=scratch,
        compiler_params=pltpu.CompilerParams(collective_id=tag, has_side_effects=True),
    )(image_src, text_src, scale.reshape(1, 1), shift.reshape(1, 1))


def exchange(image_axes, image_src, text_src, scatter, tag):
    image_count, text_count = group_size(image_axes), group_size(TEXT_AXES)
    image_shape = image_src.shape if scatter else (image_count,) + image_src.shape
    text_shape = text_src.shape[1:] if scatter else (text_count,) + text_src.shape
    block = text_src.shape[1:] if scatter else text_src.shape
    vmem = pl.BlockSpec(memory_space=pltpu.VMEM)
    scratch = [
        pltpu.SemaphoreType.DMA((image_count,)),
        pltpu.SemaphoreType.DMA((image_count,)),
        pltpu.SemaphoreType.DMA((text_count,)),
        pltpu.SemaphoreType.DMA((text_count,)),
    ]
    if scatter:
        scratch += [pltpu.VMEM((text_count,) + block, text_src.dtype)] * 2
    return pl.pallas_call(
        functools.partial(reduce_kernel if scatter else gather_kernel, image_axes),
        out_shape=(jax.ShapeDtypeStruct(image_shape, image_src.dtype), jax.ShapeDtypeStruct(text_shape, text_src.dtype)),
        in_specs=[vmem, vmem],
        out_specs=(vmem, vmem),
        scratch_shapes=scratch,
        compiler_params=pltpu.CompilerParams(collective_id=tag, has_side_effects=True),
    )(image_src, text_src)


def pair_kernel(plan, *refs):
    count_groups = len(plan)
    srcs, outs = refs[:count_groups], refs[count_groups:2 * count_groups]
    sems = refs[2 * count_groups:]
    groups = [
        (axes, scatter, srcs[g], outs[g], sems[2 * g], sems[2 * g + 1]) for g, (axes, scatter) in enumerate(plan)
    ]
    barrier = pltpu.get_barrier_semaphore()
    peers = 0
    for axes, scatter, src, out, send, recv in groups:
        count, me = group_size(axes), linear_index(axes)
        peers += count - 1

        def greet(step, carry, axes=axes, count=count, me=me):
            pl.semaphore_signal(barrier, 1, device_id=member(axes, (me + step) % count), device_id_type=MESH_IDS)
            return carry

        lax.fori_loop(1, count, greet, 0)
    pl.semaphore_wait(barrier, peers)

    for axes, scatter, src, out, send, recv in groups:
        count, me = group_size(axes), linear_index(axes)

        def start(step, carry, axes=axes, scatter=scatter, count=count, me=me, src=src, out=out, send=send, recv=recv):
            peer = (me + step) % count
            pltpu.make_async_remote_copy(
                src.at[peer] if scatter else src, out.at[me], send.at[peer], recv.at[me],
                device_id=member(axes, peer), device_id_type=MESH_IDS,
            ).start()
            return carry

        lax.fori_loop(1, count, start, 0)

    for axes, scatter, src, out, send, recv in groups:
        count, me = group_size(axes), linear_index(axes)
        out[me] = src[me] if scatter else src[...]

    for axes, scatter, src, out, send, recv in groups:
        count, me = group_size(axes), linear_index(axes)

        def finish(step, carry, axes=axes, scatter=scatter, count=count, me=me, src=src, out=out, send=send, recv=recv):
            peer = (me + step) % count
            copy = pltpu.make_async_remote_copy(
                src.at[peer] if scatter else src, out.at[peer], send.at[peer], recv.at[peer],
                device_id=member(axes, peer), device_id_type=MESH_IDS,
            )
            copy.wait_send()
            copy.wait_recv()
            return carry

        lax.fori_loop(1, count, finish, 0)


def pair_exchange(routes, tag):
    plan = tuple((axes, scatter) for axes, src, scatter in routes)
    srcs = [src for axes, src, scatter in routes]
    shapes = [
        jax.ShapeDtypeStruct(src.shape if scatter else (group_size(axes),) + src.shape, src.dtype)
        for axes, src, scatter in routes
    ]
    sems = []
    for axes, src, scatter in routes:
        sems += [pltpu.SemaphoreType.DMA((group_size(axes),))] * 2
    vmem = pl.BlockSpec(memory_space=pltpu.VMEM)
    return pl.pallas_call(
        functools.partial(pair_kernel, plan),
        out_shape=tuple(shapes),
        in_specs=[vmem] * len(routes),
        out_specs=tuple([vmem] * len(routes)),
        scratch_shapes=sems,
        compiler_params=pltpu.CompilerParams(collective_id=tag, has_side_effects=True),
    )(*srcs)


def local(images, texts, scale, shift):
    rows, width = images.shape
    chips = group_size(CHIP_AXES)
    cores = group_size(CORE_AXES)
    text_count = group_size(TEXT_AXES)
    image_part, text_part, image_unit, image_norm, text_unit, text_norm = gather_compute(
        CORE_AXES + CHIP_AXES, images, texts, scale, shift, 0
    )
    image_norm = image_norm[:, :1]
    text_norm = text_norm[:, :1]
    image_in, text_in = merged_reduce(
        CHIP_AXES, image_part.reshape(cores, chips, rows, width + LOSS_LANES), text_part.reshape(text_count, rows, width), 3
    )
    image_in = jnp.sum(image_in, 0)
    text_sum = text_in
    image_grad = back_rows(image_in[:, :width], image_unit, image_norm)
    text_grad = back_rows(text_sum, text_unit, text_norm)
    return (image_in[:, width], image_grad, text_grad)


def solution(mesh):
    blk, grp = mesh.devices.shape
    fine = Mesh(mesh.devices.reshape(blk // 2, 2, grp // 16, 8, 2), ROWS_AXES)
    in_specs = (P(ROWS_AXES, None), P(ROWS_AXES, None), P(), P())
    out_specs = (P(ROWS_AXES), P(ROWS_AXES, None), P(ROWS_AXES, None))
    return jax.shard_map(local, mesh=fine, in_specs=in_specs, out_specs=out_specs, check_vma=False)
```

```python
import functools

import jax
import jax.numpy as jnp
from jax import lax
from jax.experimental import pallas as pl
from jax.experimental.pallas import tpu as pltpu
from jax.sharding import Mesh, PartitionSpec as P

ROWS_AXES = ("x", "zh", "y", "zl", "c")
CHIP_AXES = ("x", "y")
CORE_AXES = ("c",)
TEXT_AXES = ("zh", "zl")
MESH_IDS = pl.DeviceIdType.MESH
LOSS_LANES = 128


def unit_rows(values):
    floats = values.astype(jnp.float32)
    norms = jnp.sqrt(jnp.sum(floats * floats, 1, keepdims=True) + 1e-06)
    return (floats / norms, norms)


def back_rows(grads, units, norms):
    return (grads - units * jnp.sum(units * grads, 1, keepdims=True)) / norms


def linear_index(axes):
    index = 0
    for name in axes:
        index = index * lax.axis_size(name) + lax.axis_index(name)
    return index


def group_size(axes):
    size = 1
    for name in axes:
        size *= lax.axis_size(name)
    return size


def member(axes, k):
    coords = {}
    for name in reversed(axes):
        size = lax.axis_size(name)
        coords[name] = k % size
        k = k // size
    return tuple(coords[name] if name in coords else lax.axis_index(name) for name in ROWS_AXES)


def ring_peers():
    count, me = group_size(TEXT_AXES), linear_index(TEXT_AXES)
    return count, me, member(TEXT_AXES, (me + 1) % count), member(TEXT_AXES, (me + count - 1) % count)


def remote(src, dst, send, recv, device):
    return pltpu.make_async_remote_copy(src, dst, send, recv, device_id=device, device_id_type=MESH_IDS)


def greet_all(image_axes, barrier, image_count, image_me, right, left, extra=()):
    def greet(step, carry):
        pl.semaphore_signal(barrier, 1, device_id=member(image_axes, (image_me + step) % image_count),
                            device_id_type=MESH_IDS)
        return carry

    lax.fori_loop(1, image_count, greet, 0)
    for device in (right, left) + tuple(extra):
        pl.semaphore_signal(barrier, 1, device_id=device, device_id_type=MESH_IDS)
    pl.semaphore_wait(barrier, image_count + 1 + len(extra))


def image_direct(image_axes, scatter, src, out, send, recv, count, me):
    def start(step, carry):
        peer = (me + step) % count
        remote(src.at[peer] if scatter else src, out.at[me], send.at[peer], recv.at[me],
               member(image_axes, peer)).start()
        return carry

    lax.fori_loop(1, count, start, 0)
    out[me] = src[me] if scatter else src[...]

    def finish(step, carry):
        peer = (me + step) % count
        copy = remote(src.at[peer] if scatter else src, out.at[peer], send.at[peer], recv.at[peer],
                      member(image_axes, peer))
        copy.wait_send()
        copy.wait_recv()
        return carry

    return finish


def gather_kernel(image_axes, image_raw, text_raw, scale_ref, shift_ref, image_part_out, text_part_out,
                  image_unit_out, image_norm_out, text_unit_out, text_norm_out, image_send, image_recv, text_send,
                  text_recv, image_out, text_out, image_src, text_src):
    for raw, unit_out, norm_out, emb in ((image_raw, image_unit_out, image_norm_out, image_src),
                                         (text_raw, text_unit_out, text_norm_out, text_src)):
        floats = raw[...].astype(jnp.float32)
        norms = jnp.sqrt(jnp.sum(floats * floats, 1, keepdims=True) + 1e-06)
        units = floats / norms
        unit_out[...] = units
        norm_out[...] = jnp.broadcast_to(norms, norm_out.shape)
        emb[...] = units.astype(jnp.bfloat16)
    image_count, image_me = group_size(image_axes), linear_index(image_axes)
    count, me, right, left = ring_peers()
    right2 = member(TEXT_AXES, (me + 2) % count)
    left2 = member(TEXT_AXES, (me + count - 2) % count)
    greet_all(image_axes, pltpu.get_barrier_semaphore(), image_count, image_me, right, left, (right2, left2))
    finish = image_direct(image_axes, False, image_src, image_out, image_send, image_recv, image_count, image_me)
    sends = []

    def send(src, origin, device, slot):
        copy = remote(src, text_out.at[origin], text_send.at[slot], text_recv.at[origin], device)
        copy.start()
        sends.append(copy)

    def arrive(origin):
        remote(text_out.at[origin], text_out.at[origin], text_send.at[0], text_recv.at[origin], right).wait_recv()

    half = count // 2
    for slot, device in ((0, right), (1, right2), (half, left), (half + 1, left2)):
        send(text_src, me, device, slot)
    text_out[me] = text_src[...]
    slot_right, slot_left = 2, half + 2
    for step in range(2, half // 2 + 1):
        for distance in (2 * step - 3, 2 * step - 2):
            origin = (me + count - distance) % count
            arrive(origin)
            send(text_out.at[origin], origin, right2, slot_right)
            slot_right += 1
        for distance in (2 * step - 3, 2 * step - 2):
            if distance > half - 3:
                continue
            origin = (me + distance) % count
            arrive(origin)
            send(text_out.at[origin], origin, left2, slot_left)
            slot_left += 1
    for distance in (half - 1, half):
        arrive((me + count - distance) % count)
    for distance in (half - 2, half - 1):
        arrive((me + distance) % count)
    for copy in sends:
        copy.wait_send()
    lax.fori_loop(1, image_count, finish, 0)
    rows, width = image_src.shape
    gathered = image_out[...].reshape(image_count * rows, width)
    seen = text_out[...].reshape(count * rows, width)
    scale, shift = scale_ref[...], shift_ref[...]
    shape = (image_count * rows, count * rows)
    image_ids = lax.broadcasted_iota(jnp.int32, shape, 0)
    text_ids = lax.broadcasted_iota(jnp.int32, shape, 1)
    label = ((image_ids // rows == image_me) & (text_ids // rows == me) & (image_ids % rows == text_ids % rows)).astype(
        jnp.float32)
    logit = scale * lax.dot_general(gathered, seen, (((1,), (1,)), ((), ())), preferred_element_type=jnp.float32) + shift
    total = image_count * count * rows
    loss = jnp.sum(jax.nn.softplus(logit * (1.0 - 2.0 * label)), 1, keepdims=True) / total
    coef = ((jax.nn.sigmoid(logit) - label) * scale).astype(jnp.bfloat16)
    image_part_out[:, :width] = jnp.dot(coef, seen, preferred_element_type=jnp.float32)
    image_part_out[:, width:] = jnp.broadcast_to(loss, (image_count * rows, LOSS_LANES))
    text_part_out[...] = lax.dot_general(coef, gathered, (((0,), (0,)), ((), ())), preferred_element_type=jnp.float32)


def reduce_kernel(image_axes, image_src, text_src, image_out, text_out, image_send, image_recv, text_send, text_recv,
                  inbox, outbox):
    image_count, image_me = group_size(image_axes), linear_index(image_axes)
    count, me, right, left = ring_peers()
    half = count // 2
    greet_all(image_axes, pltpu.get_barrier_semaphore(), image_count, image_me, right, left)
    finish = image_direct(image_axes, True, image_src, image_out, image_send, image_recv, image_count, image_me)
    sends = [remote(text_src.at[(me + half) % count], inbox.at[0], text_send.at[0], text_recv.at[0], right),
             remote(text_src.at[(me + half + 1) % count], inbox.at[half], text_send.at[half], text_recv.at[half], left)]
    for copy in sends:
        copy.start()
    for step in range(1, half):
        chains = ((step, (me + half - step) % count, right), (half + step, (me + half + 1 + step) % count, left))
        for slot, target, device in chains:
            if slot >= count - 1:
                continue
            remote(inbox.at[slot - 1], inbox.at[slot - 1], text_send.at[slot], text_recv.at[slot - 1], device).wait_recv()
            outbox[slot] = inbox[slot - 1] + text_src[target]
            copy = remote(outbox.at[slot], inbox.at[slot], text_send.at[slot], text_recv.at[slot], device)
            copy.start()
            sends.append(copy)
    last_right, last_left = half - 1, count - 2
    for slot in (last_right, last_left):
        remote(inbox.at[slot], inbox.at[slot], text_send.at[0], text_recv.at[slot], right).wait_recv()
    text_out[...] = text_src[me] + inbox[last_right] + inbox[last_left]
    for copy in sends:
        copy.wait_send()
    lax.fori_loop(1, image_count, finish, 0)


def merged_reduce_kernel(image_axes, image_src, text_src, image_total, text_out, image_send, image_recv, text_send,
                         text_recv, inbox, outbox, halfbox, summed, half_sems, image_out):
    image_count, image_me = group_size(image_axes), linear_index(image_axes)
    count, me, right, left = ring_peers()
    right2 = member(TEXT_AXES, (me + 2) % count)
    left2 = member(TEXT_AXES, (me + count - 2) % count)
    core = linear_index(CORE_AXES)
    partner = member(CORE_AXES, 1 - core)
    greet_all(image_axes, pltpu.get_barrier_semaphore(), image_count, image_me, right, left, (right2, left2, partner))
    chains = (
        (0, 4, lambda step: right2, lambda step: 10 - 2 * step),
        (4, 4, lambda step: right2 if step < 4 else right, lambda step: 9 - 2 * step),
        (8, 3, lambda step: left2, lambda step: 2 * step - 8),
        (11, 4, lambda step: left2 if step < 4 else left, lambda step: 2 * step - 9),
    )
    sends = []

    def step_sends(step):
        for base, steps, device, offset in chains:
            if step > steps:
                continue
            slot = base + step - 1
            target = (me + count + offset(step)) % count
            if step == 1:
                source = text_src.at[target]
            else:
                remote(inbox.at[slot - 1], inbox.at[slot - 1], text_send.at[slot], text_recv.at[slot - 1],
                       right).wait_recv()
                outbox[slot] = inbox[slot - 1] + text_src[target]
                source = outbox.at[slot]
            copy = remote(source, inbox.at[slot], text_send.at[slot], text_recv.at[slot], device(step))
            copy.start()
            sends.append(copy)

    swap = remote(image_src.at[1 - core], halfbox, half_sems.at[0], half_sems.at[1], partner)
    swap.start()
    step_sends(1)
    step_sends(2)
    swap.wait_recv()
    summed[...] = image_src[core] + halfbox[...]
    finish = image_direct(image_axes, True, summed, image_out, image_send, image_recv, image_count, image_me)
    for step in range(3, 5):
        step_sends(step)
    finals = (3, 7, 10, 14)
    for slot in finals:
        remote(inbox.at[slot], inbox.at[slot], text_send.at[0], text_recv.at[slot], right).wait_recv()
    text_out[...] = text_src[me] + inbox[finals[0]] + inbox[finals[1]] + inbox[finals[2]] + inbox[finals[3]]
    for copy in sends:
        copy.wait_send()
    swap.wait_send()
    lax.fori_loop(1, image_count, finish, 0)
    image_total[...] = jnp.sum(image_out[...], 0)


def merged_reduce(image_axes, image_src, text_src, tag):
    image_count, text_count = group_size(image_axes), group_size(TEXT_AXES)
    image_shape = image_src.shape[1:]
    block = text_src.shape[1:]
    vmem = pl.BlockSpec(memory_space=pltpu.VMEM)
    scratch = [
        pltpu.SemaphoreType.DMA((image_count,)),
        pltpu.SemaphoreType.DMA((image_count,)),
        pltpu.SemaphoreType.DMA((text_count,)),
        pltpu.SemaphoreType.DMA((text_count,)),
        pltpu.VMEM((text_count,) + block, text_src.dtype),
        pltpu.VMEM((text_count,) + block, text_src.dtype),
        pltpu.VMEM(image_shape, image_src.dtype),
        pltpu.VMEM(image_shape, image_src.dtype),
        pltpu.SemaphoreType.DMA((2,)),
        pltpu.VMEM(image_shape, image_src.dtype),
    ]
    return pl.pallas_call(
        functools.partial(merged_reduce_kernel, image_axes),
        out_shape=(jax.ShapeDtypeStruct(image_shape[1:], image_src.dtype), jax.ShapeDtypeStruct(block, text_src.dtype)),
        in_specs=[vmem, vmem],
        out_specs=(vmem, vmem),
        scratch_shapes=scratch,
        compiler_params=pltpu.CompilerParams(collective_id=tag, has_side_effects=True),
    )(image_src, text_src)


def gather_compute(image_axes, image_src, text_src, scale, shift, tag):
    image_count, text_count = group_size(image_axes), group_size(TEXT_AXES)
    rows, width = image_src.shape
    vmem = pl.BlockSpec(memory_space=pltpu.VMEM)
    scratch = [
        pltpu.SemaphoreType.DMA((image_count,)),
        pltpu.SemaphoreType.DMA((image_count,)),
        pltpu.SemaphoreType.DMA((text_count,)),
        pltpu.SemaphoreType.DMA((text_count,)),
        pltpu.VMEM((image_count,) + image_src.shape, jnp.bfloat16),
        pltpu.VMEM((text_count,) + text_src.shape, jnp.bfloat16),
        pltpu.VMEM(image_src.shape, jnp.bfloat16),
        pltpu.VMEM(text_src.shape, jnp.bfloat16),
    ]
    return pl.pallas_call(
        functools.partial(gather_kernel, image_axes),
        out_shape=(
            jax.ShapeDtypeStruct((image_count * rows, width + LOSS_LANES), jnp.float32),
            jax.ShapeDtypeStruct((text_count * rows, width), jnp.float32),
            jax.ShapeDtypeStruct((rows, width), jnp.float32),
            jax.ShapeDtypeStruct((rows, LOSS_LANES), jnp.float32),
            jax.ShapeDtypeStruct((rows, width), jnp.float32),
            jax.ShapeDtypeStruct((rows, LOSS_LANES), jnp.float32),
        ),
        in_specs=[vmem] * 4,
        out_specs=tuple([vmem] * 6),
        scratch_shapes=scratch,
        compiler_params=pltpu.CompilerParams(collective_id=tag, has_side_effects=True),
    )(image_src, text_src, scale.reshape(1, 1), shift.reshape(1, 1))


def exchange(image_axes, image_src, text_src, scatter, tag):
    image_count, text_count = group_size(image_axes), group_size(TEXT_AXES)
    image_shape = image_src.shape if scatter else (image_count,) + image_src.shape
    text_shape = text_src.shape[1:] if scatter else (text_count,) + text_src.shape
    block = text_src.shape[1:] if scatter else text_src.shape
    vmem = pl.BlockSpec(memory_space=pltpu.VMEM)
    scratch = [
        pltpu.SemaphoreType.DMA((image_count,)),
        pltpu.SemaphoreType.DMA((image_count,)),
        pltpu.SemaphoreType.DMA((text_count,)),
        pltpu.SemaphoreType.DMA((text_count,)),
    ]
    if scatter:
        scratch += [pltpu.VMEM((text_count,) + block, text_src.dtype)] * 2
    return pl.pallas_call(
        functools.partial(reduce_kernel if scatter else gather_kernel, image_axes),
        out_shape=(jax.ShapeDtypeStruct(image_shape, image_src.dtype), jax.ShapeDtypeStruct(text_shape, text_src.dtype)),
        in_specs=[vmem, vmem],
        out_specs=(vmem, vmem),
        scratch_shapes=scratch,
        compiler_params=pltpu.CompilerParams(collective_id=tag, has_side_effects=True),
    )(image_src, text_src)


def pair_kernel(plan, *refs):
    count_groups = len(plan)
    srcs, outs = refs[:count_groups], refs[count_groups:2 * count_groups]
    sems = refs[2 * count_groups:]
    groups = [
        (axes, scatter, srcs[g], outs[g], sems[2 * g], sems[2 * g + 1]) for g, (axes, scatter) in enumerate(plan)
    ]
    barrier = pltpu.get_barrier_semaphore()
    peers = 0
    for axes, scatter, src, out, send, recv in groups:
        count, me = group_size(axes), linear_index(axes)
        peers += count - 1

        def greet(step, carry, axes=axes, count=count, me=me):
            pl.semaphore_signal(barrier, 1, device_id=member(axes, (me + step) % count), device_id_type=MESH_IDS)
            return carry

        lax.fori_loop(1, count, greet, 0)
    pl.semaphore_wait(barrier, peers)

    for axes, scatter, src, out, send, recv in groups:
        count, me = group_size(axes), linear_index(axes)

        def start(step, carry, axes=axes, scatter=scatter, count=count, me=me, src=src, out=out, send=send, recv=recv):
            peer = (me + step) % count
            pltpu.make_async_remote_copy(
                src.at[peer] if scatter else src, out.at[me], send.at[peer], recv.at[me],
                device_id=member(axes, peer), device_id_type=MESH_IDS,
            ).start()
            return carry

        lax.fori_loop(1, count, start, 0)

    for axes, scatter, src, out, send, recv in groups:
        count, me = group_size(axes), linear_index(axes)
        out[me] = src[me] if scatter else src[...]

    for axes, scatter, src, out, send, recv in groups:
        count, me = group_size(axes), linear_index(axes)

        def finish(step, carry, axes=axes, scatter=scatter, count=count, me=me, src=src, out=out, send=send, recv=recv):
            peer = (me + step) % count
            copy = pltpu.make_async_remote_copy(
                src.at[peer] if scatter else src, out.at[peer], send.at[peer], recv.at[peer],
                device_id=member(axes, peer), device_id_type=MESH_IDS,
            )
            copy.wait_send()
            copy.wait_recv()
            return carry

        lax.fori_loop(1, count, finish, 0)


def pair_exchange(routes, tag):
    plan = tuple((axes, scatter) for axes, src, scatter in routes)
    srcs = [src for axes, src, scatter in routes]
    shapes = [
        jax.ShapeDtypeStruct(src.shape if scatter else (group_size(axes),) + src.shape, src.dtype)
        for axes, src, scatter in routes
    ]
    sems = []
    for axes, src, scatter in routes:
        sems += [pltpu.SemaphoreType.DMA((group_size(axes),))] * 2
    vmem = pl.BlockSpec(memory_space=pltpu.VMEM)
    return pl.pallas_call(
        functools.partial(pair_kernel, plan),
        out_shape=tuple(shapes),
        in_specs=[vmem] * len(routes),
        out_specs=tuple([vmem] * len(routes)),
        scratch_shapes=sems,
        compiler_params=pltpu.CompilerParams(collective_id=tag, has_side_effects=True),
    )(*srcs)


def local(images, texts, scale, shift):
    rows, width = images.shape
    chips = group_size(CHIP_AXES)
    cores = group_size(CORE_AXES)
    text_count = group_size(TEXT_AXES)
    image_part, text_part, image_unit, image_norm, text_unit, text_norm = gather_compute(
        CORE_AXES + CHIP_AXES, images, texts, scale, shift, 0
    )
    image_norm = image_norm[:, :1]
    text_norm = text_norm[:, :1]
    image_in, text_in = merged_reduce(
        CHIP_AXES, image_part.reshape(cores, chips, rows, width + LOSS_LANES), text_part.reshape(text_count, rows, width), 3
    )
    text_sum = text_in
    image_grad = back_rows(image_in[:, :width], image_unit, image_norm)
    text_grad = back_rows(text_sum, text_unit, text_norm)
    return (image_in[:, width], image_grad, text_grad)


def solution(mesh):
    blk, grp = mesh.devices.shape
    fine = Mesh(mesh.devices.reshape(blk // 2, 2, grp // 16, 8, 2), ROWS_AXES)
    in_specs = (P(ROWS_AXES, None), P(ROWS_AXES, None), P(), P())
    out_specs = (P(ROWS_AXES), P(ROWS_AXES, None), P(ROWS_AXES, None))
    return jax.shard_map(local, mesh=fine, in_specs=in_specs, out_specs=out_specs, check_vma=False)
```

```python
import functools

import jax
import jax.numpy as jnp
from jax import lax
from jax.experimental import pallas as pl
from jax.experimental.pallas import tpu as pltpu
from jax.sharding import Mesh, PartitionSpec as P

ROWS_AXES = ("x", "zh", "y", "zl", "c")
CHIP_AXES = ("x", "y")
CORE_AXES = ("c",)
TEXT_AXES = ("zh", "zl")
MESH_IDS = pl.DeviceIdType.MESH
LOSS_LANES = 128


def unit_rows(values):
    floats = values.astype(jnp.float32)
    norms = jnp.sqrt(jnp.sum(floats * floats, 1, keepdims=True) + 1e-06)
    return (floats / norms, norms)


def back_rows(grads, units, norms):
    return (grads - units * jnp.sum(units * grads, 1, keepdims=True)) / norms


def linear_index(axes):
    index = 0
    for name in axes:
        index = index * lax.axis_size(name) + lax.axis_index(name)
    return index


def group_size(axes):
    size = 1
    for name in axes:
        size *= lax.axis_size(name)
    return size


def member(axes, k):
    coords = {}
    for name in reversed(axes):
        size = lax.axis_size(name)
        coords[name] = k % size
        k = k // size
    return tuple(coords[name] if name in coords else lax.axis_index(name) for name in ROWS_AXES)


def ring_peers():
    count, me = group_size(TEXT_AXES), linear_index(TEXT_AXES)
    return count, me, member(TEXT_AXES, (me + 1) % count), member(TEXT_AXES, (me + count - 1) % count)


def remote(src, dst, send, recv, device):
    return pltpu.make_async_remote_copy(src, dst, send, recv, device_id=device, device_id_type=MESH_IDS)


def greet_all(image_axes, barrier, image_count, image_me, right, left, extra=()):
    def greet(step, carry):
        pl.semaphore_signal(barrier, 1, device_id=member(image_axes, (image_me + step) % image_count),
                            device_id_type=MESH_IDS)
        return carry

    lax.fori_loop(1, image_count, greet, 0)
    for device in (right, left) + tuple(extra):
        pl.semaphore_signal(barrier, 1, device_id=device, device_id_type=MESH_IDS)
    pl.semaphore_wait(barrier, image_count + 1 + len(extra))


def image_direct(image_axes, scatter, src, out, send, recv, count, me):
    def start(step, carry):
        peer = (me + step) % count
        remote(src.at[peer] if scatter else src, out.at[me], send.at[peer], recv.at[me],
               member(image_axes, peer)).start()
        return carry

    lax.fori_loop(1, count, start, 0)
    out[me] = src[me] if scatter else src[...]

    def finish(step, carry):
        peer = (me + step) % count
        copy = remote(src.at[peer] if scatter else src, out.at[peer], send.at[peer], recv.at[peer],
                      member(image_axes, peer))
        copy.wait_send()
        copy.wait_recv()
        return carry

    return finish


def gather_kernel(image_axes, image_raw, text_raw, scale_ref, shift_ref, image_part_out, text_part_out,
                  image_unit_out, image_norm_out, text_unit_out, text_norm_out, image_send, image_recv, text_send,
                  text_recv, image_out, text_out, image_src, text_src):
    for raw, unit_out, norm_out, emb in ((image_raw, image_unit_out, image_norm_out, image_src),
                                         (text_raw, text_unit_out, text_norm_out, text_src)):
        floats = raw[...].astype(jnp.float32)
        norms = jnp.sqrt(jnp.sum(floats * floats, 1, keepdims=True) + 1e-06)
        units = floats / norms
        unit_out[...] = units
        norm_out[...] = jnp.broadcast_to(norms, norm_out.shape)
        emb[...] = units.astype(jnp.bfloat16)
    image_count, image_me = group_size(image_axes), linear_index(image_axes)
    count, me, right, left = ring_peers()
    right2 = member(TEXT_AXES, (me + 2) % count)
    left2 = member(TEXT_AXES, (me + count - 2) % count)
    greet_all(image_axes, pltpu.get_barrier_semaphore(), image_count, image_me, right, left, (right2, left2))
    finish = image_direct(image_axes, False, image_src, image_out, image_send, image_recv, image_count, image_me)
    sends = []

    def send(src, origin, device, slot):
        copy = remote(src, text_out.at[origin], text_send.at[slot], text_recv.at[origin], device)
        copy.start()
        sends.append(copy)

    def arrive(origin):
        remote(text_out.at[origin], text_out.at[origin], text_send.at[0], text_recv.at[origin], right).wait_recv()

    half = count // 2
    for slot, device in ((0, right), (1, right2), (half, left), (half + 1, left2)):
        send(text_src, me, device, slot)
    text_out[me] = text_src[...]
    slot_right, slot_left = 2, half + 2
    for step in range(2, half // 2 + 1):
        for distance in (2 * step - 3, 2 * step - 2):
            origin = (me + count - distance) % count
            arrive(origin)
            send(text_out.at[origin], origin, right2, slot_right)
            slot_right += 1
        for distance in (2 * step - 3, 2 * step - 2):
            if distance > half - 3:
                continue
            origin = (me + distance) % count
            arrive(origin)
            send(text_out.at[origin], origin, left2, slot_left)
            slot_left += 1
    for distance in (half - 1, half):
        arrive((me + count - distance) % count)
    for distance in (half - 2, half - 1):
        arrive((me + distance) % count)
    for copy in sends:
        copy.wait_send()
    lax.fori_loop(1, image_count, finish, 0)
    rows, width = image_src.shape
    gathered = image_out[...].reshape(image_count * rows, width)
    seen = text_out[...].reshape(count * rows, width)
    scale, shift = scale_ref[...], shift_ref[...]
    shape = (image_count * rows, count * rows)
    image_ids = lax.broadcasted_iota(jnp.int32, shape, 0)
    text_ids = lax.broadcasted_iota(jnp.int32, shape, 1)
    label = ((image_ids // rows == image_me) & (text_ids // rows == me) & (image_ids % rows == text_ids % rows)).astype(
        jnp.float32)
    logit = scale * lax.dot_general(gathered, seen, (((1,), (1,)), ((), ())), preferred_element_type=jnp.float32) + shift
    total = image_count * count * rows
    loss = jnp.sum(jax.nn.softplus(logit * (1.0 - 2.0 * label)), 1, keepdims=True) / total
    coef = ((jax.nn.sigmoid(logit) - label) * scale).astype(jnp.bfloat16)
    image_part_out[:, :width] = jnp.dot(coef, seen, preferred_element_type=jnp.float32)
    image_part_out[:, width:] = jnp.broadcast_to(loss, (image_count * rows, LOSS_LANES))
    shape_t = (count * rows, image_count * rows)
    text_ids_t = lax.broadcasted_iota(jnp.int32, shape_t, 0)
    image_ids_t = lax.broadcasted_iota(jnp.int32, shape_t, 1)
    label_t = ((image_ids_t // rows == image_me) & (text_ids_t // rows == me)
               & (image_ids_t % rows == text_ids_t % rows)).astype(jnp.float32)
    logit_t = scale * lax.dot_general(seen, gathered, (((1,), (1,)), ((), ())), preferred_element_type=jnp.float32) + shift
    coef_t = ((jax.nn.sigmoid(logit_t) - label_t) * scale).astype(jnp.bfloat16)
    text_part_out[...] = jnp.dot(coef_t, gathered, preferred_element_type=jnp.float32)


def reduce_kernel(image_axes, image_src, text_src, image_out, text_out, image_send, image_recv, text_send, text_recv,
                  inbox, outbox):
    image_count, image_me = group_size(image_axes), linear_index(image_axes)
    count, me, right, left = ring_peers()
    half = count // 2
    greet_all(image_axes, pltpu.get_barrier_semaphore(), image_count, image_me, right, left)
    finish = image_direct(image_axes, True, image_src, image_out, image_send, image_recv, image_count, image_me)
    sends = [remote(text_src.at[(me + half) % count], inbox.at[0], text_send.at[0], text_recv.at[0], right),
             remote(text_src.at[(me + half + 1) % count], inbox.at[half], text_send.at[half], text_recv.at[half], left)]
    for copy in sends:
        copy.start()
    for step in range(1, half):
        chains = ((step, (me + half - step) % count, right), (half + step, (me + half + 1 + step) % count, left))
        for slot, target, device in chains:
            if slot >= count - 1:
                continue
            remote(inbox.at[slot - 1], inbox.at[slot - 1], text_send.at[slot], text_recv.at[slot - 1], device).wait_recv()
            outbox[slot] = inbox[slot - 1] + text_src[target]
            copy = remote(outbox.at[slot], inbox.at[slot], text_send.at[slot], text_recv.at[slot], device)
            copy.start()
            sends.append(copy)
    last_right, last_left = half - 1, count - 2
    for slot in (last_right, last_left):
        remote(inbox.at[slot], inbox.at[slot], text_send.at[0], text_recv.at[slot], right).wait_recv()
    text_out[...] = text_src[me] + inbox[last_right] + inbox[last_left]
    for copy in sends:
        copy.wait_send()
    lax.fori_loop(1, image_count, finish, 0)


def merged_reduce_kernel(image_axes, image_src, text_src, image_out, text_out, image_send, image_recv, text_send,
                         text_recv, inbox, outbox, halfbox, summed, half_sems):
    image_count, image_me = group_size(image_axes), linear_index(image_axes)
    count, me, right, left = ring_peers()
    right2 = member(TEXT_AXES, (me + 2) % count)
    left2 = member(TEXT_AXES, (me + count - 2) % count)
    core = linear_index(CORE_AXES)
    partner = member(CORE_AXES, 1 - core)
    greet_all(image_axes, pltpu.get_barrier_semaphore(), image_count, image_me, right, left, (right2, left2, partner))
    chains = (
        (0, 4, lambda step: right2, lambda step: 10 - 2 * step),
        (4, 4, lambda step: right2 if step < 4 else right, lambda step: 9 - 2 * step),
        (8, 3, lambda step: left2, lambda step: 2 * step - 8),
        (11, 4, lambda step: left2 if step < 4 else left, lambda step: 2 * step - 9),
    )
    sends = []

    def step_sends(step):
        for base, steps, device, offset in chains:
            if step > steps:
                continue
            slot = base + step - 1
            target = (me + count + offset(step)) % count
            if step == 1:
                source = text_src.at[target]
            else:
                remote(inbox.at[slot - 1], inbox.at[slot - 1], text_send.at[slot], text_recv.at[slot - 1],
                       right).wait_recv()
                outbox[slot] = inbox[slot - 1] + text_src[target]
                source = outbox.at[slot]
            copy = remote(source, inbox.at[slot], text_send.at[slot], text_recv.at[slot], device(step))
            copy.start()
            sends.append(copy)

    swap = remote(image_src.at[1 - core], halfbox, half_sems.at[0], half_sems.at[1], partner)
    swap.start()
    step_sends(1)
    step_sends(2)
    swap.wait_recv()
    summed[...] = image_src[core] + halfbox[...]
    finish = image_direct(image_axes, True, summed, image_out, image_send, image_recv, image_count, image_me)
    for step in range(3, 5):
        step_sends(step)
    finals = (3, 7, 10, 14)
    for slot in finals:
        remote(inbox.at[slot], inbox.at[slot], text_send.at[0], text_recv.at[slot], right).wait_recv()
    text_out[...] = text_src[me] + inbox[finals[0]] + inbox[finals[1]] + inbox[finals[2]] + inbox[finals[3]]
    for copy in sends:
        copy.wait_send()
    swap.wait_send()
    lax.fori_loop(1, image_count, finish, 0)


def merged_reduce(image_axes, image_src, text_src, tag):
    image_count, text_count = group_size(image_axes), group_size(TEXT_AXES)
    image_shape = image_src.shape[1:]
    block = text_src.shape[1:]
    vmem = pl.BlockSpec(memory_space=pltpu.VMEM)
    scratch = [
        pltpu.SemaphoreType.DMA((image_count,)),
        pltpu.SemaphoreType.DMA((image_count,)),
        pltpu.SemaphoreType.DMA((text_count,)),
        pltpu.SemaphoreType.DMA((text_count,)),
        pltpu.VMEM((text_count,) + block, text_src.dtype),
        pltpu.VMEM((text_count,) + block, text_src.dtype),
        pltpu.VMEM(image_shape, image_src.dtype),
        pltpu.VMEM(image_shape, image_src.dtype),
        pltpu.SemaphoreType.DMA((2,)),
    ]
    return pl.pallas_call(
        functools.partial(merged_reduce_kernel, image_axes),
        out_shape=(jax.ShapeDtypeStruct(image_shape, image_src.dtype), jax.ShapeDtypeStruct(block, text_src.dtype)),
        in_specs=[vmem, vmem],
        out_specs=(vmem, vmem),
        scratch_shapes=scratch,
        compiler_params=pltpu.CompilerParams(collective_id=tag, has_side_effects=True),
    )(image_src, text_src)


def gather_compute(image_axes, image_src, text_src, scale, shift, tag):
    image_count, text_count = group_size(image_axes), group_size(TEXT_AXES)
    rows, width = image_src.shape
    vmem = pl.BlockSpec(memory_space=pltpu.VMEM)
    scratch = [
        pltpu.SemaphoreType.DMA((image_count,)),
        pltpu.SemaphoreType.DMA((image_count,)),
        pltpu.SemaphoreType.DMA((text_count,)),
        pltpu.SemaphoreType.DMA((text_count,)),
        pltpu.VMEM((image_count,) + image_src.shape, jnp.bfloat16),
        pltpu.VMEM((text_count,) + text_src.shape, jnp.bfloat16),
        pltpu.VMEM(image_src.shape, jnp.bfloat16),
        pltpu.VMEM(text_src.shape, jnp.bfloat16),
    ]
    return pl.pallas_call(
        functools.partial(gather_kernel, image_axes),
        out_shape=(
            jax.ShapeDtypeStruct((image_count * rows, width + LOSS_LANES), jnp.float32),
            jax.ShapeDtypeStruct((text_count * rows, width), jnp.float32),
            jax.ShapeDtypeStruct((rows, width), jnp.float32),
            jax.ShapeDtypeStruct((rows, LOSS_LANES), jnp.float32),
            jax.ShapeDtypeStruct((rows, width), jnp.float32),
            jax.ShapeDtypeStruct((rows, LOSS_LANES), jnp.float32),
        ),
        in_specs=[vmem] * 4,
        out_specs=tuple([vmem] * 6),
        scratch_shapes=scratch,
        compiler_params=pltpu.CompilerParams(collective_id=tag, has_side_effects=True),
    )(image_src, text_src, scale.reshape(1, 1), shift.reshape(1, 1))


def exchange(image_axes, image_src, text_src, scatter, tag):
    image_count, text_count = group_size(image_axes), group_size(TEXT_AXES)
    image_shape = image_src.shape if scatter else (image_count,) + image_src.shape
    text_shape = text_src.shape[1:] if scatter else (text_count,) + text_src.shape
    block = text_src.shape[1:] if scatter else text_src.shape
    vmem = pl.BlockSpec(memory_space=pltpu.VMEM)
    scratch = [
        pltpu.SemaphoreType.DMA((image_count,)),
        pltpu.SemaphoreType.DMA((image_count,)),
        pltpu.SemaphoreType.DMA((text_count,)),
        pltpu.SemaphoreType.DMA((text_count,)),
    ]
    if scatter:
        scratch += [pltpu.VMEM((text_count,) + block, text_src.dtype)] * 2
    return pl.pallas_call(
        functools.partial(reduce_kernel if scatter else gather_kernel, image_axes),
        out_shape=(jax.ShapeDtypeStruct(image_shape, image_src.dtype), jax.ShapeDtypeStruct(text_shape, text_src.dtype)),
        in_specs=[vmem, vmem],
        out_specs=(vmem, vmem),
        scratch_shapes=scratch,
        compiler_params=pltpu.CompilerParams(collective_id=tag, has_side_effects=True),
    )(image_src, text_src)


def pair_kernel(plan, *refs):
    count_groups = len(plan)
    srcs, outs = refs[:count_groups], refs[count_groups:2 * count_groups]
    sems = refs[2 * count_groups:]
    groups = [
        (axes, scatter, srcs[g], outs[g], sems[2 * g], sems[2 * g + 1]) for g, (axes, scatter) in enumerate(plan)
    ]
    barrier = pltpu.get_barrier_semaphore()
    peers = 0
    for axes, scatter, src, out, send, recv in groups:
        count, me = group_size(axes), linear_index(axes)
        peers += count - 1

        def greet(step, carry, axes=axes, count=count, me=me):
            pl.semaphore_signal(barrier, 1, device_id=member(axes, (me + step) % count), device_id_type=MESH_IDS)
            return carry

        lax.fori_loop(1, count, greet, 0)
    pl.semaphore_wait(barrier, peers)

    for axes, scatter, src, out, send, recv in groups:
        count, me = group_size(axes), linear_index(axes)

        def start(step, carry, axes=axes, scatter=scatter, count=count, me=me, src=src, out=out, send=send, recv=recv):
            peer = (me + step) % count
            pltpu.make_async_remote_copy(
                src.at[peer] if scatter else src, out.at[me], send.at[peer], recv.at[me],
                device_id=member(axes, peer), device_id_type=MESH_IDS,
            ).start()
            return carry

        lax.fori_loop(1, count, start, 0)

    for axes, scatter, src, out, send, recv in groups:
        count, me = group_size(axes), linear_index(axes)
        out[me] = src[me] if scatter else src[...]

    for axes, scatter, src, out, send, recv in groups:
        count, me = group_size(axes), linear_index(axes)

        def finish(step, carry, axes=axes, scatter=scatter, count=count, me=me, src=src, out=out, send=send, recv=recv):
            peer = (me + step) % count
            copy = pltpu.make_async_remote_copy(
                src.at[peer] if scatter else src, out.at[peer], send.at[peer], recv.at[peer],
                device_id=member(axes, peer), device_id_type=MESH_IDS,
            )
            copy.wait_send()
            copy.wait_recv()
            return carry

        lax.fori_loop(1, count, finish, 0)


def pair_exchange(routes, tag):
    plan = tuple((axes, scatter) for axes, src, scatter in routes)
    srcs = [src for axes, src, scatter in routes]
    shapes = [
        jax.ShapeDtypeStruct(src.shape if scatter else (group_size(axes),) + src.shape, src.dtype)
        for axes, src, scatter in routes
    ]
    sems = []
    for axes, src, scatter in routes:
        sems += [pltpu.SemaphoreType.DMA((group_size(axes),))] * 2
    vmem = pl.BlockSpec(memory_space=pltpu.VMEM)
    return pl.pallas_call(
        functools.partial(pair_kernel, plan),
        out_shape=tuple(shapes),
        in_specs=[vmem] * len(routes),
        out_specs=tuple([vmem] * len(routes)),
        scratch_shapes=sems,
        compiler_params=pltpu.CompilerParams(collective_id=tag, has_side_effects=True),
    )(*srcs)


def local(images, texts, scale, shift):
    rows, width = images.shape
    chips = group_size(CHIP_AXES)
    cores = group_size(CORE_AXES)
    text_count = group_size(TEXT_AXES)
    image_part, text_part, image_unit, image_norm, text_unit, text_norm = gather_compute(
        CORE_AXES + CHIP_AXES, images, texts, scale, shift, 0
    )
    image_norm = image_norm[:, :1]
    text_norm = text_norm[:, :1]
    image_in, text_in = merged_reduce(
        CHIP_AXES, image_part.reshape(cores, chips, rows, width + LOSS_LANES), text_part.reshape(text_count, rows, width), 3
    )
    image_in = jnp.sum(image_in, 0)
    text_sum = text_in
    image_grad = back_rows(image_in[:, :width], image_unit, image_norm)
    text_grad = back_rows(text_sum, text_unit, text_norm)
    return (image_in[:, width], image_grad, text_grad)


def solution(mesh):
    blk, grp = mesh.devices.shape
    fine = Mesh(mesh.devices.reshape(blk // 2, 2, grp // 16, 8, 2), ROWS_AXES)
    in_specs = (P(ROWS_AXES, None), P(ROWS_AXES, None), P(), P())
    out_specs = (P(ROWS_AXES), P(ROWS_AXES, None), P(ROWS_AXES, None))
    return jax.shard_map(local, mesh=fine, in_specs=in_specs, out_specs=out_specs, check_vma=False)
```

```python
import functools

import jax
import jax.numpy as jnp
from jax import lax
from jax.experimental import pallas as pl
from jax.experimental.pallas import tpu as pltpu
from jax.sharding import Mesh, PartitionSpec as P

ROWS_AXES = ("x", "zh", "y", "zl", "c")
CHIP_AXES = ("x", "y")
CORE_AXES = ("c",)
TEXT_AXES = ("zh", "zl")
MESH_IDS = pl.DeviceIdType.MESH
LOSS_LANES = 128


def unit_rows(values):
    floats = values.astype(jnp.float32)
    norms = jnp.sqrt(jnp.sum(floats * floats, 1, keepdims=True) + 1e-06)
    return (floats / norms, norms)


def back_rows(grads, units, norms):
    return (grads - units * jnp.sum(units * grads, 1, keepdims=True)) / norms


def linear_index(axes):
    index = 0
    for name in axes:
        index = index * lax.axis_size(name) + lax.axis_index(name)
    return index


def group_size(axes):
    size = 1
    for name in axes:
        size *= lax.axis_size(name)
    return size


def member(axes, k):
    coords = {}
    for name in reversed(axes):
        size = lax.axis_size(name)
        coords[name] = k % size
        k = k // size
    return tuple(coords[name] if name in coords else lax.axis_index(name) for name in ROWS_AXES)


def ring_peers():
    count, me = group_size(TEXT_AXES), linear_index(TEXT_AXES)
    return count, me, member(TEXT_AXES, (me + 1) % count), member(TEXT_AXES, (me + count - 1) % count)


def remote(src, dst, send, recv, device):
    return pltpu.make_async_remote_copy(src, dst, send, recv, device_id=device, device_id_type=MESH_IDS)


def greet_all(image_axes, barrier, image_count, image_me, right, left, extra=()):
    def greet(step, carry):
        pl.semaphore_signal(barrier, 1, device_id=member(image_axes, (image_me + step) % image_count),
                            device_id_type=MESH_IDS)
        return carry

    lax.fori_loop(1, image_count, greet, 0)
    for device in (right, left) + tuple(extra):
        pl.semaphore_signal(barrier, 1, device_id=device, device_id_type=MESH_IDS)
    pl.semaphore_wait(barrier, image_count + 1 + len(extra))


def image_direct(image_axes, scatter, src, out, send, recv, count, me):
    def start(step, carry):
        peer = (me + step) % count
        remote(src.at[peer] if scatter else src, out.at[me], send.at[peer], recv.at[me],
               member(image_axes, peer)).start()
        return carry

    lax.fori_loop(1, count, start, 0)
    out[me] = src[me] if scatter else src[...]

    def finish(step, carry):
        peer = (me + step) % count
        copy = remote(src.at[peer] if scatter else src, out.at[peer], send.at[peer], recv.at[peer],
                      member(image_axes, peer))
        copy.wait_send()
        copy.wait_recv()
        return carry

    return finish


def gather_kernel(image_axes, image_raw, text_raw, scale_ref, shift_ref, image_part_out, text_part_out,
                  image_unit_out, image_norm_out, text_unit_out, text_norm_out, image_send, image_recv, text_send,
                  text_recv, image_out, text_out, image_src, text_src):
    for raw, unit_out, norm_out, emb in ((image_raw, image_unit_out, image_norm_out, image_src),
                                         (text_raw, text_unit_out, text_norm_out, text_src)):
        floats = raw[...].astype(jnp.float32)
        norms = jnp.sqrt(jnp.sum(floats * floats, 1, keepdims=True) + 1e-06)
        units = floats / norms
        unit_out[...] = units
        norm_out[...] = jnp.broadcast_to(norms, norm_out.shape)
        emb[...] = units.astype(jnp.bfloat16)
    image_count, image_me = group_size(image_axes), linear_index(image_axes)
    count, me, right, left = ring_peers()
    right2 = member(TEXT_AXES, (me + 2) % count)
    left2 = member(TEXT_AXES, (me + count - 2) % count)
    greet_all(image_axes, pltpu.get_barrier_semaphore(), image_count, image_me, right, left, (right2, left2))
    finish = image_direct(image_axes, False, image_src, image_out, image_send, image_recv, image_count, image_me)
    sends = []

    def send(src, origin, device, slot):
        copy = remote(src, text_out.at[origin], text_send.at[slot], text_recv.at[origin], device)
        copy.start()
        sends.append(copy)

    def arrive(origin):
        remote(text_out.at[origin], text_out.at[origin], text_send.at[0], text_recv.at[origin], right).wait_recv()

    half = count // 2
    for slot, device in ((0, right), (1, right2), (half, left), (half + 1, left2)):
        send(text_src, me, device, slot)
    text_out[me] = text_src[...]
    slot_right, slot_left = 2, half + 2
    for step in range(2, half // 2 + 1):
        for distance in (2 * step - 3, 2 * step - 2):
            origin = (me + count - distance) % count
            arrive(origin)
            send(text_out.at[origin], origin, right2, slot_right)
            slot_right += 1
        for distance in (2 * step - 3, 2 * step - 2):
            if distance > half - 3:
                continue
            origin = (me + distance) % count
            arrive(origin)
            send(text_out.at[origin], origin, left2, slot_left)
            slot_left += 1
    for distance in (half - 1, half):
        arrive((me + count - distance) % count)
    for distance in (half - 2, half - 1):
        arrive((me + distance) % count)
    for copy in sends:
        copy.wait_send()
    lax.fori_loop(1, image_count, finish, 0)
    rows, width = image_src.shape
    gathered = image_out[...].reshape(image_count * rows, width)
    seen = text_out[...].reshape(count * rows, width)
    scale, shift = scale_ref[...], shift_ref[...]
    shape = (image_count * rows, count * rows)
    image_ids = lax.broadcasted_iota(jnp.int32, shape, 0)
    text_ids = lax.broadcasted_iota(jnp.int32, shape, 1)
    label = ((image_ids - text_ids == (image_me - me) * rows) & (text_ids // rows == me)).astype(jnp.float32)
    logit = scale * lax.dot_general(gathered, seen, (((1,), (1,)), ((), ())), preferred_element_type=jnp.float32) + shift
    total = image_count * count * rows
    loss = jnp.sum(jax.nn.softplus(logit * (1.0 - 2.0 * label)), 1, keepdims=True) / total
    coef = ((jax.nn.sigmoid(logit) - label) * scale).astype(jnp.bfloat16)
    image_part_out[:, :width] = jnp.dot(coef, seen, preferred_element_type=jnp.float32)
    image_part_out[:, width:] = jnp.broadcast_to(loss, (image_count * rows, LOSS_LANES))
    shape_t = (count * rows, image_count * rows)
    text_ids_t = lax.broadcasted_iota(jnp.int32, shape_t, 0)
    image_ids_t = lax.broadcasted_iota(jnp.int32, shape_t, 1)
    label_t = ((image_ids_t - text_ids_t == (image_me - me) * rows) & (text_ids_t // rows == me)).astype(jnp.float32)
    logit_t = scale * lax.dot_general(seen, gathered, (((1,), (1,)), ((), ())), preferred_element_type=jnp.float32) + shift
    coef_t = ((jax.nn.sigmoid(logit_t) - label_t) * scale).astype(jnp.bfloat16)
    text_part_out[...] = jnp.dot(coef_t, gathered, preferred_element_type=jnp.float32)


def reduce_kernel(image_axes, image_src, text_src, image_out, text_out, image_send, image_recv, text_send, text_recv,
                  inbox, outbox):
    image_count, image_me = group_size(image_axes), linear_index(image_axes)
    count, me, right, left = ring_peers()
    half = count // 2
    greet_all(image_axes, pltpu.get_barrier_semaphore(), image_count, image_me, right, left)
    finish = image_direct(image_axes, True, image_src, image_out, image_send, image_recv, image_count, image_me)
    sends = [remote(text_src.at[(me + half) % count], inbox.at[0], text_send.at[0], text_recv.at[0], right),
             remote(text_src.at[(me + half + 1) % count], inbox.at[half], text_send.at[half], text_recv.at[half], left)]
    for copy in sends:
        copy.start()
    for step in range(1, half):
        chains = ((step, (me + half - step) % count, right), (half + step, (me + half + 1 + step) % count, left))
        for slot, target, device in chains:
            if slot >= count - 1:
                continue
            remote(inbox.at[slot - 1], inbox.at[slot - 1], text_send.at[slot], text_recv.at[slot - 1], device).wait_recv()
            outbox[slot] = inbox[slot - 1] + text_src[target]
            copy = remote(outbox.at[slot], inbox.at[slot], text_send.at[slot], text_recv.at[slot], device)
            copy.start()
            sends.append(copy)
    last_right, last_left = half - 1, count - 2
    for slot in (last_right, last_left):
        remote(inbox.at[slot], inbox.at[slot], text_send.at[0], text_recv.at[slot], right).wait_recv()
    text_out[...] = text_src[me] + inbox[last_right] + inbox[last_left]
    for copy in sends:
        copy.wait_send()
    lax.fori_loop(1, image_count, finish, 0)


def merged_reduce_kernel(image_axes, image_src, text_src, image_out, text_out, image_send, image_recv, text_send,
                         text_recv, inbox, outbox, halfbox, summed, half_sems):
    image_count, image_me = group_size(image_axes), linear_index(image_axes)
    count, me, right, left = ring_peers()
    right2 = member(TEXT_AXES, (me + 2) % count)
    left2 = member(TEXT_AXES, (me + count - 2) % count)
    core = linear_index(CORE_AXES)
    partner = member(CORE_AXES, 1 - core)
    greet_all(image_axes, pltpu.get_barrier_semaphore(), image_count, image_me, right, left, (right2, left2, partner))
    chains = (
        (0, 4, lambda step: right2, lambda step: 10 - 2 * step),
        (4, 4, lambda step: right2 if step < 4 else right, lambda step: 9 - 2 * step),
        (8, 3, lambda step: left2, lambda step: 2 * step - 8),
        (11, 4, lambda step: left2 if step < 4 else left, lambda step: 2 * step - 9),
    )
    sends = []

    def step_sends(step):
        for base, steps, device, offset in chains:
            if step > steps:
                continue
            slot = base + step - 1
            target = (me + count + offset(step)) % count
            if step == 1:
                source = text_src.at[target]
            else:
                remote(inbox.at[slot - 1], inbox.at[slot - 1], text_send.at[slot], text_recv.at[slot - 1],
                       right).wait_recv()
                outbox[slot] = inbox[slot - 1] + text_src[target]
                source = outbox.at[slot]
            copy = remote(source, inbox.at[slot], text_send.at[slot], text_recv.at[slot], device(step))
            copy.start()
            sends.append(copy)

    swap = remote(image_src.at[1 - core], halfbox, half_sems.at[0], half_sems.at[1], partner)
    swap.start()
    step_sends(1)
    step_sends(2)
    swap.wait_recv()
    summed[...] = image_src[core] + halfbox[...]
    finish = image_direct(image_axes, True, summed, image_out, image_send, image_recv, image_count, image_me)
    for step in range(3, 5):
        step_sends(step)
    finals = (3, 7, 10, 14)
    for slot in finals:
        remote(inbox.at[slot], inbox.at[slot], text_send.at[0], text_recv.at[slot], right).wait_recv()
    text_out[...] = text_src[me] + inbox[finals[0]] + inbox[finals[1]] + inbox[finals[2]] + inbox[finals[3]]
    for copy in sends:
        copy.wait_send()
    swap.wait_send()
    lax.fori_loop(1, image_count, finish, 0)


def merged_reduce(image_axes, image_src, text_src, tag):
    image_count, text_count = group_size(image_axes), group_size(TEXT_AXES)
    image_shape = image_src.shape[1:]
    block = text_src.shape[1:]
    vmem = pl.BlockSpec(memory_space=pltpu.VMEM)
    scratch = [
        pltpu.SemaphoreType.DMA((image_count,)),
        pltpu.SemaphoreType.DMA((image_count,)),
        pltpu.SemaphoreType.DMA((text_count,)),
        pltpu.SemaphoreType.DMA((text_count,)),
        pltpu.VMEM((text_count,) + block, text_src.dtype),
        pltpu.VMEM((text_count,) + block, text_src.dtype),
        pltpu.VMEM(image_shape, image_src.dtype),
        pltpu.VMEM(image_shape, image_src.dtype),
        pltpu.SemaphoreType.DMA((2,)),
    ]
    return pl.pallas_call(
        functools.partial(merged_reduce_kernel, image_axes),
        out_shape=(jax.ShapeDtypeStruct(image_shape, image_src.dtype), jax.ShapeDtypeStruct(block, text_src.dtype)),
        in_specs=[vmem, vmem],
        out_specs=(vmem, vmem),
        scratch_shapes=scratch,
        compiler_params=pltpu.CompilerParams(collective_id=tag, has_side_effects=True),
    )(image_src, text_src)


def gather_compute(image_axes, image_src, text_src, scale, shift, tag):
    image_count, text_count = group_size(image_axes), group_size(TEXT_AXES)
    rows, width = image_src.shape
    vmem = pl.BlockSpec(memory_space=pltpu.VMEM)
    scratch = [
        pltpu.SemaphoreType.DMA((image_count,)),
        pltpu.SemaphoreType.DMA((image_count,)),
        pltpu.SemaphoreType.DMA((text_count,)),
        pltpu.SemaphoreType.DMA((text_count,)),
        pltpu.VMEM((image_count,) + image_src.shape, jnp.bfloat16),
        pltpu.VMEM((text_count,) + text_src.shape, jnp.bfloat16),
        pltpu.VMEM(image_src.shape, jnp.bfloat16),
        pltpu.VMEM(text_src.shape, jnp.bfloat16),
    ]
    return pl.pallas_call(
        functools.partial(gather_kernel, image_axes),
        out_shape=(
            jax.ShapeDtypeStruct((image_count * rows, width + LOSS_LANES), jnp.float32),
            jax.ShapeDtypeStruct((text_count * rows, width), jnp.float32),
            jax.ShapeDtypeStruct((rows, width), jnp.float32),
            jax.ShapeDtypeStruct((rows, LOSS_LANES), jnp.float32),
            jax.ShapeDtypeStruct((rows, width), jnp.float32),
            jax.ShapeDtypeStruct((rows, LOSS_LANES), jnp.float32),
        ),
        in_specs=[vmem] * 4,
        out_specs=tuple([vmem] * 6),
        scratch_shapes=scratch,
        compiler_params=pltpu.CompilerParams(collective_id=tag, has_side_effects=True),
    )(image_src, text_src, scale.reshape(1, 1), shift.reshape(1, 1))


def exchange(image_axes, image_src, text_src, scatter, tag):
    image_count, text_count = group_size(image_axes), group_size(TEXT_AXES)
    image_shape = image_src.shape if scatter else (image_count,) + image_src.shape
    text_shape = text_src.shape[1:] if scatter else (text_count,) + text_src.shape
    block = text_src.shape[1:] if scatter else text_src.shape
    vmem = pl.BlockSpec(memory_space=pltpu.VMEM)
    scratch = [
        pltpu.SemaphoreType.DMA((image_count,)),
        pltpu.SemaphoreType.DMA((image_count,)),
        pltpu.SemaphoreType.DMA((text_count,)),
        pltpu.SemaphoreType.DMA((text_count,)),
    ]
    if scatter:
        scratch += [pltpu.VMEM((text_count,) + block, text_src.dtype)] * 2
    return pl.pallas_call(
        functools.partial(reduce_kernel if scatter else gather_kernel, image_axes),
        out_shape=(jax.ShapeDtypeStruct(image_shape, image_src.dtype), jax.ShapeDtypeStruct(text_shape, text_src.dtype)),
        in_specs=[vmem, vmem],
        out_specs=(vmem, vmem),
        scratch_shapes=scratch,
        compiler_params=pltpu.CompilerParams(collective_id=tag, has_side_effects=True),
    )(image_src, text_src)


def pair_kernel(plan, *refs):
    count_groups = len(plan)
    srcs, outs = refs[:count_groups], refs[count_groups:2 * count_groups]
    sems = refs[2 * count_groups:]
    groups = [
        (axes, scatter, srcs[g], outs[g], sems[2 * g], sems[2 * g + 1]) for g, (axes, scatter) in enumerate(plan)
    ]
    barrier = pltpu.get_barrier_semaphore()
    peers = 0
    for axes, scatter, src, out, send, recv in groups:
        count, me = group_size(axes), linear_index(axes)
        peers += count - 1

        def greet(step, carry, axes=axes, count=count, me=me):
            pl.semaphore_signal(barrier, 1, device_id=member(axes, (me + step) % count), device_id_type=MESH_IDS)
            return carry

        lax.fori_loop(1, count, greet, 0)
    pl.semaphore_wait(barrier, peers)

    for axes, scatter, src, out, send, recv in groups:
        count, me = group_size(axes), linear_index(axes)

        def start(step, carry, axes=axes, scatter=scatter, count=count, me=me, src=src, out=out, send=send, recv=recv):
            peer = (me + step) % count
            pltpu.make_async_remote_copy(
                src.at[peer] if scatter else src, out.at[me], send.at[peer], recv.at[me],
                device_id=member(axes, peer), device_id_type=MESH_IDS,
            ).start()
            return carry

        lax.fori_loop(1, count, start, 0)

    for axes, scatter, src, out, send, recv in groups:
        count, me = group_size(axes), linear_index(axes)
        out[me] = src[me] if scatter else src[...]

    for axes, scatter, src, out, send, recv in groups:
        count, me = group_size(axes), linear_index(axes)

        def finish(step, carry, axes=axes, scatter=scatter, count=count, me=me, src=src, out=out, send=send, recv=recv):
            peer = (me + step) % count
            copy = pltpu.make_async_remote_copy(
                src.at[peer] if scatter else src, out.at[peer], send.at[peer], recv.at[peer],
                device_id=member(axes, peer), device_id_type=MESH_IDS,
            )
            copy.wait_send()
            copy.wait_recv()
            return carry

        lax.fori_loop(1, count, finish, 0)


def pair_exchange(routes, tag):
    plan = tuple((axes, scatter) for axes, src, scatter in routes)
    srcs = [src for axes, src, scatter in routes]
    shapes = [
        jax.ShapeDtypeStruct(src.shape if scatter else (group_size(axes),) + src.shape, src.dtype)
        for axes, src, scatter in routes
    ]
    sems = []
    for axes, src, scatter in routes:
        sems += [pltpu.SemaphoreType.DMA((group_size(axes),))] * 2
    vmem = pl.BlockSpec(memory_space=pltpu.VMEM)
    return pl.pallas_call(
        functools.partial(pair_kernel, plan),
        out_shape=tuple(shapes),
        in_specs=[vmem] * len(routes),
        out_specs=tuple([vmem] * len(routes)),
        scratch_shapes=sems,
        compiler_params=pltpu.CompilerParams(collective_id=tag, has_side_effects=True),
    )(*srcs)


def local(images, texts, scale, shift):
    rows, width = images.shape
    chips = group_size(CHIP_AXES)
    cores = group_size(CORE_AXES)
    text_count = group_size(TEXT_AXES)
    image_part, text_part, image_unit, image_norm, text_unit, text_norm = gather_compute(
        CORE_AXES + CHIP_AXES, images, texts, scale, shift, 0
    )
    image_norm = image_norm[:, :1]
    text_norm = text_norm[:, :1]
    image_in, text_in = merged_reduce(
        CHIP_AXES, image_part.reshape(cores, chips, rows, width + LOSS_LANES), text_part.reshape(text_count, rows, width), 3
    )
    image_in = jnp.sum(image_in, 0)
    text_sum = text_in
    image_grad = back_rows(image_in[:, :width], image_unit, image_norm)
    text_grad = back_rows(text_sum, text_unit, text_norm)
    return (image_in[:, width], image_grad, text_grad)


def solution(mesh):
    blk, grp = mesh.devices.shape
    fine = Mesh(mesh.devices.reshape(blk // 2, 2, grp // 16, 8, 2), ROWS_AXES)
    in_specs = (P(ROWS_AXES, None), P(ROWS_AXES, None), P(), P())
    out_specs = (P(ROWS_AXES), P(ROWS_AXES, None), P(ROWS_AXES, None))
    return jax.shard_map(local, mesh=fine, in_specs=in_specs, out_specs=out_specs, check_vma=False)
```

```python
import functools

import jax
import jax.numpy as jnp
from jax import lax
from jax.experimental import pallas as pl
from jax.experimental.pallas import tpu as pltpu
from jax.sharding import Mesh, PartitionSpec as P

ROWS_AXES = ("x", "zh", "y", "zl", "c")
CHIP_AXES = ("x", "y")
CORE_AXES = ("c",)
TEXT_AXES = ("zh", "zl")
MESH_IDS = pl.DeviceIdType.MESH
LOSS_LANES = 128


def unit_rows(values):
    floats = values.astype(jnp.float32)
    norms = jnp.sqrt(jnp.sum(floats * floats, 1, keepdims=True) + 1e-06)
    return (floats / norms, norms)


def back_rows(grads, units, norms):
    return (grads - units * jnp.sum(units * grads, 1, keepdims=True)) / norms


def linear_index(axes):
    index = 0
    for name in axes:
        index = index * lax.axis_size(name) + lax.axis_index(name)
    return index


def group_size(axes):
    size = 1
    for name in axes:
        size *= lax.axis_size(name)
    return size


def member(axes, k):
    coords = {}
    for name in reversed(axes):
        size = lax.axis_size(name)
        coords[name] = k % size
        k = k // size
    return tuple(coords[name] if name in coords else lax.axis_index(name) for name in ROWS_AXES)


def ring_peers():
    count, me = group_size(TEXT_AXES), linear_index(TEXT_AXES)
    return count, me, member(TEXT_AXES, (me + 1) % count), member(TEXT_AXES, (me + count - 1) % count)


def remote(src, dst, send, recv, device):
    return pltpu.make_async_remote_copy(src, dst, send, recv, device_id=device, device_id_type=MESH_IDS)


def greet_all(image_axes, barrier, image_count, image_me, right, left, extra=()):
    def greet(step, carry):
        pl.semaphore_signal(barrier, 1, device_id=member(image_axes, (image_me + step) % image_count),
                            device_id_type=MESH_IDS)
        return carry

    lax.fori_loop(1, image_count, greet, 0)
    for device in (right, left) + tuple(extra):
        pl.semaphore_signal(barrier, 1, device_id=device, device_id_type=MESH_IDS)
    pl.semaphore_wait(barrier, image_count + 1 + len(extra))


def image_direct(image_axes, scatter, src, out, send, recv, count, me):
    def start(step, carry):
        peer = (me + step) % count
        remote(src.at[peer] if scatter else src, out.at[me], send.at[peer], recv.at[me],
               member(image_axes, peer)).start()
        return carry

    lax.fori_loop(1, count, start, 0)
    out[me] = src[me] if scatter else src[...]

    def finish(step, carry):
        peer = (me + step) % count
        copy = remote(src.at[peer] if scatter else src, out.at[peer], send.at[peer], recv.at[peer],
                      member(image_axes, peer))
        copy.wait_send()
        copy.wait_recv()
        return carry

    return finish


def gather_kernel(image_axes, image_raw, text_raw, scale_ref, shift_ref, image_part_out, text_part_out,
                  image_unit_out, image_norm_out, text_unit_out, text_norm_out, image_send, image_recv, text_send,
                  text_recv, image_out, text_out, image_src, text_src):
    for raw, unit_out, norm_out, emb in ((image_raw, image_unit_out, image_norm_out, image_src),
                                         (text_raw, text_unit_out, text_norm_out, text_src)):
        floats = raw[...].astype(jnp.float32)
        norms = jnp.sqrt(jnp.sum(floats * floats, 1, keepdims=True) + 1e-06)
        units = floats / norms
        unit_out[...] = units
        norm_out[...] = jnp.broadcast_to(norms, norm_out.shape)
        emb[...] = units.astype(jnp.bfloat16)
    image_count, image_me = group_size(image_axes), linear_index(image_axes)
    count, me, right, left = ring_peers()
    right2 = member(TEXT_AXES, (me + 2) % count)
    left2 = member(TEXT_AXES, (me + count - 2) % count)
    greet_all(image_axes, pltpu.get_barrier_semaphore(), image_count, image_me, right, left, (right2, left2))
    finish = image_direct(image_axes, False, image_src, image_out, image_send, image_recv, image_count, image_me)
    sends = []

    def send(src, origin, device, slot):
        copy = remote(src, text_out.at[origin], text_send.at[slot], text_recv.at[origin], device)
        copy.start()
        sends.append(copy)

    def arrive(origin):
        remote(text_out.at[origin], text_out.at[origin], text_send.at[0], text_recv.at[origin], right).wait_recv()

    half = count // 2
    for slot, device in ((0, right), (1, right2), (half, left), (half + 1, left2)):
        send(text_src, me, device, slot)
    text_out[me] = text_src[...]
    slot_right, slot_left = 2, half + 2
    for step in range(2, half // 2 + 1):
        for distance in (2 * step - 3, 2 * step - 2):
            origin = (me + count - distance) % count
            arrive(origin)
            send(text_out.at[origin], origin, right2, slot_right)
            slot_right += 1
        for distance in (2 * step - 3, 2 * step - 2):
            if distance > half - 3:
                continue
            origin = (me + distance) % count
            arrive(origin)
            send(text_out.at[origin], origin, left2, slot_left)
            slot_left += 1
    for distance in (half - 1, half):
        arrive((me + count - distance) % count)
    for distance in (half - 2, half - 1):
        arrive((me + distance) % count)
    for copy in sends:
        copy.wait_send()
    lax.fori_loop(1, image_count, finish, 0)
    rows, width = image_src.shape
    gathered = image_out[...].reshape(image_count * rows, width)
    seen = text_out[...].reshape(count * rows, width)
    scale, shift = scale_ref[...], shift_ref[...]
    shape = (image_count * rows, count * rows)
    image_ids = lax.broadcasted_iota(jnp.int32, shape, 0)
    text_ids = lax.broadcasted_iota(jnp.int32, shape, 1)
    label = ((image_ids // rows == image_me) & (text_ids // rows == me) & (image_ids % rows == text_ids % rows)).astype(
        jnp.float32)
    logit = scale * lax.dot_general(gathered, seen, (((1,), (1,)), ((), ())), preferred_element_type=jnp.float32) + shift
    total = image_count * count * rows
    loss = jnp.sum(jax.nn.softplus(logit * (1.0 - 2.0 * label)), 1, keepdims=True) / total
    coef = ((jax.nn.sigmoid(logit) - label) * scale).astype(jnp.bfloat16)
    image_part_out[:, :width] = jnp.dot(coef, seen, preferred_element_type=jnp.float32)
    image_part_out[:, width:] = jnp.broadcast_to(loss, (image_count * rows, LOSS_LANES))
    shape_t = (count * rows, image_count * rows)
    text_ids_t = lax.broadcasted_iota(jnp.int32, shape_t, 0)
    image_ids_t = lax.broadcasted_iota(jnp.int32, shape_t, 1)
    label_t = ((image_ids_t // rows == image_me) & (text_ids_t // rows == me)
               & (image_ids_t % rows == text_ids_t % rows)).astype(jnp.float32)
    logit_t = scale * lax.dot_general(seen, gathered, (((1,), (1,)), ((), ())), preferred_element_type=jnp.float32) + shift
    coef_t = ((jax.nn.sigmoid(logit_t) - label_t) * scale).astype(jnp.bfloat16)
    text_part_out[...] = jnp.dot(coef_t, gathered, preferred_element_type=jnp.float32)


def reduce_kernel(image_axes, image_src, text_src, image_out, text_out, image_send, image_recv, text_send, text_recv,
                  inbox, outbox):
    image_count, image_me = group_size(image_axes), linear_index(image_axes)
    count, me, right, left = ring_peers()
    half = count // 2
    greet_all(image_axes, pltpu.get_barrier_semaphore(), image_count, image_me, right, left)
    finish = image_direct(image_axes, True, image_src, image_out, image_send, image_recv, image_count, image_me)
    sends = [remote(text_src.at[(me + half) % count], inbox.at[0], text_send.at[0], text_recv.at[0], right),
             remote(text_src.at[(me + half + 1) % count], inbox.at[half], text_send.at[half], text_recv.at[half], left)]
    for copy in sends:
        copy.start()
    for step in range(1, half):
        chains = ((step, (me + half - step) % count, right), (half + step, (me + half + 1 + step) % count, left))
        for slot, target, device in chains:
            if slot >= count - 1:
                continue
            remote(inbox.at[slot - 1], inbox.at[slot - 1], text_send.at[slot], text_recv.at[slot - 1], device).wait_recv()
            outbox[slot] = inbox[slot - 1] + text_src[target]
            copy = remote(outbox.at[slot], inbox.at[slot], text_send.at[slot], text_recv.at[slot], device)
            copy.start()
            sends.append(copy)
    last_right, last_left = half - 1, count - 2
    for slot in (last_right, last_left):
        remote(inbox.at[slot], inbox.at[slot], text_send.at[0], text_recv.at[slot], right).wait_recv()
    text_out[...] = text_src[me] + inbox[last_right] + inbox[last_left]
    for copy in sends:
        copy.wait_send()
    lax.fori_loop(1, image_count, finish, 0)


def merged_reduce_kernel(image_axes, image_src, text_src, image_out, text_out, image_send, image_recv, text_send,
                         text_recv, inbox, outbox, halfbox, summed, half_sems):
    image_count, image_me = group_size(image_axes), linear_index(image_axes)
    count, me, right, left = ring_peers()
    right2 = member(TEXT_AXES, (me + 2) % count)
    left2 = member(TEXT_AXES, (me + count - 2) % count)
    core = linear_index(CORE_AXES)
    partner = member(CORE_AXES, 1 - core)
    greet_all(image_axes, pltpu.get_barrier_semaphore(), image_count, image_me, right, left, (right2, left2, partner))
    chains = (
        (0, 4, lambda step: right2, lambda step: 10 - 2 * step),
        (4, 4, lambda step: right2 if step < 4 else right, lambda step: 9 - 2 * step),
        (8, 3, lambda step: left2, lambda step: 2 * step - 8),
        (11, 4, lambda step: left2 if step < 4 else left, lambda step: 2 * step - 9),
    )
    sends = []

    def step_sends(step):
        for base, steps, device, offset in chains:
            if step > steps:
                continue
            slot = base + step - 1
            target = (me + count + offset(step)) % count
            if step == 1:
                source = text_src.at[target]
            else:
                remote(inbox.at[slot - 1], inbox.at[slot - 1], text_send.at[slot], text_recv.at[slot - 1],
                       right).wait_recv()
                outbox[slot] = inbox[slot - 1] + text_src[target]
                source = outbox.at[slot]
            copy = remote(source, inbox.at[slot], text_send.at[slot], text_recv.at[slot], device(step))
            copy.start()
            sends.append(copy)

    swap = remote(image_src.at[1 - core], halfbox, half_sems.at[0], half_sems.at[1], partner)
    swap.start()
    step_sends(1)
    step_sends(2)
    step_sends(3)
    swap.wait_recv()
    summed[...] = image_src[core] + halfbox[...]
    finish = image_direct(image_axes, True, summed, image_out, image_send, image_recv, image_count, image_me)
    step_sends(4)
    finals = (3, 7, 10, 14)
    for slot in finals:
        remote(inbox.at[slot], inbox.at[slot], text_send.at[0], text_recv.at[slot], right).wait_recv()
    text_out[...] = text_src[me] + inbox[finals[0]] + inbox[finals[1]] + inbox[finals[2]] + inbox[finals[3]]
    for copy in sends:
        copy.wait_send()
    swap.wait_send()
    lax.fori_loop(1, image_count, finish, 0)


def merged_reduce(image_axes, image_src, text_src, tag):
    image_count, text_count = group_size(image_axes), group_size(TEXT_AXES)
    image_shape = image_src.shape[1:]
    block = text_src.shape[1:]
    vmem = pl.BlockSpec(memory_space=pltpu.VMEM)
    scratch = [
        pltpu.SemaphoreType.DMA((image_count,)),
        pltpu.SemaphoreType.DMA((image_count,)),
        pltpu.SemaphoreType.DMA((text_count,)),
        pltpu.SemaphoreType.DMA((text_count,)),
        pltpu.VMEM((text_count,) + block, text_src.dtype),
        pltpu.VMEM((text_count,) + block, text_src.dtype),
        pltpu.VMEM(image_shape, image_src.dtype),
        pltpu.VMEM(image_shape, image_src.dtype),
        pltpu.SemaphoreType.DMA((2,)),
    ]
    return pl.pallas_call(
        functools.partial(merged_reduce_kernel, image_axes),
        out_shape=(jax.ShapeDtypeStruct(image_shape, image_src.dtype), jax.ShapeDtypeStruct(block, text_src.dtype)),
        in_specs=[vmem, vmem],
        out_specs=(vmem, vmem),
        scratch_shapes=scratch,
        compiler_params=pltpu.CompilerParams(collective_id=tag, has_side_effects=True),
    )(image_src, text_src)


def gather_compute(image_axes, image_src, text_src, scale, shift, tag):
    image_count, text_count = group_size(image_axes), group_size(TEXT_AXES)
    rows, width = image_src.shape
    vmem = pl.BlockSpec(memory_space=pltpu.VMEM)
    scratch = [
        pltpu.SemaphoreType.DMA((image_count,)),
        pltpu.SemaphoreType.DMA((image_count,)),
        pltpu.SemaphoreType.DMA((text_count,)),
        pltpu.SemaphoreType.DMA((text_count,)),
        pltpu.VMEM((image_count,) + image_src.shape, jnp.bfloat16),
        pltpu.VMEM((text_count,) + text_src.shape, jnp.bfloat16),
        pltpu.VMEM(image_src.shape, jnp.bfloat16),
        pltpu.VMEM(text_src.shape, jnp.bfloat16),
    ]
    return pl.pallas_call(
        functools.partial(gather_kernel, image_axes),
        out_shape=(
            jax.ShapeDtypeStruct((image_count * rows, width + LOSS_LANES), jnp.float32),
            jax.ShapeDtypeStruct((text_count * rows, width), jnp.float32),
            jax.ShapeDtypeStruct((rows, width), jnp.float32),
            jax.ShapeDtypeStruct((rows, LOSS_LANES), jnp.float32),
            jax.ShapeDtypeStruct((rows, width), jnp.float32),
            jax.ShapeDtypeStruct((rows, LOSS_LANES), jnp.float32),
        ),
        in_specs=[vmem] * 4,
        out_specs=tuple([vmem] * 6),
        scratch_shapes=scratch,
        compiler_params=pltpu.CompilerParams(collective_id=tag, has_side_effects=True),
    )(image_src, text_src, scale.reshape(1, 1), shift.reshape(1, 1))


def exchange(image_axes, image_src, text_src, scatter, tag):
    image_count, text_count = group_size(image_axes), group_size(TEXT_AXES)
    image_shape = image_src.shape if scatter else (image_count,) + image_src.shape
    text_shape = text_src.shape[1:] if scatter else (text_count,) + text_src.shape
    block = text_src.shape[1:] if scatter else text_src.shape
    vmem = pl.BlockSpec(memory_space=pltpu.VMEM)
    scratch = [
        pltpu.SemaphoreType.DMA((image_count,)),
        pltpu.SemaphoreType.DMA((image_count,)),
        pltpu.SemaphoreType.DMA((text_count,)),
        pltpu.SemaphoreType.DMA((text_count,)),
    ]
    if scatter:
        scratch += [pltpu.VMEM((text_count,) + block, text_src.dtype)] * 2
    return pl.pallas_call(
        functools.partial(reduce_kernel if scatter else gather_kernel, image_axes),
        out_shape=(jax.ShapeDtypeStruct(image_shape, image_src.dtype), jax.ShapeDtypeStruct(text_shape, text_src.dtype)),
        in_specs=[vmem, vmem],
        out_specs=(vmem, vmem),
        scratch_shapes=scratch,
        compiler_params=pltpu.CompilerParams(collective_id=tag, has_side_effects=True),
    )(image_src, text_src)


def pair_kernel(plan, *refs):
    count_groups = len(plan)
    srcs, outs = refs[:count_groups], refs[count_groups:2 * count_groups]
    sems = refs[2 * count_groups:]
    groups = [
        (axes, scatter, srcs[g], outs[g], sems[2 * g], sems[2 * g + 1]) for g, (axes, scatter) in enumerate(plan)
    ]
    barrier = pltpu.get_barrier_semaphore()
    peers = 0
    for axes, scatter, src, out, send, recv in groups:
        count, me = group_size(axes), linear_index(axes)
        peers += count - 1

        def greet(step, carry, axes=axes, count=count, me=me):
            pl.semaphore_signal(barrier, 1, device_id=member(axes, (me + step) % count), device_id_type=MESH_IDS)
            return carry

        lax.fori_loop(1, count, greet, 0)
    pl.semaphore_wait(barrier, peers)

    for axes, scatter, src, out, send, recv in groups:
        count, me = group_size(axes), linear_index(axes)

        def start(step, carry, axes=axes, scatter=scatter, count=count, me=me, src=src, out=out, send=send, recv=recv):
            peer = (me + step) % count
            pltpu.make_async_remote_copy(
                src.at[peer] if scatter else src, out.at[me], send.at[peer], recv.at[me],
                device_id=member(axes, peer), device_id_type=MESH_IDS,
            ).start()
            return carry

        lax.fori_loop(1, count, start, 0)

    for axes, scatter, src, out, send, recv in groups:
        count, me = group_size(axes), linear_index(axes)
        out[me] = src[me] if scatter else src[...]

    for axes, scatter, src, out, send, recv in groups:
        count, me = group_size(axes), linear_index(axes)

        def finish(step, carry, axes=axes, scatter=scatter, count=count, me=me, src=src, out=out, send=send, recv=recv):
            peer = (me + step) % count
            copy = pltpu.make_async_remote_copy(
                src.at[peer] if scatter else src, out.at[peer], send.at[peer], recv.at[peer],
                device_id=member(axes, peer), device_id_type=MESH_IDS,
            )
            copy.wait_send()
            copy.wait_recv()
            return carry

        lax.fori_loop(1, count, finish, 0)


def pair_exchange(routes, tag):
    plan = tuple((axes, scatter) for axes, src, scatter in routes)
    srcs = [src for axes, src, scatter in routes]
    shapes = [
        jax.ShapeDtypeStruct(src.shape if scatter else (group_size(axes),) + src.shape, src.dtype)
        for axes, src, scatter in routes
    ]
    sems = []
    for axes, src, scatter in routes:
        sems += [pltpu.SemaphoreType.DMA((group_size(axes),))] * 2
    vmem = pl.BlockSpec(memory_space=pltpu.VMEM)
    return pl.pallas_call(
        functools.partial(pair_kernel, plan),
        out_shape=tuple(shapes),
        in_specs=[vmem] * len(routes),
        out_specs=tuple([vmem] * len(routes)),
        scratch_shapes=sems,
        compiler_params=pltpu.CompilerParams(collective_id=tag, has_side_effects=True),
    )(*srcs)


def local(images, texts, scale, shift):
    rows, width = images.shape
    chips = group_size(CHIP_AXES)
    cores = group_size(CORE_AXES)
    text_count = group_size(TEXT_AXES)
    image_part, text_part, image_unit, image_norm, text_unit, text_norm = gather_compute(
        CORE_AXES + CHIP_AXES, images, texts, scale, shift, 0
    )
    image_norm = image_norm[:, :1]
    text_norm = text_norm[:, :1]
    image_in, text_in = merged_reduce(
        CHIP_AXES, image_part.reshape(cores, chips, rows, width + LOSS_LANES), text_part.reshape(text_count, rows, width), 3
    )
    image_in = jnp.sum(image_in, 0)
    text_sum = text_in
    image_grad = back_rows(image_in[:, :width], image_unit, image_norm)
    text_grad = back_rows(text_sum, text_unit, text_norm)
    return (image_in[:, width], image_grad, text_grad)


def solution(mesh):
    blk, grp = mesh.devices.shape
    fine = Mesh(mesh.devices.reshape(blk // 2, 2, grp // 16, 8, 2), ROWS_AXES)
    in_specs = (P(ROWS_AXES, None), P(ROWS_AXES, None), P(), P())
    out_specs = (P(ROWS_AXES), P(ROWS_AXES, None), P(ROWS_AXES, None))
    return jax.shard_map(local, mesh=fine, in_specs=in_specs, out_specs=out_specs, check_vma=False)
```

```python
import functools

import jax
import jax.numpy as jnp
from jax import lax
from jax.experimental import pallas as pl
from jax.experimental.pallas import tpu as pltpu
from jax.sharding import Mesh, PartitionSpec as P

ROWS_AXES = ("x", "zh", "y", "zl", "c")
CHIP_AXES = ("x", "y")
CORE_AXES = ("c",)
TEXT_AXES = ("zh", "zl")
MESH_IDS = pl.DeviceIdType.MESH
LOSS_LANES = 128


def unit_rows(values):
    floats = values.astype(jnp.float32)
    norms = jnp.sqrt(jnp.sum(floats * floats, 1, keepdims=True) + 1e-06)
    return (floats / norms, norms)


def back_rows(grads, units, norms):
    return (grads - units * jnp.sum(units * grads, 1, keepdims=True)) / norms


def linear_index(axes):
    index = 0
    for name in axes:
        index = index * lax.axis_size(name) + lax.axis_index(name)
    return index


def group_size(axes):
    size = 1
    for name in axes:
        size *= lax.axis_size(name)
    return size


def member(axes, k):
    coords = {}
    for name in reversed(axes):
        size = lax.axis_size(name)
        coords[name] = k % size
        k = k // size
    return tuple(coords[name] if name in coords else lax.axis_index(name) for name in ROWS_AXES)


def ring_peers():
    count, me = group_size(TEXT_AXES), linear_index(TEXT_AXES)
    return count, me, member(TEXT_AXES, (me + 1) % count), member(TEXT_AXES, (me + count - 1) % count)


def remote(src, dst, send, recv, device):
    return pltpu.make_async_remote_copy(src, dst, send, recv, device_id=device, device_id_type=MESH_IDS)


def greet_all(image_axes, barrier, image_count, image_me, right, left, extra=()):
    def greet(step, carry):
        pl.semaphore_signal(barrier, 1, device_id=member(image_axes, (image_me + step) % image_count),
                            device_id_type=MESH_IDS)
        return carry

    lax.fori_loop(1, image_count, greet, 0)
    for device in (right, left) + tuple(extra):
        pl.semaphore_signal(barrier, 1, device_id=device, device_id_type=MESH_IDS)
    pl.semaphore_wait(barrier, image_count + 1 + len(extra))


def image_direct(image_axes, scatter, src, out, send, recv, count, me):
    def start(step, carry):
        peer = (me + step) % count
        remote(src.at[peer] if scatter else src, out.at[me], send.at[peer], recv.at[me],
               member(image_axes, peer)).start()
        return carry

    lax.fori_loop(1, count, start, 0)
    out[me] = src[me] if scatter else src[...]

    def finish(step, carry):
        peer = (me + step) % count
        copy = remote(src.at[peer] if scatter else src, out.at[peer], send.at[peer], recv.at[peer],
                      member(image_axes, peer))
        copy.wait_send()
        copy.wait_recv()
        return carry

    return finish


def gather_kernel(image_axes, image_raw, text_raw, scale_ref, shift_ref, image_part_out, text_part_out,
                  image_unit_out, image_norm_out, text_unit_out, text_norm_out, image_send, image_recv, text_send,
                  text_recv, image_out, text_out, image_src, text_src):
    for raw, unit_out, norm_out, emb in ((image_raw, image_unit_out, image_norm_out, image_src),
                                         (text_raw, text_unit_out, text_norm_out, text_src)):
        floats = raw[...].astype(jnp.float32)
        norms = jnp.sqrt(jnp.sum(floats * floats, 1, keepdims=True) + 1e-06)
        units = floats / norms
        unit_out[...] = units
        norm_out[...] = jnp.broadcast_to(norms, norm_out.shape)
        emb[...] = units.astype(jnp.bfloat16)
    image_count, image_me = group_size(image_axes), linear_index(image_axes)
    count, me, right, left = ring_peers()
    right2 = member(TEXT_AXES, (me + 2) % count)
    left2 = member(TEXT_AXES, (me + count - 2) % count)
    greet_all(image_axes, pltpu.get_barrier_semaphore(), image_count, image_me, right, left, (right2, left2))
    sends = []

    def send(src, origin, device, slot):
        copy = remote(src, text_out.at[origin], text_send.at[slot], text_recv.at[origin], device)
        copy.start()
        sends.append(copy)

    def arrive(origin):
        remote(text_out.at[origin], text_out.at[origin], text_send.at[0], text_recv.at[origin], right).wait_recv()

    half = count // 2
    for slot, device in ((0, right), (1, right2), (half, left), (half + 1, left2)):
        send(text_src, me, device, slot)
    text_out[me] = text_src[...]
    finish = image_direct(image_axes, False, image_src, image_out, image_send, image_recv, image_count, image_me)
    slot_right, slot_left = 2, half + 2
    for step in range(2, half // 2 + 1):
        for distance in (2 * step - 3, 2 * step - 2):
            origin = (me + count - distance) % count
            arrive(origin)
            send(text_out.at[origin], origin, right2, slot_right)
            slot_right += 1
        for distance in (2 * step - 3, 2 * step - 2):
            if distance > half - 3:
                continue
            origin = (me + distance) % count
            arrive(origin)
            send(text_out.at[origin], origin, left2, slot_left)
            slot_left += 1
    for distance in (half - 1, half):
        arrive((me + count - distance) % count)
    for distance in (half - 2, half - 1):
        arrive((me + distance) % count)
    for copy in sends:
        copy.wait_send()
    lax.fori_loop(1, image_count, finish, 0)
    rows, width = image_src.shape
    gathered = image_out[...].reshape(image_count * rows, width)
    seen = text_out[...].reshape(count * rows, width)
    scale, shift = scale_ref[...], shift_ref[...]
    shape = (image_count * rows, count * rows)
    image_ids = lax.broadcasted_iota(jnp.int32, shape, 0)
    text_ids = lax.broadcasted_iota(jnp.int32, shape, 1)
    label = ((image_ids // rows == image_me) & (text_ids // rows == me) & (image_ids % rows == text_ids % rows)).astype(
        jnp.float32)
    logit = scale * lax.dot_general(gathered, seen, (((1,), (1,)), ((), ())), preferred_element_type=jnp.float32) + shift
    total = image_count * count * rows
    loss = jnp.sum(jax.nn.softplus(logit * (1.0 - 2.0 * label)), 1, keepdims=True) / total
    coef = ((jax.nn.sigmoid(logit) - label) * scale).astype(jnp.bfloat16)
    image_part_out[:, :width] = jnp.dot(coef, seen, preferred_element_type=jnp.float32)
    image_part_out[:, width:] = jnp.broadcast_to(loss, (image_count * rows, LOSS_LANES))
    shape_t = (count * rows, image_count * rows)
    text_ids_t = lax.broadcasted_iota(jnp.int32, shape_t, 0)
    image_ids_t = lax.broadcasted_iota(jnp.int32, shape_t, 1)
    label_t = ((image_ids_t // rows == image_me) & (text_ids_t // rows == me)
               & (image_ids_t % rows == text_ids_t % rows)).astype(jnp.float32)
    logit_t = scale * lax.dot_general(seen, gathered, (((1,), (1,)), ((), ())), preferred_element_type=jnp.float32) + shift
    coef_t = ((jax.nn.sigmoid(logit_t) - label_t) * scale).astype(jnp.bfloat16)
    text_part_out[...] = jnp.dot(coef_t, gathered, preferred_element_type=jnp.float32)


def reduce_kernel(image_axes, image_src, text_src, image_out, text_out, image_send, image_recv, text_send, text_recv,
                  inbox, outbox):
    image_count, image_me = group_size(image_axes), linear_index(image_axes)
    count, me, right, left = ring_peers()
    half = count // 2
    greet_all(image_axes, pltpu.get_barrier_semaphore(), image_count, image_me, right, left)
    finish = image_direct(image_axes, True, image_src, image_out, image_send, image_recv, image_count, image_me)
    sends = [remote(text_src.at[(me + half) % count], inbox.at[0], text_send.at[0], text_recv.at[0], right),
             remote(text_src.at[(me + half + 1) % count], inbox.at[half], text_send.at[half], text_recv.at[half], left)]
    for copy in sends:
        copy.start()
    for step in range(1, half):
        chains = ((step, (me + half - step) % count, right), (half + step, (me + half + 1 + step) % count, left))
        for slot, target, device in chains:
            if slot >= count - 1:
                continue
            remote(inbox.at[slot - 1], inbox.at[slot - 1], text_send.at[slot], text_recv.at[slot - 1], device).wait_recv()
            outbox[slot] = inbox[slot - 1] + text_src[target]
            copy = remote(outbox.at[slot], inbox.at[slot], text_send.at[slot], text_recv.at[slot], device)
            copy.start()
            sends.append(copy)
    last_right, last_left = half - 1, count - 2
    for slot in (last_right, last_left):
        remote(inbox.at[slot], inbox.at[slot], text_send.at[0], text_recv.at[slot], right).wait_recv()
    text_out[...] = text_src[me] + inbox[last_right] + inbox[last_left]
    for copy in sends:
        copy.wait_send()
    lax.fori_loop(1, image_count, finish, 0)


def merged_reduce_kernel(image_axes, image_src, text_src, image_out, text_out, image_send, image_recv, text_send,
                         text_recv, inbox, outbox, halfbox, summed, half_sems):
    image_count, image_me = group_size(image_axes), linear_index(image_axes)
    count, me, right, left = ring_peers()
    right2 = member(TEXT_AXES, (me + 2) % count)
    left2 = member(TEXT_AXES, (me + count - 2) % count)
    core = linear_index(CORE_AXES)
    partner = member(CORE_AXES, 1 - core)
    greet_all(image_axes, pltpu.get_barrier_semaphore(), image_count, image_me, right, left, (right2, left2, partner))
    chains = (
        (0, 4, lambda step: right2, lambda step: 10 - 2 * step),
        (4, 4, lambda step: right2 if step < 4 else right, lambda step: 9 - 2 * step),
        (8, 3, lambda step: left2, lambda step: 2 * step - 8),
        (11, 4, lambda step: left2 if step < 4 else left, lambda step: 2 * step - 9),
    )
    sends = []

    def step_sends(step):
        for base, steps, device, offset in chains:
            if step > steps:
                continue
            slot = base + step - 1
            target = (me + count + offset(step)) % count
            if step == 1:
                source = text_src.at[target]
            else:
                remote(inbox.at[slot - 1], inbox.at[slot - 1], text_send.at[slot], text_recv.at[slot - 1],
                       right).wait_recv()
                outbox[slot] = inbox[slot - 1] + text_src[target]
                source = outbox.at[slot]
            copy = remote(source, inbox.at[slot], text_send.at[slot], text_recv.at[slot], device(step))
            copy.start()
            sends.append(copy)

    swap = remote(image_src.at[1 - core], halfbox, half_sems.at[0], half_sems.at[1], partner)
    swap.start()
    step_sends(1)
    step_sends(2)
    swap.wait_recv()
    summed[...] = image_src[core] + halfbox[...]
    finish = image_direct(image_axes, True, summed, image_out, image_send, image_recv, image_count, image_me)
    for step in range(3, 5):
        step_sends(step)
    finals = (3, 7, 10, 14)
    for slot in finals:
        remote(inbox.at[slot], inbox.at[slot], text_send.at[0], text_recv.at[slot], right).wait_recv()
    text_out[...] = text_src[me] + inbox[finals[0]] + inbox[finals[1]] + inbox[finals[2]] + inbox[finals[3]]
    for copy in sends:
        copy.wait_send()
    swap.wait_send()
    lax.fori_loop(1, image_count, finish, 0)


def merged_reduce(image_axes, image_src, text_src, tag):
    image_count, text_count = group_size(image_axes), group_size(TEXT_AXES)
    image_shape = image_src.shape[1:]
    block = text_src.shape[1:]
    vmem = pl.BlockSpec(memory_space=pltpu.VMEM)
    scratch = [
        pltpu.SemaphoreType.DMA((image_count,)),
        pltpu.SemaphoreType.DMA((image_count,)),
        pltpu.SemaphoreType.DMA((text_count,)),
        pltpu.SemaphoreType.DMA((text_count,)),
        pltpu.VMEM((text_count,) + block, text_src.dtype),
        pltpu.VMEM((text_count,) + block, text_src.dtype),
        pltpu.VMEM(image_shape, image_src.dtype),
        pltpu.VMEM(image_shape, image_src.dtype),
        pltpu.SemaphoreType.DMA((2,)),
    ]
    return pl.pallas_call(
        functools.partial(merged_reduce_kernel, image_axes),
        out_shape=(jax.ShapeDtypeStruct(image_shape, image_src.dtype), jax.ShapeDtypeStruct(block, text_src.dtype)),
        in_specs=[vmem, vmem],
        out_specs=(vmem, vmem),
        scratch_shapes=scratch,
        compiler_params=pltpu.CompilerParams(collective_id=tag, has_side_effects=True),
    )(image_src, text_src)


def gather_compute(image_axes, image_src, text_src, scale, shift, tag):
    image_count, text_count = group_size(image_axes), group_size(TEXT_AXES)
    rows, width = image_src.shape
    vmem = pl.BlockSpec(memory_space=pltpu.VMEM)
    scratch = [
        pltpu.SemaphoreType.DMA((image_count,)),
        pltpu.SemaphoreType.DMA((image_count,)),
        pltpu.SemaphoreType.DMA((text_count,)),
        pltpu.SemaphoreType.DMA((text_count,)),
        pltpu.VMEM((image_count,) + image_src.shape, jnp.bfloat16),
        pltpu.VMEM((text_count,) + text_src.shape, jnp.bfloat16),
        pltpu.VMEM(image_src.shape, jnp.bfloat16),
        pltpu.VMEM(text_src.shape, jnp.bfloat16),
    ]
    return pl.pallas_call(
        functools.partial(gather_kernel, image_axes),
        out_shape=(
            jax.ShapeDtypeStruct((image_count * rows, width + LOSS_LANES), jnp.float32),
            jax.ShapeDtypeStruct((text_count * rows, width), jnp.float32),
            jax.ShapeDtypeStruct((rows, width), jnp.float32),
            jax.ShapeDtypeStruct((rows, LOSS_LANES), jnp.float32),
            jax.ShapeDtypeStruct((rows, width), jnp.float32),
            jax.ShapeDtypeStruct((rows, LOSS_LANES), jnp.float32),
        ),
        in_specs=[vmem] * 4,
        out_specs=tuple([vmem] * 6),
        scratch_shapes=scratch,
        compiler_params=pltpu.CompilerParams(collective_id=tag, has_side_effects=True),
    )(image_src, text_src, scale.reshape(1, 1), shift.reshape(1, 1))


def exchange(image_axes, image_src, text_src, scatter, tag):
    image_count, text_count = group_size(image_axes), group_size(TEXT_AXES)
    image_shape = image_src.shape if scatter else (image_count,) + image_src.shape
    text_shape = text_src.shape[1:] if scatter else (text_count,) + text_src.shape
    block = text_src.shape[1:] if scatter else text_src.shape
    vmem = pl.BlockSpec(memory_space=pltpu.VMEM)
    scratch = [
        pltpu.SemaphoreType.DMA((image_count,)),
        pltpu.SemaphoreType.DMA((image_count,)),
        pltpu.SemaphoreType.DMA((text_count,)),
        pltpu.SemaphoreType.DMA((text_count,)),
    ]
    if scatter:
        scratch += [pltpu.VMEM((text_count,) + block, text_src.dtype)] * 2
    return pl.pallas_call(
        functools.partial(reduce_kernel if scatter else gather_kernel, image_axes),
        out_shape=(jax.ShapeDtypeStruct(image_shape, image_src.dtype), jax.ShapeDtypeStruct(text_shape, text_src.dtype)),
        in_specs=[vmem, vmem],
        out_specs=(vmem, vmem),
        scratch_shapes=scratch,
        compiler_params=pltpu.CompilerParams(collective_id=tag, has_side_effects=True),
    )(image_src, text_src)


def pair_kernel(plan, *refs):
    count_groups = len(plan)
    srcs, outs = refs[:count_groups], refs[count_groups:2 * count_groups]
    sems = refs[2 * count_groups:]
    groups = [
        (axes, scatter, srcs[g], outs[g], sems[2 * g], sems[2 * g + 1]) for g, (axes, scatter) in enumerate(plan)
    ]
    barrier = pltpu.get_barrier_semaphore()
    peers = 0
    for axes, scatter, src, out, send, recv in groups:
        count, me = group_size(axes), linear_index(axes)
        peers += count - 1

        def greet(step, carry, axes=axes, count=count, me=me):
            pl.semaphore_signal(barrier, 1, device_id=member(axes, (me + step) % count), device_id_type=MESH_IDS)
            return carry

        lax.fori_loop(1, count, greet, 0)
    pl.semaphore_wait(barrier, peers)

    for axes, scatter, src, out, send, recv in groups:
        count, me = group_size(axes), linear_index(axes)

        def start(step, carry, axes=axes, scatter=scatter, count=count, me=me, src=src, out=out, send=send, recv=recv):
            peer = (me + step) % count
            pltpu.make_async_remote_copy(
                src.at[peer] if scatter else src, out.at[me], send.at[peer], recv.at[me],
                device_id=member(axes, peer), device_id_type=MESH_IDS,
            ).start()
            return carry

        lax.fori_loop(1, count, start, 0)

    for axes, scatter, src, out, send, recv in groups:
        count, me = group_size(axes), linear_index(axes)
        out[me] = src[me] if scatter else src[...]

    for axes, scatter, src, out, send, recv in groups:
        count, me = group_size(axes), linear_index(axes)

        def finish(step, carry, axes=axes, scatter=scatter, count=count, me=me, src=src, out=out, send=send, recv=recv):
            peer = (me + step) % count
            copy = pltpu.make_async_remote_copy(
                src.at[peer] if scatter else src, out.at[peer], send.at[peer], recv.at[peer],
                device_id=member(axes, peer), device_id_type=MESH_IDS,
            )
            copy.wait_send()
            copy.wait_recv()
            return carry

        lax.fori_loop(1, count, finish, 0)


def pair_exchange(routes, tag):
    plan = tuple((axes, scatter) for axes, src, scatter in routes)
    srcs = [src for axes, src, scatter in routes]
    shapes = [
        jax.ShapeDtypeStruct(src.shape if scatter else (group_size(axes),) + src.shape, src.dtype)
        for axes, src, scatter in routes
    ]
    sems = []
    for axes, src, scatter in routes:
        sems += [pltpu.SemaphoreType.DMA((group_size(axes),))] * 2
    vmem = pl.BlockSpec(memory_space=pltpu.VMEM)
    return pl.pallas_call(
        functools.partial(pair_kernel, plan),
        out_shape=tuple(shapes),
        in_specs=[vmem] * len(routes),
        out_specs=tuple([vmem] * len(routes)),
        scratch_shapes=sems,
        compiler_params=pltpu.CompilerParams(collective_id=tag, has_side_effects=True),
    )(*srcs)


def local(images, texts, scale, shift):
    rows, width = images.shape
    chips = group_size(CHIP_AXES)
    cores = group_size(CORE_AXES)
    text_count = group_size(TEXT_AXES)
    image_part, text_part, image_unit, image_norm, text_unit, text_norm = gather_compute(
        CORE_AXES + CHIP_AXES, images, texts, scale, shift, 0
    )
    image_norm = image_norm[:, :1]
    text_norm = text_norm[:, :1]
    image_in, text_in = merged_reduce(
        CHIP_AXES, image_part.reshape(cores, chips, rows, width + LOSS_LANES), text_part.reshape(text_count, rows, width), 3
    )
    image_in = jnp.sum(image_in, 0)
    text_sum = text_in
    image_grad = back_rows(image_in[:, :width], image_unit, image_norm)
    text_grad = back_rows(text_sum, text_unit, text_norm)
    return (image_in[:, width], image_grad, text_grad)


def solution(mesh):
    blk, grp = mesh.devices.shape
    fine = Mesh(mesh.devices.reshape(blk // 2, 2, grp // 16, 8, 2), ROWS_AXES)
    in_specs = (P(ROWS_AXES, None), P(ROWS_AXES, None), P(), P())
    out_specs = (P(ROWS_AXES), P(ROWS_AXES, None), P(ROWS_AXES, None))
    return jax.shard_map(local, mesh=fine, in_specs=in_specs, out_specs=out_specs, check_vma=False)
```

```python
import functools

import jax
import jax.numpy as jnp
from jax import lax
from jax.experimental import pallas as pl
from jax.experimental.pallas import tpu as pltpu
from jax.sharding import Mesh, PartitionSpec as P

ROWS_AXES = ("x", "zh", "y", "zl", "c")
CHIP_AXES = ("x", "y")
CORE_AXES = ("c",)
TEXT_AXES = ("zh", "zl")
MESH_IDS = pl.DeviceIdType.MESH
LOSS_LANES = 128


def unit_rows(values):
    floats = values.astype(jnp.float32)
    norms = jnp.sqrt(jnp.sum(floats * floats, 1, keepdims=True) + 1e-06)
    return (floats / norms, norms)


def back_rows(grads, units, norms):
    return (grads - units * jnp.sum(units * grads, 1, keepdims=True)) / norms


def linear_index(axes):
    index = 0
    for name in axes:
        index = index * lax.axis_size(name) + lax.axis_index(name)
    return index


def group_size(axes):
    size = 1
    for name in axes:
        size *= lax.axis_size(name)
    return size


def member(axes, k):
    coords = {}
    for name in reversed(axes):
        size = lax.axis_size(name)
        coords[name] = k % size
        k = k // size
    return tuple(coords[name] if name in coords else lax.axis_index(name) for name in ROWS_AXES)


def ring_peers():
    count, me = group_size(TEXT_AXES), linear_index(TEXT_AXES)
    return count, me, member(TEXT_AXES, (me + 1) % count), member(TEXT_AXES, (me + count - 1) % count)


def remote(src, dst, send, recv, device):
    return pltpu.make_async_remote_copy(src, dst, send, recv, device_id=device, device_id_type=MESH_IDS)


def greet_all(image_axes, barrier, image_count, image_me, right, left, extra=()):
    def greet(step, carry):
        pl.semaphore_signal(barrier, 1, device_id=member(image_axes, (image_me + step) % image_count),
                            device_id_type=MESH_IDS)
        return carry

    lax.fori_loop(1, image_count, greet, 0)
    for device in (right, left) + tuple(extra):
        pl.semaphore_signal(barrier, 1, device_id=device, device_id_type=MESH_IDS)
    pl.semaphore_wait(barrier, image_count + 1 + len(extra))


def image_direct(image_axes, scatter, src, out, send, recv, count, me):
    def start(step, carry):
        peer = (me + step) % count
        remote(src.at[peer] if scatter else src, out.at[me], send.at[peer], recv.at[me],
               member(image_axes, peer)).start()
        return carry

    lax.fori_loop(1, count, start, 0)
    out[me] = src[me] if scatter else src[...]

    def finish(step, carry):
        peer = (me + step) % count
        copy = remote(src.at[peer] if scatter else src, out.at[peer], send.at[peer], recv.at[peer],
                      member(image_axes, peer))
        copy.wait_send()
        copy.wait_recv()
        return carry

    return finish


def gather_kernel(image_axes, image_raw, text_raw, scale_ref, shift_ref, image_part_out, text_part_out,
                  image_unit_out, image_norm_out, text_unit_out, text_norm_out, image_send, image_recv, text_send,
                  text_recv, image_out, text_out, image_src, text_src):
    for raw, unit_out, norm_out, emb in ((image_raw, image_unit_out, image_norm_out, image_src),
                                         (text_raw, text_unit_out, text_norm_out, text_src)):
        floats = raw[...].astype(jnp.float32)
        norms = jnp.sqrt(jnp.sum(floats * floats, 1, keepdims=True) + 1e-06)
        units = floats / norms
        unit_out[...] = units
        norm_out[...] = jnp.broadcast_to(norms, norm_out.shape)
        emb[...] = units.astype(jnp.bfloat16)
    image_count, image_me = group_size(image_axes), linear_index(image_axes)
    count, me, right, left = ring_peers()
    right2 = member(TEXT_AXES, (me + 2) % count)
    left2 = member(TEXT_AXES, (me + count - 2) % count)
    greet_all(image_axes, pltpu.get_barrier_semaphore(), image_count, image_me, right, left, (right2, left2))
    sends = []

    def send(src, origin, device, slot):
        copy = remote(src, text_out.at[origin], text_send.at[slot], text_recv.at[origin], device)
        copy.start()
        sends.append(copy)

    def arrive(origin):
        remote(text_out.at[origin], text_out.at[origin], text_send.at[0], text_recv.at[origin], right).wait_recv()

    half = count // 2
    for slot, device in ((0, right), (1, right2), (half, left), (half + 1, left2)):
        send(text_src, me, device, slot)
    text_out[me] = text_src[...]
    finish = image_direct(image_axes, False, image_src, image_out, image_send, image_recv, image_count, image_me)
    slot_right, slot_left = 2, half + 2
    for step in range(2, half // 2 + 1):
        for distance in (2 * step - 3, 2 * step - 2):
            origin = (me + count - distance) % count
            arrive(origin)
            send(text_out.at[origin], origin, right2, slot_right)
            slot_right += 1
        for distance in (2 * step - 3, 2 * step - 2):
            if distance > half - 3:
                continue
            origin = (me + distance) % count
            arrive(origin)
            send(text_out.at[origin], origin, left2, slot_left)
            slot_left += 1
    for distance in (half - 1, half):
        arrive((me + count - distance) % count)
    for distance in (half - 2, half - 1):
        arrive((me + distance) % count)
    for copy in sends:
        copy.wait_send()
    lax.fori_loop(1, image_count, finish, 0)
    rows, width = image_src.shape
    gathered = image_out[...].reshape(image_count * rows, width)
    seen = text_out[...].reshape(count * rows, width)
    scale, shift = scale_ref[...], shift_ref[...]
    shape = (image_count * rows, count * rows)
    image_ids = lax.broadcasted_iota(jnp.int32, shape, 0)
    text_ids = lax.broadcasted_iota(jnp.int32, shape, 1)
    label = ((image_ids // rows == image_me) & (text_ids // rows == me) & (image_ids % rows == text_ids % rows)).astype(
        jnp.float32)
    logit = scale * lax.dot_general(gathered, seen, (((1,), (1,)), ((), ())), preferred_element_type=jnp.float32) + shift
    total = image_count * count * rows
    loss = jnp.sum(jax.nn.softplus(logit * (1.0 - 2.0 * label)), 1, keepdims=True) / total
    coef = ((jax.nn.sigmoid(logit) - label) * scale).astype(jnp.bfloat16)
    image_part_out[:, :width] = jnp.dot(coef, seen, preferred_element_type=jnp.float32)
    image_part_out[:, width:] = jnp.broadcast_to(loss, (image_count * rows, LOSS_LANES))
    shape_t = (count * rows, image_count * rows)
    text_ids_t = lax.broadcasted_iota(jnp.int32, shape_t, 0)
    image_ids_t = lax.broadcasted_iota(jnp.int32, shape_t, 1)
    label_t = ((image_ids_t // rows == image_me) & (text_ids_t // rows == me)
               & (image_ids_t % rows == text_ids_t % rows)).astype(jnp.float32)
    logit_t = scale * lax.dot_general(seen, gathered, (((1,), (1,)), ((), ())), preferred_element_type=jnp.float32) + shift
    coef_t = ((jax.nn.sigmoid(logit_t) - label_t) * scale).astype(jnp.bfloat16)
    text_part_out[...] = jnp.dot(coef_t, gathered, preferred_element_type=jnp.float32)


def reduce_kernel(image_axes, image_src, text_src, image_out, text_out, image_send, image_recv, text_send, text_recv,
                  inbox, outbox):
    image_count, image_me = group_size(image_axes), linear_index(image_axes)
    count, me, right, left = ring_peers()
    half = count // 2
    greet_all(image_axes, pltpu.get_barrier_semaphore(), image_count, image_me, right, left)
    finish = image_direct(image_axes, True, image_src, image_out, image_send, image_recv, image_count, image_me)
    sends = [remote(text_src.at[(me + half) % count], inbox.at[0], text_send.at[0], text_recv.at[0], right),
             remote(text_src.at[(me + half + 1) % count], inbox.at[half], text_send.at[half], text_recv.at[half], left)]
    for copy in sends:
        copy.start()
    for step in range(1, half):
        chains = ((step, (me + half - step) % count, right), (half + step, (me + half + 1 + step) % count, left))
        for slot, target, device in chains:
            if slot >= count - 1:
                continue
            remote(inbox.at[slot - 1], inbox.at[slot - 1], text_send.at[slot], text_recv.at[slot - 1], device).wait_recv()
            outbox[slot] = inbox[slot - 1] + text_src[target]
            copy = remote(outbox.at[slot], inbox.at[slot], text_send.at[slot], text_recv.at[slot], device)
            copy.start()
            sends.append(copy)
    last_right, last_left = half - 1, count - 2
    for slot in (last_right, last_left):
        remote(inbox.at[slot], inbox.at[slot], text_send.at[0], text_recv.at[slot], right).wait_recv()
    text_out[...] = text_src[me] + inbox[last_right] + inbox[last_left]
    for copy in sends:
        copy.wait_send()
    lax.fori_loop(1, image_count, finish, 0)


def merged_reduce_kernel(image_axes, image_src, text_src, image_out, text_out, image_send, image_recv, text_send,
                         text_recv, inbox, outbox, halfbox, summed, half_sems):
    image_count, image_me = group_size(image_axes), linear_index(image_axes)
    count, me, right, left = ring_peers()
    right2 = member(TEXT_AXES, (me + 2) % count)
    left2 = member(TEXT_AXES, (me + count - 2) % count)
    core = linear_index(CORE_AXES)
    partner = member(CORE_AXES, 1 - core)
    greet_all(image_axes, pltpu.get_barrier_semaphore(), image_count, image_me, right, left, (right2, left2, partner))
    chains = (
        (0, 4, lambda step: right2, lambda step: 10 - 2 * step),
        (4, 4, lambda step: right2 if step < 4 else right, lambda step: 9 - 2 * step),
        (8, 3, lambda step: left2, lambda step: 2 * step - 8),
        (11, 4, lambda step: left2 if step < 4 else left, lambda step: 2 * step - 9),
    )
    sends = []

    def step_sends(step):
        for base, steps, device, offset in chains:
            if step > steps:
                continue
            slot = base + step - 1
            target = (me + count + offset(step)) % count
            if step == 1:
                source = text_src.at[target]
            else:
                remote(inbox.at[slot - 1], inbox.at[slot - 1], text_send.at[slot], text_recv.at[slot - 1],
                       right).wait_recv()
                outbox[slot] = inbox[slot - 1] + text_src[target]
                source = outbox.at[slot]
            copy = remote(source, inbox.at[slot], text_send.at[slot], text_recv.at[slot], device(step))
            copy.start()
            sends.append(copy)

    step_sends(1)
    swap = remote(image_src.at[1 - core], halfbox, half_sems.at[0], half_sems.at[1], partner)
    swap.start()
    step_sends(2)
    swap.wait_recv()
    summed[...] = image_src[core] + halfbox[...]
    finish = image_direct(image_axes, True, summed, image_out, image_send, image_recv, image_count, image_me)
    for step in range(3, 5):
        step_sends(step)
    finals = (3, 7, 10, 14)
    for slot in finals:
        remote(inbox.at[slot], inbox.at[slot], text_send.at[0], text_recv.at[slot], right).wait_recv()
    text_out[...] = text_src[me] + inbox[finals[0]] + inbox[finals[1]] + inbox[finals[2]] + inbox[finals[3]]
    for copy in sends:
        copy.wait_send()
    swap.wait_send()
    lax.fori_loop(1, image_count, finish, 0)


def merged_reduce(image_axes, image_src, text_src, tag):
    image_count, text_count = group_size(image_axes), group_size(TEXT_AXES)
    image_shape = image_src.shape[1:]
    block = text_src.shape[1:]
    vmem = pl.BlockSpec(memory_space=pltpu.VMEM)
    scratch = [
        pltpu.SemaphoreType.DMA((image_count,)),
        pltpu.SemaphoreType.DMA((image_count,)),
        pltpu.SemaphoreType.DMA((text_count,)),
        pltpu.SemaphoreType.DMA((text_count,)),
        pltpu.VMEM((text_count,) + block, text_src.dtype),
        pltpu.VMEM((text_count,) + block, text_src.dtype),
        pltpu.VMEM(image_shape, image_src.dtype),
        pltpu.VMEM(image_shape, image_src.dtype),
        pltpu.SemaphoreType.DMA((2,)),
    ]
    return pl.pallas_call(
        functools.partial(merged_reduce_kernel, image_axes),
        out_shape=(jax.ShapeDtypeStruct(image_shape, image_src.dtype), jax.ShapeDtypeStruct(block, text_src.dtype)),
        in_specs=[vmem, vmem],
        out_specs=(vmem, vmem),
        scratch_shapes=scratch,
        compiler_params=pltpu.CompilerParams(collective_id=tag, has_side_effects=True),
    )(image_src, text_src)


def gather_compute(image_axes, image_src, text_src, scale, shift, tag):
    image_count, text_count = group_size(image_axes), group_size(TEXT_AXES)
    rows, width = image_src.shape
    vmem = pl.BlockSpec(memory_space=pltpu.VMEM)
    scratch = [
        pltpu.SemaphoreType.DMA((image_count,)),
        pltpu.SemaphoreType.DMA((image_count,)),
        pltpu.SemaphoreType.DMA((text_count,)),
        pltpu.SemaphoreType.DMA((text_count,)),
        pltpu.VMEM((image_count,) + image_src.shape, jnp.bfloat16),
        pltpu.VMEM((text_count,) + text_src.shape, jnp.bfloat16),
        pltpu.VMEM(image_src.shape, jnp.bfloat16),
        pltpu.VMEM(text_src.shape, jnp.bfloat16),
    ]
    return pl.pallas_call(
        functools.partial(gather_kernel, image_axes),
        out_shape=(
            jax.ShapeDtypeStruct((image_count * rows, width + LOSS_LANES), jnp.float32),
            jax.ShapeDtypeStruct((text_count * rows, width), jnp.float32),
            jax.ShapeDtypeStruct((rows, width), jnp.float32),
            jax.ShapeDtypeStruct((rows, LOSS_LANES), jnp.float32),
            jax.ShapeDtypeStruct((rows, width), jnp.float32),
            jax.ShapeDtypeStruct((rows, LOSS_LANES), jnp.float32),
        ),
        in_specs=[vmem] * 4,
        out_specs=tuple([vmem] * 6),
        scratch_shapes=scratch,
        compiler_params=pltpu.CompilerParams(collective_id=tag, has_side_effects=True),
    )(image_src, text_src, scale.reshape(1, 1), shift.reshape(1, 1))


def exchange(image_axes, image_src, text_src, scatter, tag):
    image_count, text_count = group_size(image_axes), group_size(TEXT_AXES)
    image_shape = image_src.shape if scatter else (image_count,) + image_src.shape
    text_shape = text_src.shape[1:] if scatter else (text_count,) + text_src.shape
    block = text_src.shape[1:] if scatter else text_src.shape
    vmem = pl.BlockSpec(memory_space=pltpu.VMEM)
    scratch = [
        pltpu.SemaphoreType.DMA((image_count,)),
        pltpu.SemaphoreType.DMA((image_count,)),
        pltpu.SemaphoreType.DMA((text_count,)),
        pltpu.SemaphoreType.DMA((text_count,)),
    ]
    if scatter:
        scratch += [pltpu.VMEM((text_count,) + block, text_src.dtype)] * 2
    return pl.pallas_call(
        functools.partial(reduce_kernel if scatter else gather_kernel, image_axes),
        out_shape=(jax.ShapeDtypeStruct(image_shape, image_src.dtype), jax.ShapeDtypeStruct(text_shape, text_src.dtype)),
        in_specs=[vmem, vmem],
        out_specs=(vmem, vmem),
        scratch_shapes=scratch,
        compiler_params=pltpu.CompilerParams(collective_id=tag, has_side_effects=True),
    )(image_src, text_src)


def pair_kernel(plan, *refs):
    count_groups = len(plan)
    srcs, outs = refs[:count_groups], refs[count_groups:2 * count_groups]
    sems = refs[2 * count_groups:]
    groups = [
        (axes, scatter, srcs[g], outs[g], sems[2 * g], sems[2 * g + 1]) for g, (axes, scatter) in enumerate(plan)
    ]
    barrier = pltpu.get_barrier_semaphore()
    peers = 0
    for axes, scatter, src, out, send, recv in groups:
        count, me = group_size(axes), linear_index(axes)
        peers += count - 1

        def greet(step, carry, axes=axes, count=count, me=me):
            pl.semaphore_signal(barrier, 1, device_id=member(axes, (me + step) % count), device_id_type=MESH_IDS)
            return carry

        lax.fori_loop(1, count, greet, 0)
    pl.semaphore_wait(barrier, peers)

    for axes, scatter, src, out, send, recv in groups:
        count, me = group_size(axes), linear_index(axes)

        def start(step, carry, axes=axes, scatter=scatter, count=count, me=me, src=src, out=out, send=send, recv=recv):
            peer = (me + step) % count
            pltpu.make_async_remote_copy(
                src.at[peer] if scatter else src, out.at[me], send.at[peer], recv.at[me],
                device_id=member(axes, peer), device_id_type=MESH_IDS,
            ).start()
            return carry

        lax.fori_loop(1, count, start, 0)

    for axes, scatter, src, out, send, recv in groups:
        count, me = group_size(axes), linear_index(axes)
        out[me] = src[me] if scatter else src[...]

    for axes, scatter, src, out, send, recv in groups:
        count, me = group_size(axes), linear_index(axes)

        def finish(step, carry, axes=axes, scatter=scatter, count=count, me=me, src=src, out=out, send=send, recv=recv):
            peer = (me + step) % count
            copy = pltpu.make_async_remote_copy(
                src.at[peer] if scatter else src, out.at[peer], send.at[peer], recv.at[peer],
                device_id=member(axes, peer), device_id_type=MESH_IDS,
            )
            copy.wait_send()
            copy.wait_recv()
            return carry

        lax.fori_loop(1, count, finish, 0)


def pair_exchange(routes, tag):
    plan = tuple((axes, scatter) for axes, src, scatter in routes)
    srcs = [src for axes, src, scatter in routes]
    shapes = [
        jax.ShapeDtypeStruct(src.shape if scatter else (group_size(axes),) + src.shape, src.dtype)
        for axes, src, scatter in routes
    ]
    sems = []
    for axes, src, scatter in routes:
        sems += [pltpu.SemaphoreType.DMA((group_size(axes),))] * 2
    vmem = pl.BlockSpec(memory_space=pltpu.VMEM)
    return pl.pallas_call(
        functools.partial(pair_kernel, plan),
        out_shape=tuple(shapes),
        in_specs=[vmem] * len(routes),
        out_specs=tuple([vmem] * len(routes)),
        scratch_shapes=sems,
        compiler_params=pltpu.CompilerParams(collective_id=tag, has_side_effects=True),
    )(*srcs)


def local(images, texts, scale, shift):
    rows, width = images.shape
    chips = group_size(CHIP_AXES)
    cores = group_size(CORE_AXES)
    text_count = group_size(TEXT_AXES)
    image_part, text_part, image_unit, image_norm, text_unit, text_norm = gather_compute(
        CORE_AXES + CHIP_AXES, images, texts, scale, shift, 0
    )
    image_norm = image_norm[:, :1]
    text_norm = text_norm[:, :1]
    image_in, text_in = merged_reduce(
        CHIP_AXES, image_part.reshape(cores, chips, rows, width + LOSS_LANES), text_part.reshape(text_count, rows, width), 3
    )
    image_in = jnp.sum(image_in, 0)
    text_sum = text_in
    image_grad = back_rows(image_in[:, :width], image_unit, image_norm)
    text_grad = back_rows(text_sum, text_unit, text_norm)
    return (image_in[:, width], image_grad, text_grad)


def solution(mesh):
    blk, grp = mesh.devices.shape
    fine = Mesh(mesh.devices.reshape(blk // 2, 2, grp // 16, 8, 2), ROWS_AXES)
    in_specs = (P(ROWS_AXES, None), P(ROWS_AXES, None), P(), P())
    out_specs = (P(ROWS_AXES), P(ROWS_AXES, None), P(ROWS_AXES, None))
    return jax.shard_map(local, mesh=fine, in_specs=in_specs, out_specs=out_specs, check_vma=False)
```
